32 devices in a mesh: dp: 16 (over z, y, x), pair: 2 (over core).
Axes of the slice: x: 2, y: 2, z: 4, core: 2. Of those that a mesh axis runs over, the one named last changes fastest.
Arguments:
- tokens: bfloat16 [2, 32, 64, 2048], P(None, ('dp', 'pair')), may hold values from -6 to 6
- doc_starts: int32 [2, 32, 64], P(None, ('dp', 'pair')), may hold values 0 or 1
- seq_lengths: int32 [2, 32], P(None, ('dp', 'pair')), may hold values from 32 to 64, as said below
- attn_gain: bfloat16 [2048], P(('dp', 'pair')), may hold values from 0.25 to 1.75
- query_weight: bfloat16 [2048, 2048], P(('dp', 'pair')), may hold values from -0.125 to 0.125
- key_weight: bfloat16 [2048, 2048], P(('dp', 'pair')), may hold values from -0.125 to 0.125
- value_weight: bfloat16 [2048, 2048], P(('dp', 'pair')), may hold values from -0.125 to 0.125
- out_gate_weight: bfloat16 [2048, 2048], P(('dp', 'pair')), may hold values from -0.125 to 0.125
- beta_weight: bfloat16 [2048, 16], P(('dp', 'pair')), may hold values from -0.125 to 0.125
- query_conv: bfloat16 [2048, 4], P(('dp', 'pair')), may hold values from -3 to 3
- key_conv: bfloat16 [2048, 4], P(('dp', 'pair')), may hold values from -3 to 3
- value_conv: bfloat16 [2048, 4], P(('dp', 'pair')), may hold values from -3 to 3
- head_gain: bfloat16 [128], P(('dp', 'pair')), may hold values from 0.25 to 1.75
- out_weight: bfloat16 [2048, 2048], P(('dp', 'pair')), may hold values from -0.125 to 0.125
- mlp_gain: bfloat16 [2048], P(('dp', 'pair')), may hold values from 0.25 to 1.75
- mlp_gate_weight: bfloat16 [2048, 5632], P(('dp', 'pair')), may hold values from -0.125 to 0.125
- mlp_up_weight: bfloat16 [2048, 5632], P(('dp', 'pair')), may hold values from -0.125 to 0.125
- mlp_down_weight: bfloat16 [5632, 2048], P(('dp', 'pair')), may hold values from -0.078125 to 0.078125
- cotangent: bfloat16 [2, 32, 64, 2048], P(None, ('dp', 'pair')), may hold values from -6 to 6
Outputs:
- layer_out: bfloat16 [2, 32, 64, 2048], P(None, ('dp', 'pair'))
- input_grad: float32 [2, 32, 64, 2048], P(None, ('dp', 'pair'))
- grad_attn_gain: float32 [2048], P(('dp', 'pair'))
- grad_query_weight: float32 [2048, 2048], P(('dp', 'pair'))
- grad_key_weight: float32 [2048, 2048], P(('dp', 'pair'))
- grad_value_weight: float32 [2048, 2048], P(('dp', 'pair'))
- grad_out_gate_weight: float32 [2048, 2048], P(('dp', 'pair'))
- grad_beta_weight: float32 [2048, 16], P(('dp', 'pair'))
- grad_query_conv: float32 [2048, 4], P(('dp', 'pair'))
- grad_key_conv: float32 [2048, 4], P(('dp', 'pair'))
- grad_value_conv: float32 [2048, 4], P(('dp', 'pair'))
- grad_head_gain: float32 [128], P(('dp', 'pair'))
- grad_out_weight: float32 [2048, 2048], P(('dp', 'pair'))
- grad_mlp_gain: float32 [2048], P(('dp', 'pair'))
- grad_mlp_gate_weight: float32 [2048, 5632], P(('dp', 'pair'))
- grad_mlp_up_weight: float32 [2048, 5632], P(('dp', 'pair'))
- grad_mlp_down_weight: float32 [5632, 2048], P(('dp', 'pair'))
The draws below stay inside these ranges and needn't reach their ends.
Inputs may be any that keep to these rules, and one draw needn't show every extreme that they name: `doc_starts`: position 0 of every sequence begins a document whatever its flag. The first seq_lengths positions of a sequence hold tokens, the rest is padding.
All inputs are finite; a program needn't handle non-finite values. No bound on the sum of `doc_starts` on one device may be relied on, other than what follows from the above.
Results may differ from the reference program's by a relative error of at most 0.0095.
The reference program's roundings to bfloat16 on the way count: a program that leaves them out, or rounds other values in their place, can miss the bound.
Values may be sent and summed in bfloat16 or wider, within the bound.
A program may use at most 352 MiB of HBM per device.

```python
import math
import jax
import jax.numpy as jnp
from jax import lax

D = 2048
H = 16
DK = 128
FF = 5632
CONV = 4
SPAN = 64
MICRO = 2
SEQ = 64
SEQS = 32


def draw_seq_lengths(key, part):
    drawn = jax.random.randint(key, (MICRO, SEQS), SEQ // 2, SEQ + 1)
    drawn = drawn.at[:, 0].set(SEQ)
    drawn = drawn.at[:, 1].set(SEQ // 2)
    return drawn.astype(jnp.int32)


def set_ends(entries, key, smallest, high):
    longest = entries.shape.index(max(entries.shape))
    spots = []
    for shift in (0, 1):
        where = [jax.random.randint(jax.random.fold_in(key, axis), (), 0, length) for axis, length in enumerate(entries.shape)]
        where[longest] = (where[longest] + shift) % entries.shape[longest]
        spots.append(tuple(where))
    return entries.at[spots[0]].set(smallest).at[spots[1]].set(high)


def with_spikes(values, own_key, source, target, parts, factor):
    owner, partner = [(jnp.arange(values.shape[axis_at]) // (values.shape[axis_at] // parts)).reshape([-1 if axis == axis_at else 1 for axis in range(values.ndim)]) for axis_at in (source, target)]
    chosen = jax.random.permutation(own_key, parts)[partner]
    strong = (owner == chosen) | (owner == (partner + parts // 2) % parts)
    return jnp.where(strong, factor * values, values)


def levels(rng, dims, pieces, low, largest):
    def one(axis_at, shards_of):
        draws = jax.random.uniform(jax.random.fold_in(jax.random.fold_in(rng, 6), axis_at), (shards_of,), jnp.float32, low / len(pieces), largest / len(pieces))
        return jnp.repeat(jnp.exp(draws), dims[axis_at] // shards_of).reshape((-1,) + (1,) * (len(dims) - axis_at - 1))

    level = one(*pieces[0])
    for cut in pieces[1:]:
        level = level * one(*cut)
    return level


def noise(key, extent, deviation, most, shards=(), held_as=jnp.bfloat16):
    values = jax.random.normal(key, extent, jnp.float32) * deviation
    if len(shards) > 0:
        values = levels(key, extent, shards, -0.22, 0.18) * values
    return jnp.clip(values, min=-most, max=most).astype(held_as)


def bell_draw_with(rng, dims, deviation, reach, split, heavy, held_as=jnp.bfloat16):
    values = deviation * jax.random.normal(rng, dims, jnp.float32)
    if split:
        values = values * levels(rng, dims, split, -0.22, 0.18)
    return jnp.clip(with_spikes(values, jax.random.fold_in(rng, 3), *heavy), -reach, reach).astype(held_as)


def setup_inputs(seed: int = 0) -> dict:
    splits = jax.random.split(jax.random.key(seed), 20)
    return {
        "tokens": bell_draw_with(splits[0], (MICRO, SEQS, SEQ, D), 1.0, 6.0, ((1, 32),), (1, 3, 32, 2.75)),
        "doc_starts": set_ends((jax.random.randint(splits[1], (MICRO, SEQS, SEQ), 0, 48) < 1).astype(jnp.int32), jax.random.fold_in(splits[1], 1), 0, 1),
        "seq_lengths": draw_seq_lengths(jax.random.fold_in(splits[19], 71), 0),
        "attn_gain": jnp.clip(1.0 + 0.15 * jax.random.normal(splits[3], (D,), jnp.float32), 0.25, 1.75).astype(jnp.bfloat16),
        "query_weight": noise(splits[4], (D, D), D ** -0.5, 0.125, ((0, 32),)),
        "key_weight": noise(splits[5], (D, D), D ** -0.5, 0.125, ((0, 32),)),
        "value_weight": noise(splits[6], (D, D), D ** -0.5, 0.125, ((0, 32),)),
        "out_gate_weight": noise(splits[7], (D, D), D ** -0.5, 0.125, ((0, 32),)),
        "beta_weight": noise(splits[8], (D, H), D ** -0.5, 0.125, ((0, 32),)),
        "query_conv": noise(splits[9], (D, CONV), CONV ** -0.5, 3.0, ((0, 32),)),
        "key_conv": noise(splits[10], (D, CONV), CONV ** -0.5, 3.0, ((0, 32),)),
        "value_conv": noise(splits[11], (D, CONV), CONV ** -0.5, 3.0, ((0, 32),)),
        "head_gain": jnp.clip(1.0 + 0.15 * jax.random.normal(splits[12], (DK,), jnp.float32), 0.25, 1.75).astype(jnp.bfloat16),
        "out_weight": noise(splits[13], (D, D), D ** -0.5, 0.125, ((0, 32),)),
        "mlp_gain": jnp.clip(1.0 + 0.15 * jax.random.normal(splits[14], (D,), jnp.float32), 0.25, 1.75).astype(jnp.bfloat16),
        "mlp_gate_weight": noise(splits[15], (D, FF), D ** -0.5, 0.125, ((0, 32),)),
        "mlp_up_weight": noise(splits[16], (D, FF), D ** -0.5, 0.125, ((0, 32),)),
        "mlp_down_weight": noise(splits[17], (FF, D), FF ** -0.5, 0.078125, ((0, 32),)),
        "cotangent": noise(splits[18], (MICRO, SEQS, SEQ, D), 1.0, 6.0, ((1, 32),)),
    }


EPS = 1e-05
HIGH = lax.Precision.HIGHEST

@jax.custom_vjp
def low(v):
    return lax.optimization_barrier(v.astype(jnp.bfloat16)).astype(jnp.float32)

@jax.custom_vjp
def low_back(v):
    return v

def low_keep(v):
    return (low(v), None)

def low_pass(kept, grad):
    return (grad,)

def back_keep(v):
    return (v, None)

def back_low(kept, grad):
    return (low(grad),)
low.defvjp(low_keep, low_pass)
low_back.defvjp(back_keep, back_low)

def normalize(values, gain):
    return values * lax.rsqrt(lax.optimization_barrier(jnp.mean(values * values, axis=-1, keepdims=True)) + EPS) * gain

def unit_heads(values):
    return values * lax.rsqrt(lax.optimization_barrier(jnp.sum(values * values, axis=-1, keepdims=True)) + 1e-06)

def document_ids(starts):
    position = lax.broadcasted_iota(jnp.int32, starts.shape, 1)
    flags = jnp.where(position == 0, 1, starts).astype(jnp.int32)
    return jnp.cumsum(flags, axis=-1).astype(jnp.int32)

def short_conv(values, taps, doc_ids):
    width = taps.shape[1]
    result = values * taps[:, width - 1]
    for offset in range(1, width):
        shifted = jnp.pad(values, ((0, 0), (offset, 0), (0, 0)))[:, :-offset]
        earlier = jnp.pad(doc_ids, ((0, 0), (offset, 0)), constant_values=-1)[:, :-offset]
        keep = (earlier == doc_ids).astype(jnp.float32)[..., None]
        result = result + shifted * keep * taps[:, width - 1 - offset]
    return result

def delta_rule(query, keys, values, beta, doc_ids):
    batch, length, heads, size = query.shape
    count = length // SPAN

    def blocks(array):
        return jnp.moveaxis(array.reshape(batch, count, SPAN, heads, -1), 3, 1)
    query_blocks = blocks(query)
    key_blocks = blocks(keys)
    value_blocks = blocks(values)
    beta_blocks = blocks(beta[..., None])[..., 0]
    doc_blocks = doc_ids.reshape(batch, count, SPAN)
    previous = jnp.concatenate([jnp.full((batch, 1), -1, jnp.int32), doc_blocks[:, :-1, SPAN - 1]], axis=1)
    carried = (doc_blocks == previous[:, :, None]).astype(jnp.float32)
    same = doc_blocks[:, :, :, None] == doc_blocks[:, :, None, :]
    row_index = lax.broadcasted_iota(jnp.int32, (SPAN, SPAN), 0)
    col_index = lax.broadcasted_iota(jnp.int32, (SPAN, SPAN), 1)
    strict = (same & (row_index > col_index)).astype(jnp.float32)[:, None]
    causal = (same & (row_index >= col_index)).astype(jnp.float32)[:, None]
    final_doc = same[:, :, SPAN - 1, :].astype(jnp.float32)
    key_gram = jnp.einsum('bhncd,bhnmd->bhncm', key_blocks, key_blocks, precision=HIGH)
    system = jnp.eye(SPAN, dtype=jnp.float32) + beta_blocks[..., None] * strict * key_gram
    weighted = beta_blocks[..., None]
    right = jnp.concatenate([weighted * value_blocks, weighted * carried[:, None, :, :, None] * key_blocks], axis=-1)
    solved = lax.linalg.triangular_solve(system, right, left_side=True, lower=True, unit_diagonal=True)
    value_size = value_blocks.shape[-1]
    fresh = solved[..., :value_size]
    carry_keys = solved[..., value_size:]
    query_key = jnp.einsum('bhncd,bhnmd->bhncm', query_blocks, key_blocks, precision=HIGH) * causal
    stacked = tuple((jnp.moveaxis(array, 2, 0) for array in (query_blocks, key_blocks, fresh, carry_keys, query_key)))
    kept_steps = jnp.moveaxis(carried, 1, 0)[:, :, None]
    tail_steps = jnp.moveaxis(final_doc, 1, 0)[:, :, None]
    last_steps = kept_steps[..., SPAN - 1]

    def advance(state, inputs):
        query_now, key_now, fresh_now, carry_now, mixed_now, kept, tail, last = inputs
        update = fresh_now - jnp.einsum('bhcd,bhed->bhce', carry_now, state, precision=HIGH)
        output = kept[..., None] * jnp.einsum('bhcd,bhed->bhce', query_now, state, precision=HIGH)
        output = output + jnp.einsum('bhcm,bhme->bhce', mixed_now, update, precision=HIGH)
        state = last[..., None, None] * state + jnp.einsum('bhme,bhmd->bhed', update * tail[..., None], key_now, precision=HIGH)
        return (state, output)
    start_state = jnp.zeros((batch, heads, value_size, size), jnp.float32)
    final_state, outputs = lax.scan(jax.checkpoint(advance), start_state, stacked + (kept_steps, tail_steps, last_steps))
    outputs = jnp.transpose(outputs, (1, 0, 3, 2, 4))
    return outputs.reshape(batch, length, heads, value_size)

def mixer_pre(query_proj, key_proj, value_proj, query_taps, key_taps, value_taps, doc_ids):
    batch, length, width = query_proj.shape
    query = unit_heads(jax.nn.silu(short_conv(query_proj, query_taps, doc_ids)).reshape(batch, length, -1, DK))
    keys = unit_heads(jax.nn.silu(short_conv(key_proj, key_taps, doc_ids)).reshape(batch, length, -1, DK))
    values = jax.nn.silu(short_conv(value_proj, value_taps, doc_ids)).reshape(batch, length, -1, DK)
    return (query, keys, values)

def mixer_core(query, keys, values, beta_logit, gate_proj, head_gain, doc_ids, live):
    batch, length = (query.shape[0], query.shape[1])
    beta = jax.nn.sigmoid(beta_logit) * live[..., None]
    mixed = delta_rule(query, keys, values, beta, doc_ids)
    gate_heads = jax.nn.silu(gate_proj.reshape(mixed.shape))
    normed = mixed * lax.rsqrt(lax.optimization_barrier(jnp.mean(mixed * mixed, axis=-1, keepdims=True)) + EPS) * head_gain * gate_heads
    return normed.reshape(batch, length, -1)

def project(values, weight):
    return jnp.einsum('gsd,de->gse', values, weight, precision=HIGH)

def layer_forward(tokens, params, doc_ids, live):
    attn_gain, query_weight, key_weight, value_weight, out_gate_weight, beta_weight, query_conv, key_conv, value_conv, head_gain, out_weight, mlp_gain, mlp_gate_weight, mlp_up_weight, mlp_down_weight = params
    normed_in = low(normalize(tokens, attn_gain))
    query_proj = low_back(project(normed_in, query_weight))
    key_proj = low_back(project(normed_in, key_weight))
    value_proj = low_back(project(normed_in, value_weight))
    gate_proj = low_back(project(normed_in, out_gate_weight))
    beta_logit = low_back(project(normed_in, beta_weight))
    query, keys, values = mixer_pre(query_proj, key_proj, value_proj, query_conv, key_conv, value_conv, doc_ids)
    mixed = low(mixer_core(low(query), low(keys), low(values), beta_logit, gate_proj, head_gain, doc_ids, live))
    resid = tokens + low_back(project(mixed, out_weight))
    normed_mid = low(normalize(resid, mlp_gain))
    gate_act = low_back(project(normed_mid, mlp_gate_weight))
    up_act = low_back(project(normed_mid, mlp_up_weight))
    hidden = low(jax.nn.silu(gate_act) * up_act)
    return resid + project(hidden, mlp_down_weight)

def group_pass(params, block_tokens, block_grad, block_starts, block_lengths):
    doc_ids = document_ids(block_starts)
    position = lax.broadcasted_iota(jnp.int32, block_starts.shape, 1)
    live = (position < block_lengths[:, None]).astype(jnp.float32)
    result, pull = jax.vjp(lambda values, weights: layer_forward(values, weights, doc_ids, live), block_tokens, params)
    grad_tokens, grad_params = pull(block_grad)
    return (result, grad_tokens, grad_params)

def reference(tokens, doc_starts, seq_lengths, attn_gain, query_weight, key_weight, value_weight, out_gate_weight, beta_weight, query_conv, key_conv, value_conv, head_gain, out_weight, mlp_gain, mlp_gate_weight, mlp_up_weight, mlp_down_weight, cotangent):
    params = tuple((weight.astype(jnp.float32) for weight in (attn_gain, query_weight, key_weight, value_weight, out_gate_weight, beta_weight, query_conv, key_conv, value_conv, head_gain, out_weight, mlp_gain, mlp_gate_weight, mlp_up_weight, mlp_down_weight)))
    total_seqs = MICRO * SEQS
    group = math.gcd(total_seqs, 16)
    groups = total_seqs // group
    token_groups = tokens.astype(jnp.float32).reshape(groups, group, SEQ, D)
    grad_groups = cotangent.astype(jnp.float32).reshape(groups, group, SEQ, D)
    start_groups = doc_starts.reshape(groups, group, SEQ)
    length_groups = seq_lengths.reshape(groups, group)

    def advance(totals, inputs):
        block_tokens, block_grad, block_starts, block_lengths = inputs
        result, grad_tokens, grad_params = group_pass(params, block_tokens, block_grad, block_starts, block_lengths)
        totals = tuple((earlier + added for earlier, added in zip(totals, grad_params)))
        return (totals, (result, grad_tokens))
    start_totals = tuple((jnp.zeros_like(weight) for weight in params))
    totals, (layer_full, input_grad) = lax.scan(advance, start_totals, (token_groups, grad_groups, start_groups, length_groups))
    layer_out = layer_full.reshape(tokens.shape).astype(jnp.bfloat16)
    return (layer_out, input_grad.reshape(tokens.shape), totals[0], totals[1], totals[2], totals[3], totals[4], totals[5], totals[6], totals[7], totals[8], totals[9], totals[10], totals[11], totals[12], totals[13], totals[14])
```

```python
import functools

import jax
import jax.numpy as jnp
from jax import lax
from jax.experimental import pallas as pl
from jax.experimental.pallas import tpu as pltpu
from jax.sharding import Mesh
from jax.sharding import PartitionSpec as P

DK = 128
EPS = 1e-05
L2EPS = 1e-06
CHUNK = 256
SEQ = 64
TAPS = 4
BF = jnp.bfloat16
F32 = jnp.float32
VMEM_LIMIT = 56 << 20


def mm(a, b, ca, cb):
    return lax.dot_general(a, b, (((ca,), (cb,)), ((), ())), preferred_element_type=F32)


def split(x):
    hi = x.astype(BF)
    return hi, (x - hi.astype(F32)).astype(BF)


def mm3(a, b, ca, cb):
    (ah, al), (bh, bl) = a, b
    out = mm(ah, bh, ca, cb)
    if bl is not None:
        out = out + mm(ah, bl, ca, cb)
    if al is not None:
        out = out + mm(al, bh, ca, cb)
    return out


def sigmoid(x):
    return 1.0 / (1.0 + jnp.exp(-x))


def iotas():
    row = lax.broadcasted_iota(jnp.int32, (CHUNK, CHUNK), 0)
    col = lax.broadcasted_iota(jnp.int32, (CHUNK, CHUNK), 1)
    return row, col


def unit_lower_inverse(a, row, col):
    eye = (row == col).astype(F32)
    x = eye - jnp.where((row // 2) == (col // 2), a, 0.0)
    size = 2
    while size < SEQ:
        off = jnp.where(
            ((row // (2 * size)) == (col // (2 * size))) & ((row // size) != (col // size)), a, 0.0
        )
        xs = split(x)
        y = mm3(split(off), xs, 1, 0)
        x = x - mm3(xs, split(y), 1, 0)
        size *= 2
    return x


def conv_forward(x, taps, base, masks):
    out = x * taps[base + TAPS - 1 : base + TAPS]
    for o in range(1, TAPS):
        out = out + pltpu.roll(x, o, 0) * masks[o - 1] * taps[base + TAPS - 1 - o : base + TAPS - o]
    return out


def unit(act):
    r = lax.rsqrt(jnp.sum(act * act, axis=-1, keepdims=True) + L2EPS)
    return act * r, r


def att_fwd_kernel(
    tok_ref, gain_ref, w_ref, wb_ref, taps_ref, hg_ref, hot_ref, wo_ref, meta_ref, doc_ref,
    nx_ref, proj_ref, bl_ref, t_ref, u_ref, o_ref, mixed_ref, part_ref,
):
    x = tok_ref[...].astype(F32)
    nx = (x * lax.rsqrt(jnp.mean(x * x, axis=-1, keepdims=True) + EPS) * gain_ref[...]).astype(BF)
    nx_ref[...] = nx
    proj = mm(nx, w_ref[...], 1, 0)
    proj_ref[...] = proj
    logits = mm(nx, wb_ref[...], 1, 0)
    logit = jnp.sum(logits * hot_ref[...], axis=-1, keepdims=True)
    bl_ref[...] = jnp.broadcast_to(logit, (CHUNK, DK))
    meta = meta_ref[...]
    doc = meta[:, 0:1]
    masks = [meta[:, o : o + 1] for o in range(1, TAPS)]
    beta = sigmoid(logit) * meta[:, 4:5]
    taps = taps_ref[...]
    acts = []
    for i in range(3):
        c = conv_forward(proj[:, i * DK : (i + 1) * DK], taps, i * TAPS, masks)
        acts.append(c * sigmoid(c))
    q = unit(acts[0])[0].astype(BF)
    k = unit(acts[1])[0].astype(BF)
    v = acts[2].astype(BF)
    row, col = iotas()
    same = doc == doc_ref[0]
    kk = mm(k, k, 1, 1)
    a = jnp.where(same & (row > col), beta * kk, 0.0)
    t = unit_lower_inverse(a, row, col)
    t_ref[...] = t
    u = mm3(split(t), split(beta * v.astype(F32)), 1, 0)
    u_ref[...] = u
    p = jnp.where(same & (row >= col), mm(q, k, 1, 1), 0.0)
    o = mm3(split(p), split(u), 1, 0)
    o_ref[...] = o
    gate = proj[:, 3 * DK :]
    n_o = o * lax.rsqrt(jnp.mean(o * o, axis=-1, keepdims=True) + EPS)
    mixed = (n_o * hg_ref[...] * (gate * sigmoid(gate))).astype(BF)
    mixed_ref[...] = mixed
    part_ref[...] = mm(mixed, wo_ref[...], 1, 0).astype(BF)


def att_bwd_kernel(
    ga_ref, wo_ref, proj_ref, bl_ref, t_ref, u_ref, o_ref, meta_ref, doc_ref, taps_ref, hg_ref, hot_ref, w_ref, wb_ref,
    gproj_ref, gb_ref, part_ref, gtaps_ref, ghg_ref,
):
    @pl.when(pl.program_id(0) == 0)
    def _():
        gtaps_ref[...] = jnp.zeros_like(gtaps_ref)
        ghg_ref[...] = jnp.zeros_like(ghg_ref)

    proj = proj_ref[...]
    meta = meta_ref[...]
    doc = meta[:, 0:1]
    masks = [meta[:, o : o + 1] for o in range(1, TAPS)]
    logit = bl_ref[:, 0:1]
    sig = sigmoid(logit)
    live = meta[:, 4:5]
    beta = sig * live
    taps = taps_ref[...]
    convs, sigs, acts = [], [], []
    for i in range(3):
        c = conv_forward(proj[:, i * DK : (i + 1) * DK], taps, i * TAPS, masks)
        s = sigmoid(c)
        convs.append(c)
        sigs.append(s)
        acts.append(c * s)
    uq, rq = unit(acts[0])
    uk, rk = unit(acts[1])
    q, k, v = uq.astype(BF), uk.astype(BF), acts[2].astype(BF)
    vf = v.astype(F32)

    gm = mm(ga_ref[...], wo_ref[...], 1, 1)
    o = o_ref[...]
    gate = proj[:, 3 * DK :]
    sg = sigmoid(gate)
    z = gate * sg
    r_o = lax.rsqrt(jnp.mean(o * o, axis=-1, keepdims=True) + EPS)
    n_o = o * r_o
    gmh = gm * hg_ref[...]
    e = gmh * z
    go = r_o * (e - n_o * jnp.mean(e * n_o, axis=-1, keepdims=True))
    ggate = gmh * n_o * (sg * (1.0 + gate * (1.0 - sg)))
    ghg_ref[0:1] += jnp.sum(gm * n_o * z, axis=0, keepdims=True)

    row, col = iotas()
    same = doc == doc_ref[0]
    strict = same & (row > col)
    causal = same & (row >= col)
    kk = mm(k, k, 1, 1)
    p = jnp.where(causal, mm(q, k, 1, 1), 0.0)
    us = split(u_ref[...])
    gos = split(go)
    dp = split(jnp.where(causal, mm3(gos, us, 1, 1), 0.0))
    du = mm3(split(p), gos, 0, 0)
    gq = mm3(dp, (k, None), 1, 0)
    gk = mm3(dp, (q, None), 0, 0)
    dw = mm3(split(t_ref[...]), split(du), 0, 0)
    da = jnp.where(strict, -mm3(split(dw), us, 1, 1), 0.0)
    gv = beta * dw
    gbeta = jnp.sum(dw * vf, axis=-1, keepdims=True) + jnp.sum(da * kk, axis=-1, keepdims=True)
    dkk = split(beta * da)
    gk = gk + mm3(dkk, (k, None), 1, 0) + mm3(dkk, (k, None), 0, 0)
    gbl = gbeta * live * sig * (1.0 - sig)
    gb = (gbl * hot_ref[...]).astype(BF)
    gb_ref[...] = gb

    gacts = [
        (gq - uq * jnp.sum(uq * gq, axis=-1, keepdims=True)) * rq,
        (gk - uk * jnp.sum(uk * gk, axis=-1, keepdims=True)) * rk,
        gv,
    ]
    for i in range(3):
        x = proj[:, i * DK : (i + 1) * DK]
        gc = gacts[i] * (sigs[i] * (1.0 + convs[i] * (1.0 - sigs[i])))
        base = i * TAPS
        gx = gc * taps[base + TAPS - 1 : base + TAPS]
        j = base + TAPS - 1
        gtaps_ref[j : j + 1] += jnp.sum(gc * x, axis=0, keepdims=True)
        for off in range(1, TAPS):
            gco = gc * masks[off - 1]
            j = base + TAPS - 1 - off
            gtaps_ref[j : j + 1] += jnp.sum(gco * pltpu.roll(x, off, 0), axis=0, keepdims=True)
            gx = gx + pltpu.roll(gco, CHUNK - off, 0) * taps[j : j + 1]
        gproj_ref[:, i * DK : (i + 1) * DK] = gx.astype(BF)
    gproj_ref[:, 3 * DK :] = ggate.astype(BF)
    part = mm(gproj_ref[...], w_ref[...], 1, 1) + mm(gb, wb_ref[...], 1, 1)
    part_ref[...] = part.astype(BF)


def rows(width):
    return pl.BlockSpec((CHUNK, width), lambda i: (i, 0))


def whole(shape):
    return pl.BlockSpec(shape, lambda i: (0,) * len(shape))


DOCROW = pl.BlockSpec((1, 1, CHUNK), lambda i: (i, 0, 0))


def att_forward(tok, gain, w, wb, taps, hg, hot, wo, meta, docs):
    count, width = tok.shape
    shape = jax.ShapeDtypeStruct
    return pl.pallas_call(
        att_fwd_kernel,
        grid=(count // CHUNK,),
        in_specs=[
            rows(width), whole((1, width)), whole(w.shape), whole(wb.shape), whole(taps.shape), whole((1, DK)),
            whole((1, DK)), whole(wo.shape), rows(DK), DOCROW,
        ],
        out_specs=[rows(width), rows(4 * DK), rows(DK), rows(CHUNK), rows(DK), rows(DK), rows(DK), rows(width)],
        out_shape=[
            shape((count, width), BF), shape((count, 4 * DK), F32), shape((count, DK), F32), shape((count, CHUNK), F32),
            shape((count, DK), F32), shape((count, DK), F32), shape((count, DK), BF), shape((count, width), BF),
        ],
        compiler_params=pltpu.CompilerParams(vmem_limit_bytes=VMEM_LIMIT),
        name="att_fwd",
    )(tok, gain, w, wb, taps, hg, hot, wo, meta, docs)


def att_backward(ga, wo, proj, bl, t, u, o, meta, docs, taps, hg, hot, w, wb):
    count, width = ga.shape
    shape = jax.ShapeDtypeStruct
    return pl.pallas_call(
        att_bwd_kernel,
        grid=(count // CHUNK,),
        in_specs=[
            rows(width), whole(wo.shape), rows(4 * DK), rows(DK), rows(CHUNK), rows(DK), rows(DK), rows(DK), DOCROW,
            whole(taps.shape), whole((1, DK)), whole((1, DK)), whole(w.shape), whole(wb.shape),
        ],
        out_specs=[rows(4 * DK), rows(DK), rows(width), whole((16, DK)), whole((8, DK))],
        out_shape=[
            shape((count, 4 * DK), BF), shape((count, DK), BF), shape((count, width), BF), shape((16, DK), F32),
            shape((8, DK), F32),
        ],
        compiler_params=pltpu.CompilerParams(vmem_limit_bytes=VMEM_LIMIT),
        name="att_bwd",
    )(ga, wo, proj, bl, t, u, o, meta, docs, taps, hg, hot, w, wb)


def gather_tokens(x):
    return lax.all_gather(x, "m", axis=0, tiled=True)


def scatter_tokens(x):
    return lax.psum_scatter(x, "m", scatter_dimension=0, tiled=True).astype(F32)


def norm_stats(x):
    return lax.rsqrt(jnp.mean(x * x, axis=-1, keepdims=True) + EPS)


def norm_back(grad, x, r, gain):
    n = x * r
    e = grad * gain
    return r * (e - n * jnp.mean(e * n, axis=-1, keepdims=True)), jnp.sum(grad * n, axis=0)


def exchange_groups(x, groups):
    me = lax.axis_index("g")
    total = lax.dynamic_index_in_dim(x, me, 0, keepdims=False)
    for step in range(1, groups):
        perm = [(i, (i + step) % groups) for i in range(groups)]
        piece = lax.dynamic_index_in_dim(x, lax.rem(me + step, groups), 0, keepdims=False).astype(BF)
        total = total + lax.ppermute(piece, "g", perm).astype(F32)
    return total


def make_shards(groups, members):
    def shards(
        tokens, doc_starts, seq_lengths, attn_gain, query_weight, key_weight, value_weight, out_gate_weight, beta_weight,
        query_conv, key_conv, value_conv, head_gain, out_weight, mlp_gain, mlp_gate_weight, mlp_up_weight,
        mlp_down_weight, cotangent,
    ):
        n = groups * members
        width = tokens.shape[-1]
        r = attn_gain.shape[0]
        f = mlp_down_weight.shape[0]
        hgr = head_gain.shape[0]
        heads = beta_weight.shape[1]
        rho = DK // r
        srange = members // rho
        me_g, me_m = lax.axis_index("g"), lax.axis_index("m")
        head = lax.rem(me_m, rho) * srange + me_m // rho
        seqs = tokens.shape[0] * tokens.shape[1]
        seq = tokens.shape[2]
        own = seqs * seq
        flat_bf = tokens.reshape(own, width)
        flat = flat_bf.astype(F32)
        grad_out = cotangent.reshape(own, width)

        position = lax.broadcasted_iota(jnp.int32, (seqs, seq), 1)
        starts = doc_starts.reshape(seqs, seq)
        doc_ids = jnp.cumsum(jnp.where(position == 0, 1, starts), axis=-1) - 1
        live = position < seq_lengths.reshape(seqs, 1)

        pieces = [attn_gain, mlp_gain, head_gain, beta_weight.reshape(-1), query_conv.reshape(-1), key_conv.reshape(-1),
                  value_conv.reshape(-1), doc_ids.astype(BF).reshape(-1), live.astype(BF).reshape(-1)]
        sizes = [p.shape[0] for p in pieces]
        pack = jnp.concatenate(pieces)
        total = -(-pack.shape[0] // 2048) * 2048
        pack = jnp.pad(pack, (0, total - pack.shape[0])).reshape(-1, 128)
        packs = lax.all_gather(lax.all_gather(pack, "m", axis=0), "g", axis=0).reshape(n, total)
        parts, at = [], 0
        for s in sizes:
            parts.append(packs[:, at : at + s])
            at += s
        gain_in = parts[0].reshape(1, width).astype(F32)
        gain_mid = parts[1].reshape(1, width).astype(F32)
        hg = parts[2].reshape(1, DK).astype(F32)
        beta_full = jnp.pad(parts[3].reshape(width, heads), ((0, 0), (0, DK - heads)))
        taps = [
            lax.dynamic_slice_in_dim(p.reshape(width, TAPS), head * DK, DK, 0).astype(F32).T for p in parts[4:7]
        ]
        taps = jnp.concatenate(taps + [jnp.zeros((4, DK), F32)], axis=0)
        group_docs = lax.dynamic_slice_in_dim(parts[7], me_g * members, members, 0).astype(F32)
        group_live = lax.dynamic_slice_in_dim(parts[8], me_g * members, members, 0).astype(F32)
        count = members * own
        seq_of = jnp.arange(count, dtype=jnp.int32) // seq
        docs = group_docs.reshape(count) + seq_of.astype(F32) * seq
        columns = [docs] + [
            jnp.where(jnp.pad(docs, (o, 0), constant_values=-1.0)[:count] == docs, 1.0, 0.0) for o in range(1, TAPS)
        ] + [group_live.reshape(count)]
        meta = jnp.pad(jnp.stack(columns, axis=1), ((0, 0), (0, DK - len(columns))))
        docs_row = docs.reshape(count // CHUNK, 1, CHUNK)
        hot = (jnp.arange(DK) == head).astype(F32).reshape(1, DK)

        def by_member(w):
            return w.reshape(r, groups, srange, DK).transpose(2, 1, 0, 3).reshape(members, r, DK)

        def ff_by_member(w):
            return w.reshape(r, groups, members, f).transpose(2, 0, 1, 3).reshape(members, r, groups * f)

        att_cols = jnp.concatenate(
            [by_member(w) for w in (query_weight, key_weight, value_weight, out_gate_weight)], axis=-1
        )
        att_cols = lax.all_to_all(att_cols, "m", 0, 0, tiled=True).reshape(members * r, 4 * DK)
        w_att = lax.all_gather(att_cols, "g", axis=0, tiled=True)
        w_out = lax.all_gather(out_weight, "g", axis=0)
        groups_of_rho = [[s * rho + i for i in range(rho)] for s in range(srange)]
        w_out = lax.all_to_all(w_out, "m", 0, 0, axis_index_groups=groups_of_rho, tiled=True).reshape(DK, width)
        ff_cols = jnp.stack([ff_by_member(mlp_gate_weight), ff_by_member(mlp_up_weight)], axis=1)
        ff_cols = lax.all_to_all(ff_cols, "m", 0, 0, tiled=True)
        w_gate = lax.all_gather(ff_cols[:, 0].reshape(members * r, groups * f), "g", axis=0, tiled=True)
        w_up = lax.all_gather(ff_cols[:, 1].reshape(members * r, groups * f), "g", axis=0, tiled=True)
        w_down = lax.all_gather(mlp_down_weight, "g", axis=0, tiled=True)

        tok_all = gather_tokens(flat_bf)
        cot_all = gather_tokens(grad_out)
        nx, proj, bl, t, u, o, mixed, part = att_forward(
            tok_all, gain_in, w_att, beta_full, taps, hg, hot, w_out, meta, docs_row
        )
        resid = flat + scatter_tokens(part)
        r_mid = norm_stats(resid)
        nm = gather_tokens((resid * r_mid * gain_mid).astype(BF))
        gate_act = mm(nm, w_gate, 1, 0)
        up_act = mm(nm, w_up, 1, 0)
        sg = jax.nn.sigmoid(gate_act)
        hidden = (gate_act * sg * up_act).astype(BF)
        grad_hidden = mm(cot_all, w_down, 1, 1)
        gg = (grad_hidden * up_act * (sg * (1.0 + gate_act * (1.0 - sg)))).astype(BF)
        gu = (grad_hidden * (gate_act * sg)).astype(BF)
        gmid = scatter_tokens((mm(gg, w_gate, 1, 1) + mm(gu, w_up, 1, 1)).astype(BF))
        layer_out = (resid + scatter_tokens(mm(hidden, w_down, 1, 0).astype(BF))).astype(BF)
        back, g_mid_gain = norm_back(gmid, resid, r_mid, gain_mid)
        grad_resid = grad_out.astype(F32) + back
        ga = gather_tokens(grad_resid.astype(BF))
        gproj, gb, gpart, gtaps, ghg = att_backward(
            ga, w_out, proj, bl, t, u, o, meta, docs_row, taps, hg, hot, w_att, beta_full
        )
        grad_in = scatter_tokens(gpart)
        back, g_in_gain = norm_back(grad_in, flat, norm_stats(flat), gain_in)
        input_grad = grad_resid + back

        g_down = exchange_groups(mm(hidden, cot_all, 0, 0).reshape(groups, f, width), groups)
        g_ff = []
        for grad in (gg, gu):
            piece = exchange_groups(mm(nm, grad, 0, 0).reshape(groups, members * r, groups * f), groups)
            g_ff.append(piece.reshape(members, r, groups * f))
        g_ff = lax.all_to_all(jnp.stack(g_ff, axis=1), "m", 0, 0, tiled=True)
        g_ff = g_ff.reshape(members, 2, r, groups, f).transpose(1, 2, 3, 0, 4).reshape(2, r, -1)
        g_out = lax.all_to_all(
            mm(mixed, ga, 0, 0).reshape(rho, r, width), "m", 0, 0, axis_index_groups=groups_of_rho, tiled=True
        )
        g_out = exchange_groups(g_out, groups)
        g_att = exchange_groups(mm(nx, gproj, 0, 0).reshape(groups, members * r, 4 * DK), groups)
        g_att = lax.all_to_all(g_att.reshape(members, r, 4 * DK), "m", 0, 0, tiled=True)
        g_att = g_att.reshape(srange, groups, r, 4, DK).transpose(3, 2, 1, 0, 4).reshape(4, r, width)

        g_beta = mm(nx, gb, 0, 0)[:, :heads].reshape(n, r * heads)
        at_head = lambda x: lax.dynamic_update_slice_in_dim(
            jnp.zeros((width, TAPS), F32), x.T, head * DK, 0
        ).reshape(n, r * TAPS)
        small = jnp.concatenate(
            [g_in_gain.reshape(n, r), g_mid_gain.reshape(n, r), ghg[0].reshape(n, hgr), g_beta]
            + [at_head(gtaps[i * TAPS : (i + 1) * TAPS]) for i in range(3)],
            axis=1,
        )
        small = lax.psum_scatter(
            small.reshape(groups, members, -1).transpose(1, 0, 2), "m", scatter_dimension=0, tiled=True
        )
        small = lax.psum_scatter(small[0], "g", scatter_dimension=0, tiled=True).reshape(-1)
        outs, at = [], 0
        for shape in ((r,), (r,), (hgr,), (r, heads), (r, TAPS), (r, TAPS), (r, TAPS)):
            size = 1
            for s in shape:
                size *= s
            outs.append(small[at : at + size].reshape(shape))
            at += size
        s_in, s_mid, s_hg, s_beta, s_q, s_k, s_v = outs
        return (
            layer_out.reshape(tokens.shape), input_grad.reshape(tokens.shape),
            s_in, g_att[0], g_att[1], g_att[2], g_att[3], s_beta, s_q, s_k, s_v, s_hg, g_out, s_mid, g_ff[0], g_ff[1],
            g_down,
        )

    return shards


def solution(mesh):
    n = mesh.devices.size
    members = 16
    groups = n // members
    inner = Mesh(mesh.devices.reshape(groups, members), ("g", "m"))
    both = ("g", "m")
    acts, mat, vec = P(None, both, None, None), P(both, None), P(both)
    return jax.shard_map(
        make_shards(groups, members),
        mesh=inner,
        in_specs=(acts, P(None, both, None), P(None, both), vec, mat, mat, mat, mat, mat, mat, mat, mat, vec, mat, vec,
                  mat, mat, mat, acts),
        out_specs=(acts, acts, vec, mat, mat, mat, mat, mat, mat, mat, mat, vec, mat, vec, mat, mat, mat),
        check_vma=False,
    )
```

```python
import functools

import jax
import jax.numpy as jnp
from jax import lax
from jax.experimental import pallas as pl
from jax.experimental.pallas import tpu as pltpu
from jax.sharding import Mesh
from jax.sharding import PartitionSpec as P

DK = 128
EPS = 1e-05
L2EPS = 1e-06
CHUNK = 256
SEQ = 64
TAPS = 4
BF = jnp.bfloat16
F32 = jnp.float32
VMEM_LIMIT = 56 << 20


def mm(a, b, ca, cb):
    return lax.dot_general(a, b, (((ca,), (cb,)), ((), ())), preferred_element_type=F32)


def split(x):
    hi = x.astype(BF)
    return hi, (x - hi.astype(F32)).astype(BF)


def mm3(a, b, ca, cb):
    (ah, al), (bh, bl) = a, b
    out = mm(ah, bh, ca, cb)
    if bl is not None:
        out = out + mm(ah, bl, ca, cb)
    if al is not None:
        out = out + mm(al, bh, ca, cb)
    return out


def sigmoid(x):
    return 1.0 / (1.0 + jnp.exp(-x))


def iotas():
    row = lax.broadcasted_iota(jnp.int32, (CHUNK, CHUNK), 0)
    col = lax.broadcasted_iota(jnp.int32, (CHUNK, CHUNK), 1)
    return row, col


def unit_lower_inverse(a, row, col):
    eye = (row == col).astype(F32)
    x = eye - jnp.where((row // 2) == (col // 2), a, 0.0)
    size = 2
    while size < SEQ:
        off = jnp.where(
            ((row // (2 * size)) == (col // (2 * size))) & ((row // size) != (col // size)), a, 0.0
        )
        xs = split(x)
        y = mm3(split(off), xs, 1, 0)
        x = x - mm3(xs, split(y), 1, 0)
        size *= 2
    return x


def conv_forward(x, taps, base, masks):
    out = x * taps[base + TAPS - 1 : base + TAPS]
    for o in range(1, TAPS):
        out = out + pltpu.roll(x, o, 0) * masks[o - 1] * taps[base + TAPS - 1 - o : base + TAPS - o]
    return out


def unit(act):
    r = lax.rsqrt(jnp.sum(act * act, axis=-1, keepdims=True) + L2EPS)
    return act * r, r


def att_fwd_kernel(
    tok_ref, gain_ref, w_ref, wb_ref, taps_ref, hg_ref, hot_ref, wo_ref, meta_ref, doc_ref,
    nx_ref, proj_ref, bl_ref, t_ref, u_ref, o_ref, mixed_ref, part_ref,
):
    x = tok_ref[...].astype(F32)
    nx = (x * lax.rsqrt(jnp.mean(x * x, axis=-1, keepdims=True) + EPS) * gain_ref[...]).astype(BF)
    nx_ref[...] = nx
    proj = mm(nx, w_ref[...], 1, 0)
    proj_ref[...] = proj
    logits = mm(nx, wb_ref[...], 1, 0)
    logit = jnp.sum(logits * hot_ref[...], axis=-1, keepdims=True)
    bl_ref[...] = jnp.broadcast_to(logit, (CHUNK, DK))
    meta = meta_ref[...]
    doc = meta[:, 0:1]
    masks = [meta[:, o : o + 1] for o in range(1, TAPS)]
    beta = sigmoid(logit) * meta[:, 4:5]
    taps = taps_ref[...]
    acts = []
    for i in range(3):
        c = conv_forward(proj[:, i * DK : (i + 1) * DK], taps, i * TAPS, masks)
        acts.append(c * sigmoid(c))
    q = unit(acts[0])[0].astype(BF)
    k = unit(acts[1])[0].astype(BF)
    v = acts[2].astype(BF)
    row, col = iotas()
    same = doc == doc_ref[0]
    kk = mm(k, k, 1, 1)
    a = jnp.where(same & (row > col), beta * kk, 0.0)
    t = unit_lower_inverse(a, row, col)
    t_ref[...] = t
    u = mm3(split(t), split(beta * v.astype(F32)), 1, 0)
    u_ref[...] = u
    p = jnp.where(same & (row >= col), mm(q, k, 1, 1), 0.0)
    o = mm3(split(p), split(u), 1, 0)
    o_ref[...] = o
    gate = proj[:, 3 * DK :]
    n_o = o * lax.rsqrt(jnp.mean(o * o, axis=-1, keepdims=True) + EPS)
    mixed = (n_o * hg_ref[...] * (gate * sigmoid(gate))).astype(BF)
    mixed_ref[...] = mixed
    part_ref[...] = mm(mixed, wo_ref[...], 1, 0).astype(BF)


def att_bwd_kernel(
    ga_ref, wo_ref, proj_ref, bl_ref, t_ref, u_ref, o_ref, meta_ref, doc_ref, taps_ref, hg_ref, hot_ref, w_ref, wb_ref,
    gproj_ref, gb_ref, part_ref, gtaps_ref, ghg_ref,
):
    @pl.when(pl.program_id(0) == 0)
    def _():
        gtaps_ref[...] = jnp.zeros_like(gtaps_ref)
        ghg_ref[...] = jnp.zeros_like(ghg_ref)

    proj = proj_ref[...]
    meta = meta_ref[...]
    doc = meta[:, 0:1]
    masks = [meta[:, o : o + 1] for o in range(1, TAPS)]
    logit = bl_ref[:, 0:1]
    sig = sigmoid(logit)
    live = meta[:, 4:5]
    beta = sig * live
    taps = taps_ref[...]
    convs, sigs, acts = [], [], []
    for i in range(3):
        c = conv_forward(proj[:, i * DK : (i + 1) * DK], taps, i * TAPS, masks)
        s = sigmoid(c)
        convs.append(c)
        sigs.append(s)
        acts.append(c * s)
    uq, rq = unit(acts[0])
    uk, rk = unit(acts[1])
    q, k, v = uq.astype(BF), uk.astype(BF), acts[2].astype(BF)
    vf = v.astype(F32)

    gm = mm(ga_ref[...], wo_ref[...], 1, 1)
    o = o_ref[...]
    gate = proj[:, 3 * DK :]
    sg = sigmoid(gate)
    z = gate * sg
    r_o = lax.rsqrt(jnp.mean(o * o, axis=-1, keepdims=True) + EPS)
    n_o = o * r_o
    gmh = gm * hg_ref[...]
    e = gmh * z
    go = r_o * (e - n_o * jnp.mean(e * n_o, axis=-1, keepdims=True))
    ggate = gmh * n_o * (sg * (1.0 + gate * (1.0 - sg)))
    ghg_ref[0:1] += jnp.sum(gm * n_o * z, axis=0, keepdims=True)

    row, col = iotas()
    same = doc == doc_ref[0]
    strict = same & (row > col)
    causal = same & (row >= col)
    kk = mm(k, k, 1, 1)
    p = jnp.where(causal, mm(q, k, 1, 1), 0.0)
    us = split(u_ref[...])
    gos = split(go)
    dp = split(jnp.where(causal, mm3(gos, us, 1, 1), 0.0))
    du = mm3(split(p), gos, 0, 0)
    gq = mm3(dp, (k, None), 1, 0)
    gk = mm3(dp, (q, None), 0, 0)
    dw = mm3(split(t_ref[...]), split(du), 0, 0)
    da = jnp.where(strict, -mm3(split(dw), us, 1, 1), 0.0)
    gv = beta * dw
    gbeta = jnp.sum(dw * vf, axis=-1, keepdims=True) + jnp.sum(da * kk, axis=-1, keepdims=True)
    dkk = split(beta * da)
    gk = gk + mm3(dkk, (k, None), 1, 0) + mm3(dkk, (k, None), 0, 0)
    gbl = gbeta * live * sig * (1.0 - sig)
    gb = (gbl * hot_ref[...]).astype(BF)
    gb_ref[...] = gb

    gacts = [
        (gq - uq * jnp.sum(uq * gq, axis=-1, keepdims=True)) * rq,
        (gk - uk * jnp.sum(uk * gk, axis=-1, keepdims=True)) * rk,
        gv,
    ]
    for i in range(3):
        x = proj[:, i * DK : (i + 1) * DK]
        gc = gacts[i] * (sigs[i] * (1.0 + convs[i] * (1.0 - sigs[i])))
        base = i * TAPS
        gx = gc * taps[base + TAPS - 1 : base + TAPS]
        j = base + TAPS - 1
        gtaps_ref[j : j + 1] += jnp.sum(gc * x, axis=0, keepdims=True)
        for off in range(1, TAPS):
            gco = gc * masks[off - 1]
            j = base + TAPS - 1 - off
            gtaps_ref[j : j + 1] += jnp.sum(gco * pltpu.roll(x, off, 0), axis=0, keepdims=True)
            gx = gx + pltpu.roll(gco, CHUNK - off, 0) * taps[j : j + 1]
        gproj_ref[:, i * DK : (i + 1) * DK] = gx.astype(BF)
    gproj_ref[:, 3 * DK :] = ggate.astype(BF)
    part = mm(gproj_ref[...], w_ref[...], 1, 1) + mm(gb, wb_ref[...], 1, 1)
    part_ref[...] = part.astype(BF)


def rows(width):
    return pl.BlockSpec((CHUNK, width), lambda i: (i, 0))


def whole(shape):
    return pl.BlockSpec(shape, lambda i: (0,) * len(shape))


DOCROW = pl.BlockSpec((1, 1, CHUNK), lambda i: (i, 0, 0))


def att_forward(tok, gain, w, wb, taps, hg, hot, wo, meta, docs):
    count, width = tok.shape
    shape = jax.ShapeDtypeStruct
    return pl.pallas_call(
        att_fwd_kernel,
        grid=(count // CHUNK,),
        in_specs=[
            rows(width), whole((1, width)), whole(w.shape), whole(wb.shape), whole(taps.shape), whole((1, DK)),
            whole((1, DK)), whole(wo.shape), rows(DK), DOCROW,
        ],
        out_specs=[rows(width), rows(4 * DK), rows(DK), rows(CHUNK), rows(DK), rows(DK), rows(DK), rows(width)],
        out_shape=[
            shape((count, width), BF), shape((count, 4 * DK), F32), shape((count, DK), F32), shape((count, CHUNK), F32),
            shape((count, DK), F32), shape((count, DK), F32), shape((count, DK), BF), shape((count, width), BF),
        ],
        compiler_params=pltpu.CompilerParams(vmem_limit_bytes=VMEM_LIMIT),
        name="att_fwd",
    )(tok, gain, w, wb, taps, hg, hot, wo, meta, docs)


def att_backward(ga, wo, proj, bl, t, u, o, meta, docs, taps, hg, hot, w, wb):
    count, width = ga.shape
    shape = jax.ShapeDtypeStruct
    return pl.pallas_call(
        att_bwd_kernel,
        grid=(count // CHUNK,),
        in_specs=[
            rows(width), whole(wo.shape), rows(4 * DK), rows(DK), rows(CHUNK), rows(DK), rows(DK), rows(DK), DOCROW,
            whole(taps.shape), whole((1, DK)), whole((1, DK)), whole(w.shape), whole(wb.shape),
        ],
        out_specs=[rows(4 * DK), rows(DK), rows(width), whole((16, DK)), whole((8, DK))],
        out_shape=[
            shape((count, 4 * DK), BF), shape((count, DK), BF), shape((count, width), BF), shape((16, DK), F32),
            shape((8, DK), F32),
        ],
        compiler_params=pltpu.CompilerParams(vmem_limit_bytes=VMEM_LIMIT),
        name="att_bwd",
    )(ga, wo, proj, bl, t, u, o, meta, docs, taps, hg, hot, w, wb)


MESH = pl.DeviceIdType.MESH
CORE = 1
BITS = (2, 4, 8)
COLS = ((0, 640), (640, 640), (1280, 768))
ANY = pl.BlockSpec(memory_space=pl.ANY)
VM = pl.BlockSpec(memory_space=pltpu.VMEM)


def flip(me, mask):
    out = me
    bit = 1
    while bit <= mask:
        if mask & bit:
            out = out + bit * (1 - 2 * lax.rem(me // bit, 2))
        bit *= 2
    return out


def order_of(j):
    return [BITS[(j + i) % 3] for i in range(3)]


def greet_cube(me_g, me):
    barrier = pltpu.get_barrier_semaphore()
    for bit in (CORE,) + BITS:
        pl.semaphore_signal(barrier, inc=1, device_id=(me_g, flip(me, bit)), device_id_type=MESH)
    pl.semaphore_wait(barrier, 1 + len(BITS))


def remote(src, dst, send, recv, g, m):
    return pltpu.make_async_remote_copy(
        src_ref=src, dst_ref=dst, send_sem=send, recv_sem=recv, device_id=(g, m), device_id_type=MESH
    )


class CubeGather:
    def __init__(self, me_g, me, block, out, local, link_send, link_recv, core_send, core_recv):
        self.me_g, self.me, self.block, self.out = me_g, me, block, out
        self.local, self.ls, self.lr, self.cs, self.cr = local, link_send, link_recv, core_send, core_recv
        self.sent = []

    def view(self, slot, j):
        at, size = COLS[j]
        return self.out.at[slot, :, pl.ds(at, size)]

    def source(self, mask, j):
        at, size = COLS[j]
        return self.block.at[:, pl.ds(at, size)] if mask == 0 else self.view(flip(self.me, mask), j)

    def hop(self, mask, j, step, count):
        bit = order_of(j)[step]
        slot = flip(self.me, mask)
        i = (1 << step) - 1 + count
        copy = remote(
            self.source(mask, j), self.view(slot, j), self.ls.at[j, i], self.lr.at[j, i], self.me_g, flip(self.me, bit)
        )
        copy.start()
        self.sent.append(copy)

    def core(self, mask, j):
        i = mask // 2
        copy = remote(
            self.source(mask, j), self.view(flip(self.me, mask), j), self.cs.at[j, i], self.cr.at[j, i], self.me_g,
            flip(self.me, CORE),
        )
        copy.start()
        self.sent.append(copy)

    def masks(self, j, step):
        held = [0]
        for bit in order_of(j)[:step]:
            held = held + [h + bit for h in held]
        return held

    def start(self):
        self.own = pltpu.make_async_copy(self.block, self.out.at[self.me], self.local)
        self.own.start()
        for j in range(3):
            self.hop(0, j, 0, 0)
        for j in range(3):
            self.core(0, j)

    def arrive(self, j, step):
        bit = order_of(j)[step]
        got = []
        for count, mask in enumerate(self.masks(j, step)):
            i = (1 << step) - 1 + count
            slot = flip(self.me, mask + bit)
            remote(
                self.view(slot, j), self.view(slot, j), self.ls.at[j, i], self.lr.at[j, i], self.me_g, flip(self.me, bit)
            ).wait_recv()
            got.append(mask + bit)
        return got

    def advance(self, step):
        for j in range(3):
            got = self.arrive(j, step)
            if step < 2:
                for count, mask in enumerate(self.masks(j, step + 1)):
                    self.hop(mask, j, step + 1, count)
            for mask in got:
                self.core(mask, j)

    def finish(self):
        for j in range(3):
            for mask in range(0, 16, 2):
                slot = flip(self.me, mask + CORE)
                remote(
                    self.view(slot, j), self.view(slot, j), self.cs.at[j, mask // 2], self.cr.at[j, mask // 2], self.me_g,
                    flip(self.me, CORE),
                ).wait_recv()
        for copy in self.sent:
            copy.wait_send()
        self.own.wait()


GATHER_SEMS = [
    pltpu.SemaphoreType.DMA(()), pltpu.SemaphoreType.DMA((3, 7)), pltpu.SemaphoreType.DMA((3, 7)),
    pltpu.SemaphoreType.DMA((3, 8)), pltpu.SemaphoreType.DMA((3, 8)),
]


class CubeScatter:
    def __init__(self, me_g, me, part, mine, other, sums, got, local, core_send, core_recv, link_send, link_recv):
        self.me_g, self.me, self.part, self.mine, self.other = me_g, me, part, mine, other
        self.sums, self.got, self.local = sums, got, local
        self.cs, self.cr, self.ls, self.lr = core_send, core_recv, link_send, link_recv
        self.sent = []

    ORDER = (14, 6, 10, 12, 2, 4, 8, 0)

    def core_copy(self, mask):
        i = mask // 2
        return remote(
            self.part.at[flip(self.me, mask + CORE)], self.other.at[i], self.cs.at[i], self.cr.at[i], self.me_g,
            flip(self.me, CORE),
        )

    def load_copy(self, mask):
        i = mask // 2
        return pltpu.make_async_copy(self.part.at[flip(self.me, mask)], self.mine.at[i], self.local.at[i])

    def masks(self, j, step):
        b = order_of(j)
        rest = [0]
        for bit in b[step + 1 :]:
            rest = rest + [h + bit for h in rest]
        return [b[step] + h for h in rest]

    def slot(self, j, step, mask):
        return (0, 4, 6)[step] + self.masks(j, step).index(mask)

    def copy(self, j, step, mask):
        bit = order_of(j)[step]
        i = self.slot(j, step, mask)
        at, size = COLS[j]
        return remote(
            self.sums.at[i, :, pl.ds(at, size)], self.got.at[i, :, pl.ds(at, size)], self.ls.at[j, i], self.lr.at[j, i],
            self.me_g, flip(self.me, bit),
        )

    def total(self, j, mask, steps):
        at, size = COLS[j]
        i = mask // 2
        x = self.mine[i, :, at : at + size].astype(F32) + self.other[i, :, at : at + size].astype(F32)
        for step in range(steps):
            k = self.slot(j, step, mask + order_of(j)[step])
            x = x + self.got[k, :, at : at + size].astype(F32)
        return x

    def send(self, j, step, mask):
        at, size = COLS[j]
        self.sums[self.slot(j, step, mask), :, at : at + size] = self.total(j, mask, step).astype(BF)
        copy = self.copy(j, step, mask)
        copy.start()
        self.sent.append(copy)

    def start(self):
        for mask in self.ORDER:
            copy = self.core_copy(mask)
            copy.start()
            self.sent.append(copy)
            self.load_copy(mask).start()

    def run(self, out):
        for mask in self.ORDER:
            self.core_copy(mask).wait_recv()
            self.load_copy(mask).wait()
            for j in range(3):
                if mask in self.masks(j, 0):
                    self.send(j, 0, mask)
        for step in (1, 2):
            for j in range(3):
                bits = order_of(j)
                for mask in self.masks(j, step):
                    for earlier in range(step):
                        self.copy(j, earlier, mask + bits[earlier]).wait_recv()
                    self.send(j, step, mask)
        for j in range(3):
            at, size = COLS[j]
            for step in range(3):
                self.copy(j, step, order_of(j)[step]).wait_recv()
            out[:, at : at + size] = self.total(j, 0, 3)

    def finish(self):
        for copy in self.sent:
            copy.wait_send()


def scatter_scratch(rows, width):
    return [
        pltpu.VMEM((8, rows, width), BF), pltpu.VMEM((8, rows, width), BF), pltpu.VMEM((7, rows, width), BF),
        pltpu.VMEM((7, rows, width), BF), pltpu.SemaphoreType.DMA((8,)), pltpu.SemaphoreType.DMA((8,)),
        pltpu.SemaphoreType.DMA((8,)), pltpu.SemaphoreType.DMA((3, 7)), pltpu.SemaphoreType.DMA((3, 7)),
    ]


NS = 9
NG = len(GATHER_SEMS)


def middle_forward(got, flat, gain):
    resid = flat.astype(F32) + got
    r = lax.rsqrt(jnp.mean(resid * resid, axis=-1, keepdims=True) + EPS)
    return resid, (resid * r * gain).astype(BF)


def norm_backward(grad, x, gain):
    r = lax.rsqrt(jnp.mean(x * x, axis=-1, keepdims=True) + EPS)
    n = x * r
    e = grad * gain
    return r * (e - n * jnp.mean(e * n, axis=-1, keepdims=True)), jnp.sum(grad * n, axis=0, keepdims=True)


def forward_turn_kernel(part, flat, gain, resid, out, total, block, *sems):
    me_g, me = lax.axis_index("g"), lax.axis_index("m")
    greet_cube(me_g, me)
    scatter = CubeScatter(me_g, me, part, *sems[:NS])
    scatter.start()
    scatter.run(total)
    resid[...], block[...] = middle_forward(total[...], flat[...], gain[...])
    gather = CubeGather(me_g, me, block, out, *sems[NS:])
    gather.start()
    for step in range(3):
        gather.advance(step)
    gather.finish()
    scatter.finish()


def backward_turn_kernel(part, resid, gain, cot, grad_resid, ggain, out, total, block, *sems):
    me_g, me = lax.axis_index("g"), lax.axis_index("m")
    greet_cube(me_g, me)
    scatter = CubeScatter(me_g, me, part, *sems[:NS])
    scatter.start()
    scatter.run(total)
    back, gsum = norm_backward(total[...], resid[...], gain[...])
    grad = cot[...].astype(F32) + back
    grad_resid[...] = grad
    ggain[...] = jnp.broadcast_to(gsum, ggain.shape)
    block[...] = grad.astype(BF)
    gather = CubeGather(me_g, me, block, out, *sems[NS:])
    gather.start()
    for step in range(3):
        gather.advance(step)
    gather.finish()
    scatter.finish()


def turn_call(kernel, outs, rows, width, members, cid, name, args):
    shape = jax.ShapeDtypeStruct
    return pl.pallas_call(
        kernel,
        in_specs=[ANY] + [VM] * (len(args) - 1),
        out_specs=[VM] * len(outs) + [ANY],
        out_shape=outs + [shape((members, rows, width), BF)],
        scratch_shapes=[pltpu.VMEM((rows, width), F32), pltpu.VMEM((rows, width), BF)]
        + scatter_scratch(rows, width) + GATHER_SEMS,
        compiler_params=pltpu.CompilerParams(collective_id=cid, has_side_effects=True, vmem_limit_bytes=VMEM_LIMIT),
        name=name,
    )(*args)


def forward_turn(part, flat, gain):
    members, rows, width = part.shape
    outs = [jax.ShapeDtypeStruct((rows, width), F32)]
    return turn_call(forward_turn_kernel, outs, rows, width, members, 1, "turn_fwd", (part, flat, gain))


def backward_turn(part, resid, gain, cot):
    members, rows, width = part.shape
    outs = [jax.ShapeDtypeStruct((rows, width), F32), jax.ShapeDtypeStruct((8, width), F32)]
    return turn_call(backward_turn_kernel, outs, rows, width, members, 2, "turn_bwd", (part, resid, gain, cot))


class Spread:
    def __init__(self, groups, members, me_g, me):
        self.groups, self.members = groups, members
        self.count = groups * members
        self.me_d = me_g * members + me

    def peer(self, k):
        d = lax.rem(self.me_d + k, self.count)
        return d, d // self.members, lax.rem(d, self.members)

    def back(self, k):
        return lax.rem(self.me_d + self.count - k, self.count)

    def greet(self):
        barrier = pltpu.get_barrier_semaphore()

        @pl.loop(1, self.count)
        def _(k):
            _, g, m = self.peer(k)
            pl.semaphore_signal(barrier, inc=1, device_id=(g, m), device_id_type=MESH)

        pl.semaphore_wait(barrier, self.count - 1)


def start_kernel(
    groups, members, rho, tok, att, ff, wo, pack,
    tok_all, w_att, ff_half, w_out, packs, sa, ra, sp, rp, sf, rf, so, ro, loc, *sems,
):
    me_g, me = lax.axis_index("g"), lax.axis_index("m")
    spread = Spread(groups, members, me_g, me)
    me_d = spread.me_d
    spread.greet()
    gather = CubeGather(me_g, me, tok, tok_all, *sems)
    gather.start()

    def att_copy(k, g, m):
        return remote(att.at[m], w_att.at[me_d], sa.at[k], ra.at[k], g, m)

    def pack_copy(k, g, m):
        return remote(pack, packs.at[me_d], sp.at[k], rp.at[k], g, m)

    def ff_copy(k, m):
        return remote(ff.at[m], ff_half.at[me], sf.at[k], rf.at[k], me_g, m)

    target = (me // rho) * rho + me_g
    place = lax.rem(me, rho)
    sources = [(lax.rem(me, rho), (me // rho) * rho + i) for i in range(rho)]

    def out_copy(k, g):
        return remote(wo, w_out.at[place], so.at[k], ro.at[place], g, target)

    @pl.loop(1, spread.count)
    def _(k):
        _, g, m = spread.peer(k)
        pack_copy(k, g, m).start()
        att_copy(k, g, m).start()

    copies = [
        pltpu.make_async_copy(att.at[me], w_att.at[me_d], loc.at[0]),
        pltpu.make_async_copy(pack, packs.at[me_d], loc.at[1]),
        pltpu.make_async_copy(ff.at[me], ff_half.at[me], loc.at[2]),
    ]
    for copy in copies:
        copy.start()
    for g in range(groups):
        @pl.when((me_g != g) | (me != target))
        def _():
            out_copy(g, g).start()

    @pl.when(me == target)
    def _():
        pltpu.make_async_copy(wo, w_out.at[place], loc.at[3]).start()

    gather.advance(0)

    @pl.loop(1, members)
    def _(k):
        ff_copy(k, lax.rem(me + k, members)).start()

    gather.advance(1)
    gather.advance(2)
    gather.finish()

    @pl.loop(1, spread.count)
    def _(k):
        _, g, m = spread.peer(k)
        pack_copy(k, g, m).wait()
        att_copy(k, g, m).wait()

    @pl.loop(1, members)
    def _(k):
        ff_copy(k, lax.rem(me + k, members)).wait()

    for copy in copies:
        copy.wait()
    for g in range(groups):
        @pl.when((me_g != g) | (me != target))
        def _():
            out_copy(g, g).wait_send()
    for i in range(rho):
        src_g, src_m = sources[i]
        @pl.when((me_g != src_g) | (me != src_m))
        def _():
            remote(wo, w_out.at[i], so.at[0], ro.at[i], me_g, me).wait_recv()

    @pl.when(me == target)
    def _():
        pltpu.make_async_copy(wo, w_out.at[place], loc.at[3]).wait()


def start_call(groups, members, rho, tok, att, ff, wo, pack):
    shape = jax.ShapeDtypeStruct
    n = groups * members
    dma = pltpu.SemaphoreType.DMA
    return pl.pallas_call(
        functools.partial(start_kernel, groups, members, rho),
        in_specs=[ANY] * 5,
        out_specs=[ANY] * 5,
        out_shape=[
            shape((members,) + tok.shape, BF), shape((n,) + att.shape[1:], BF), shape((members,) + ff.shape[1:], BF),
            shape((rho,) + wo.shape, BF), shape((n,) + pack.shape, BF),
        ],
        scratch_shapes=[
            dma((n,)), dma((n,)), dma((n,)), dma((n,)), dma((members,)), dma((members,)), dma((groups,)), dma((rho,)),
            dma((4,)),
        ] + GATHER_SEMS,
        compiler_params=pltpu.CompilerParams(collective_id=3, has_side_effects=True, vmem_limit_bytes=VMEM_LIMIT),
        name="start",
    )(tok, att, ff, wo, pack)


def end_kernel(
    groups, members, rho, part, flat, grad_resid, gain, gatt, gff, gout, small, tapg,
    input_grad, att_in, ff_in, out_in, small_in, tap_in, gain_in,
    total, vec, sa, ra, ss, rs, sf, rf, so, ro, st, rt, sg, rg, loc, *sems,
):
    me_g, me = lax.axis_index("g"), lax.axis_index("m")
    spread = Spread(groups, members, me_g, me)
    me_d = spread.me_d
    spread.greet()
    scatter = CubeScatter(me_g, me, part, *sems)
    scatter.start()

    def att_copy(k, d, g, m):
        return remote(gatt.at[d], att_in.at[me_d], sa.at[k], ra.at[k], g, m)

    def small_copy(k, d, g, m):
        return remote(small.at[d], small_in.at[me_d], ss.at[k], rs.at[k], g, m)

    def ff_copy(k, m):
        return remote(gff.at[m], ff_in.at[me], sf.at[k], rf.at[k], me_g, m)

    def gain_copy(k, g, m):
        return remote(vec, gain_in.at[me_d], sg.at[k], rg.at[k], g, m)

    home = lax.rem(me, rho)
    base = (me // rho) * rho

    def out_copy(i):
        return remote(gout.at[i], out_in.at[me_g], so.at[i], ro.at[me_g], home, base + i)

    def tap_copy(i):
        return remote(tapg.at[i], tap_in.at[me_g], st.at[i], rt.at[me_g], home, base + i)

    @pl.loop(1, spread.count)
    def _(k):
        d, g, m = spread.peer(k)
        att_copy(k, d, g, m).start()
        small_copy(k, d, g, m).start()

    copies = [
        pltpu.make_async_copy(gatt.at[me_d], att_in.at[me_d], loc.at[0]),
        pltpu.make_async_copy(small.at[me_d], small_in.at[me_d], loc.at[1]),
        pltpu.make_async_copy(gff.at[me], ff_in.at[me], loc.at[2]),
    ]
    for copy in copies:
        copy.start()
    for i in range(rho):
        @pl.when((me_g != home) | (me != base + i))
        def _():
            out_copy(i).start()
            tap_copy(i).start()

        @pl.when((me_g == home) & (me == base + i))
        def _():
            pltpu.make_async_copy(gout.at[i], out_in.at[me_g], loc.at[3]).start()
            pltpu.make_async_copy(tapg.at[i], tap_in.at[me_g], loc.at[4]).start()

    @pl.loop(1, members)
    def _(k):
        ff_copy(k, lax.rem(me + k, members)).start()

    scatter.run(total)
    back, gsum = norm_backward(total[...], flat[...].astype(F32), gain[...])
    input_grad[...] = grad_resid[...] + back
    for i in range(vec.shape[0]):
        vec[i : i + 1, :] = gsum[:, i * DK : (i + 1) * DK]

    @pl.loop(1, spread.count)
    def _(k):
        _, g, m = spread.peer(k)
        gain_copy(k, g, m).start()

    own = pltpu.make_async_copy(vec, gain_in.at[me_d], loc.at[5])
    own.start()
    scatter.finish()

    @pl.loop(1, spread.count)
    def _(k):
        d, g, m = spread.peer(k)
        att_copy(k, d, g, m).wait()
        small_copy(k, d, g, m).wait()
        gain_copy(k, g, m).wait()

    @pl.loop(1, members)
    def _(k):
        ff_copy(k, lax.rem(me + k, members)).wait()

    for copy in copies:
        copy.wait()
    own.wait()
    for i in range(rho):
        @pl.when((me_g != home) | (me != base + i))
        def _():
            out_copy(i).wait_send()
            tap_copy(i).wait_send()

        @pl.when((me_g == home) & (me == base + i))
        def _():
            pltpu.make_async_copy(gout.at[i], out_in.at[me_g], loc.at[3]).wait()
            pltpu.make_async_copy(tapg.at[i], tap_in.at[me_g], loc.at[4]).wait()
    holder = base + me_g
    for g in range(groups):
        @pl.when((me_g != g) | (me != holder))
        def _():
            remote(gout.at[0], out_in.at[g], so.at[0], ro.at[g], me_g, me).wait_recv()
            remote(tapg.at[0], tap_in.at[g], st.at[0], rt.at[g], me_g, me).wait_recv()


def end_call(groups, members, rho, part, flat, grad_resid, gain, gatt, gff, gout, small, tapg):
    shape = jax.ShapeDtypeStruct
    n = groups * members
    _, rows, width = part.shape
    dma = pltpu.SemaphoreType.DMA
    return pl.pallas_call(
        functools.partial(end_kernel, groups, members, rho),
        in_specs=[ANY, VM, VM, VM] + [ANY] * 5,
        out_specs=[VM] + [ANY] * 6,
        out_shape=[
            shape((rows, width), F32), shape(gatt.shape, BF), shape(gff.shape, BF), shape((groups,) + gout.shape[1:], BF),
            shape(small.shape, F32), shape((groups,) + tapg.shape[1:], F32), shape((n, width // DK, DK), F32),
        ],
        scratch_shapes=[
            pltpu.VMEM((rows, width), F32), pltpu.VMEM((width // DK, DK), F32), dma((n,)), dma((n,)), dma((n,)), dma((n,)),
            dma((members,)), dma((members,)), dma((rho,)), dma((groups,)), dma((rho,)), dma((groups,)), dma((n,)), dma((n,)),
            dma((6,)),
        ] + scatter_scratch(rows, width),
        compiler_params=pltpu.CompilerParams(collective_id=4, has_side_effects=True, vmem_limit_bytes=VMEM_LIMIT),
        name="end",
    )(part, flat, grad_resid, gain, gatt, gff, gout, small, tapg)


def exchange_groups(x, groups):
    me = lax.axis_index("g")
    total = lax.dynamic_index_in_dim(x, me, 0, keepdims=False)
    for step in range(1, groups):
        perm = [(i, (i + step) % groups) for i in range(groups)]
        piece = lax.dynamic_index_in_dim(x, lax.rem(me + step, groups), 0, keepdims=False).astype(BF)
        total = total + lax.ppermute(piece, "g", perm).astype(F32)
    return total


def make_shards(groups, members):
    def shards(
        tokens, doc_starts, seq_lengths, attn_gain, query_weight, key_weight, value_weight, out_gate_weight, beta_weight,
        query_conv, key_conv, value_conv, head_gain, out_weight, mlp_gain, mlp_gate_weight, mlp_up_weight,
        mlp_down_weight, cotangent,
    ):
        n = groups * members
        width = tokens.shape[-1]
        r = attn_gain.shape[0]
        f = mlp_down_weight.shape[0]
        hgr = head_gain.shape[0]
        heads = beta_weight.shape[1]
        rho = DK // r
        srange = members // rho
        me_g, me_m = lax.axis_index("g"), lax.axis_index("m")
        head = lax.rem(me_m, rho) * srange + me_m // rho
        seqs = tokens.shape[0] * tokens.shape[1]
        seq = tokens.shape[2]
        own = seqs * seq
        flat_bf = tokens.reshape(own, width)
        grad_out = cotangent.reshape(own, width)

        position = lax.broadcasted_iota(jnp.int32, (seqs, seq), 1)
        starts = doc_starts.reshape(seqs, seq)
        doc_ids = jnp.cumsum(jnp.where(position == 0, 1, starts), axis=-1) - 1
        live = position < seq_lengths.reshape(seqs, 1)

        pieces = [attn_gain, mlp_gain, head_gain, beta_weight.reshape(-1), query_conv.reshape(-1), key_conv.reshape(-1),
                  value_conv.reshape(-1), doc_ids.astype(BF).reshape(-1), live.astype(BF).reshape(-1)]
        sizes = [p.shape[0] for p in pieces]
        pack = jnp.concatenate(pieces)
        total = -(-pack.shape[0] // 2048) * 2048
        pack = jnp.pad(pack, (0, total - pack.shape[0])).reshape(-1, DK)

        def by_member(w):
            return w.reshape(r, groups, srange, DK).transpose(2, 1, 0, 3).reshape(members, r, DK)

        ffw = groups * f
        ffp = -(-ffw // DK) * DK

        def ff_by_member(w):
            w = w.reshape(r, groups, members, f).transpose(2, 0, 1, 3).reshape(members, r, ffw)
            return jnp.pad(w, ((0, 0), (0, 0), (0, ffp - ffw)))

        att_cols = jnp.concatenate(
            [by_member(w) for w in (query_weight, key_weight, value_weight, out_gate_weight)], axis=-1
        )
        ff_cols = jnp.concatenate([ff_by_member(mlp_gate_weight), ff_by_member(mlp_up_weight)], axis=-1)
        tok_all, w_att, ff_half, w_out, packs = start_call(
            groups, members, rho, flat_bf, att_cols, ff_cols, out_weight, pack
        )
        count = members * own
        w_att = w_att.reshape(width, 4 * DK)
        w_out = w_out.reshape(DK, width)
        packs = packs.reshape(n, total)
        w_ff = lax.all_gather(ff_half, "g", axis=0).reshape(width, 2 * ffp)
        w_down = lax.all_gather(mlp_down_weight, "g", axis=0).reshape(ffw, width)
        w_down = jnp.pad(w_down, ((0, ffp - ffw), (0, 0)))
        cot_all = lax.all_gather(grad_out, "m", axis=0, tiled=True)

        parts, at = [], 0
        for s in sizes:
            parts.append(packs[:, at : at + s])
            at += s
        gain_in = parts[0].reshape(1, width).astype(F32)
        gain_mid = parts[1].reshape(1, width).astype(F32)
        hg = parts[2].reshape(1, DK).astype(F32)
        beta_full = jnp.pad(parts[3].reshape(width, heads), ((0, 0), (0, DK - heads)))
        taps = [
            lax.dynamic_slice_in_dim(p.reshape(width, TAPS), head * DK, DK, 0).astype(F32).T for p in parts[4:7]
        ]
        taps = jnp.concatenate(taps + [jnp.zeros((4, DK), F32)], axis=0)
        group_docs = lax.dynamic_slice_in_dim(parts[7], me_g * members, members, 0).astype(F32)
        group_live = lax.dynamic_slice_in_dim(parts[8], me_g * members, members, 0).astype(F32)
        seq_of = jnp.arange(count, dtype=jnp.int32) // seq
        docs = group_docs.reshape(count) + seq_of.astype(F32) * seq
        columns = [docs] + [
            jnp.where(jnp.pad(docs, (o, 0), constant_values=-1.0)[:count] == docs, 1.0, 0.0) for o in range(1, TAPS)
        ] + [group_live.reshape(count)]
        meta = jnp.pad(jnp.stack(columns, axis=1), ((0, 0), (0, DK - len(columns))))
        docs_row = docs.reshape(count // CHUNK, 1, CHUNK)
        hot = (jnp.arange(DK) == head).astype(F32).reshape(1, DK)

        blocks = (members, own, width)
        nx, proj, bl, t, u, o, mixed, part = att_forward(
            tok_all.reshape(count, width), gain_in, w_att, beta_full, taps, hg, hot, w_out, meta, docs_row
        )
        resid, nm = forward_turn(part.reshape(blocks), flat_bf, gain_mid)
        nm = nm.reshape(count, width)
        act = mm(nm, w_ff, 1, 0)
        gate_act, up_act = act[:, :ffp], act[:, ffp:]
        sg = jax.nn.sigmoid(gate_act)
        hidden = (gate_act * sg * up_act).astype(BF)
        grad_hidden = mm(cot_all, w_down, 1, 1)
        gg = (grad_hidden * up_act * (sg * (1.0 + gate_act * (1.0 - sg)))).astype(BF)
        gu = (grad_hidden * (gate_act * sg)).astype(BF)
        gff = jnp.concatenate([gg, gu], axis=1)
        gmid_part = mm(gff, w_ff, 1, 1).astype(BF)
        out_part = mm(hidden, w_down, 1, 0).astype(BF)
        mlp_out = lax.psum_scatter(out_part, "m", scatter_dimension=0, tiled=True).astype(F32)
        g_down = exchange_groups(mm(hidden, cot_all, 0, 0)[:ffw].reshape(groups, f, width), groups)
        g_ff = exchange_groups(mm(nm, gff, 0, 0).reshape(groups, members * r, 2 * ffp), groups)
        g_ff = g_ff.astype(BF).reshape(members, r, 2 * ffp)
        grad_resid, g_mid_gain, ga = backward_turn(gmid_part.reshape(blocks), resid, gain_mid, grad_out)
        ga = ga.reshape(count, width)
        gproj, gb, gpart, gtaps, ghg = att_backward(
            ga, w_out, proj, bl, t, u, o, meta, docs_row, taps, hg, hot, w_att, beta_full
        )
        layer_out = (resid + mlp_out).astype(BF)
        gatt = mm(nx, gproj, 0, 0).astype(BF).reshape(n, r, 4 * DK)
        gout = mm(mixed, ga, 0, 0).astype(BF).reshape(rho, r, width)
        g_beta = jnp.sum(mm(gb, nx, 0, 0), axis=0)
        small = jnp.stack(
            [
                jnp.pad(g_mid_gain[0].reshape(n, r), ((0, 0), (0, DK - r))),
                jnp.pad(g_beta.reshape(n, r), ((0, 0), (0, DK - r))),
                jnp.pad(ghg[0].reshape(n, hgr), ((0, 0), (0, DK - hgr))),
            ],
            axis=1,
        )
        small = jnp.pad(small, ((0, 0), (0, 5), (0, 0)))
        tapg = jnp.stack([gtaps[: 3 * TAPS, i * r : (i + 1) * r] for i in range(rho)])
        tapg = jnp.pad(tapg, ((0, 0), (0, 16 - 3 * TAPS), (0, DK - r)))
        input_grad, att_in, ff_in, out_in, small_in, tap_in, gain_grad = end_call(
            groups, members, rho, gpart.reshape(blocks), flat_bf, grad_resid, gain_in, gatt, g_ff, gout, small, tapg
        )
        g_att = jnp.sum(att_in.astype(F32).reshape(groups, members, r, 4 * DK), axis=0)
        g_att = g_att.reshape(srange, groups, r, 4, DK).transpose(3, 2, 1, 0, 4).reshape(4, r, width)
        g_ff = ff_in.reshape(members, r, 2, ffp)[..., :ffw].reshape(members, r, 2, groups, f)
        g_ff = g_ff.transpose(2, 1, 3, 0, 4).reshape(2, r, -1).astype(F32)
        g_out = jnp.sum(out_in.astype(F32), axis=0)
        small = jnp.sum(small_in, axis=0)
        me_d = me_g * members + me_m
        s_in = lax.dynamic_slice_in_dim(jnp.sum(gain_grad, axis=0).reshape(width), me_d * r, r, 0)
        s_mid, s_hg = small[0, :r], small[2, :hgr]
        s_beta = small_in[:, 1, :r].reshape(groups, members, r).sum(axis=0)
        s_beta = s_beta.reshape(srange, rho, r).transpose(2, 1, 0).reshape(r, heads)
        gt = jnp.sum(tap_in, axis=0)[: 3 * TAPS, :r]
        s_q, s_k, s_v = (gt[i * TAPS : (i + 1) * TAPS].T for i in range(3))
        return (
            layer_out.reshape(tokens.shape), input_grad.reshape(tokens.shape),
            s_in, g_att[0], g_att[1], g_att[2], g_att[3], s_beta, s_q, s_k, s_v, s_hg, g_out, s_mid, g_ff[0], g_ff[1],
            g_down,
        )

    return shards


def solution(mesh):
    n = mesh.devices.size
    members = 16
    groups = n // members
    inner = Mesh(mesh.devices.reshape(groups, members), ("g", "m"))
    both = ("g", "m")
    acts, mat, vec = P(None, both, None, None), P(both, None), P(both)
    return jax.shard_map(
        make_shards(groups, members),
        mesh=inner,
        in_specs=(acts, P(None, both, None), P(None, both), vec, mat, mat, mat, mat, mat, mat, mat, mat, vec, mat, vec,
                  mat, mat, mat, acts),
        out_specs=(acts, acts, vec, mat, mat, mat, mat, mat, mat, mat, mat, vec, mat, vec, mat, mat, mat),
        check_vma=False,
    )
```

```python
import functools

import jax
import jax.numpy as jnp
from jax import lax
from jax.experimental import pallas as pl
from jax.experimental.pallas import tpu as pltpu
from jax.sharding import Mesh
from jax.sharding import PartitionSpec as P

DK = 128
EPS = 1e-05
L2EPS = 1e-06
CHUNK = 256
SEQ = 64
SUB = 128
TAPS = 4
BF = jnp.bfloat16
F32 = jnp.float32
VMEM_LIMIT = 60 << 20


def mm(a, b, ca, cb):
    return lax.dot_general(a, b, (((ca,), (cb,)), ((), ())), preferred_element_type=F32)


def split(x):
    hi = x.astype(BF)
    return hi, (x - hi.astype(F32)).astype(BF)


def mm3(a, b, ca, cb):
    (ah, al), (bh, bl) = a, b
    out = mm(ah, bh, ca, cb)
    if bl is not None:
        out = out + mm(ah, bl, ca, cb)
    if al is not None:
        out = out + mm(al, bh, ca, cb)
    return out


def sigmoid(x):
    return 1.0 / (1.0 + jnp.exp(-x))


def iotas():
    row = lax.broadcasted_iota(jnp.int32, (SUB, SUB), 0)
    col = lax.broadcasted_iota(jnp.int32, (SUB, SUB), 1)
    return row, col


def unit_lower_inverses(blocks, row, col):
    eye = (row == col).astype(F32)
    pair = (row // 2) == (col // 2)
    xs = [eye - jnp.where(pair, a, 0.0) for a in blocks]
    size = 2
    while size < SEQ:
        keep = ((row // (2 * size)) == (col // (2 * size))) & ((row // size) != (col // size))
        offs = [split(jnp.where(keep, a, 0.0)) for a in blocks]
        parts = [split(x) for x in xs]
        ys = [split(mm3(off, p, 1, 0)) for off, p in zip(offs, parts)]
        xs = [x - mm3(p, y, 1, 0) for x, p, y in zip(xs, parts, ys)]
        size *= 2
    return xs


def conv_forward(x, taps, base, masks):
    out = x * taps[base + TAPS - 1 : base + TAPS]
    for o in range(1, TAPS):
        out = out + pltpu.roll(x, o, 0) * masks[o - 1] * taps[base + TAPS - 1 - o : base + TAPS - o]
    return out


def unit(act):
    r = lax.rsqrt(jnp.sum(act * act, axis=-1, keepdims=True) + L2EPS)
    return act * r, r


def subs(x):
    return [x[i * SUB : (i + 1) * SUB] for i in range(CHUNK // SUB)]


def att_fwd_kernel(
    groups, members,
    tok_ref, gain_ref, w_ref, wb_ref, taps_ref, hg_ref, hot_ref, wo_ref, meta_ref, doc_ref, cot_ref, wd_ref,
    nx_ref, proj_ref, bl_ref, t_ref, u_ref, o_ref, mixed_ref, part_ref, cot_all, down_all, *sems,
):
    step = pl.program_id(0)
    me_g, me = lax.axis_index("g"), lax.axis_index("m")
    sd, rd, loc = sems[NG:]

    def down_copy(k):
        return remote(wd_ref, down_all.at[me_g], sd.at[k], rd.at[k], lax.rem(me_g + k, groups), me)

    def down_arrival(k):
        src = lax.rem(me_g + groups - k, groups)
        return remote(wd_ref, down_all.at[src], sd.at[k], rd.at[k], me_g, me)

    def down_own():
        return pltpu.make_async_copy(wd_ref, down_all.at[me_g], loc)

    def gather():
        return CubeGather(LIGHT, me_g, me, cot_ref, cot_all, *sems[:NG])

    @pl.when(step == 0)
    def _():
        greet_cube(me_g, me, groups)
        gather().start()
        down_own().start()
        for k in range(1, groups):
            down_copy(k).start()

    for at, hop in ((2, 0), (4, 1), (6, 2)):
        @pl.when(step == at)
        def _():
            gather().advance(hop)

    x = tok_ref[...].astype(F32)
    nx = (x * lax.rsqrt(jnp.mean(x * x, axis=-1, keepdims=True) + EPS) * gain_ref[...]).astype(BF)
    nx_ref[...] = nx
    proj = mm(nx, w_ref[...], 1, 0)
    proj_ref[...] = proj
    logits = mm(nx, wb_ref[...], 1, 0)
    logit = jnp.sum(logits * hot_ref[...], axis=-1, keepdims=True)
    bl_ref[...] = jnp.broadcast_to(logit, (CHUNK, DK))
    meta = meta_ref[...]
    doc = meta[:, 0:1]
    masks = [meta[:, o : o + 1] for o in range(1, TAPS)]
    beta = sigmoid(logit) * meta[:, 4:5]
    taps = taps_ref[...]
    acts = []
    for i in range(3):
        c = conv_forward(proj[:, i * DK : (i + 1) * DK], taps, i * TAPS, masks)
        acts.append(c * sigmoid(c))
    qs = subs(unit(acts[0])[0].astype(BF))
    ks = subs(unit(acts[1])[0].astype(BF))
    vs = subs(acts[2].astype(BF))
    betas, docs = subs(beta), subs(doc)
    row, col = iotas()
    sames = [d == doc_ref[i] for i, d in enumerate(docs)]
    blocks = [jnp.where(same & (row > col), bt * mm(k, k, 1, 1), 0.0) for same, bt, k in zip(sames, betas, ks)]
    ts = unit_lower_inverses(blocks, row, col)
    os = []
    for i, (t, bt, v, q, k, same) in enumerate(zip(ts, betas, vs, qs, ks, sames)):
        at = pl.ds(i * SUB, SUB)
        t_ref[at, :] = t
        u = mm3(split(t), split(bt * v.astype(F32)), 1, 0)
        u_ref[at, :] = u
        p = jnp.where(same & (row >= col), mm(q, k, 1, 1), 0.0)
        os.append(mm3(split(p), split(u), 1, 0))
    o = jnp.concatenate(os, axis=0)
    o_ref[...] = o
    gate = proj[:, 3 * DK :]
    n_o = o * lax.rsqrt(jnp.mean(o * o, axis=-1, keepdims=True) + EPS)
    mixed = (n_o * hg_ref[...] * (gate * sigmoid(gate))).astype(BF)
    mixed_ref[...] = mixed
    part_ref[...] = mm(mixed, wo_ref[...], 1, 0).astype(BF)

    @pl.when(step == pl.num_programs(0) - 1)
    def _():
        gather().finish()
        down_own().wait()
        for k in range(1, groups):
            down_copy(k).wait_send()
            down_arrival(k).wait_recv()


def att_bwd_kernel(
    own_ref, wo_ref, nx_ref, mixed_ref, proj_ref, bl_ref, t_ref, u_ref, o_ref, meta_ref, doc_ref, taps_ref, hg_ref, hot_ref,
    w_ref, wb_ref, outp_ref, resid_ref,
    part_ref, gtaps_ref, ghg_ref, gatt_ref, gout_ref, gbeta_ref, layer_ref,
    gatt_acc, gout_acc, gbeta_acc, ga_all, *sems,
):
    step = pl.program_id(0)
    me_g, me = lax.axis_index("g"), lax.axis_index("m")

    def scatter():
        return CubeScatter(TURNED, me_g, me, outp_ref, *sems[:NS])

    gather = CubeGather(LIGHT, me_g, me, own_ref, ga_all, *sems[NS:])

    @pl.when(step == 0)
    def _():
        greet_cube(me_g, me)
        gather.start()
        gtaps_ref[...] = jnp.zeros_like(gtaps_ref)
        ghg_ref[...] = jnp.zeros_like(ghg_ref)
        gatt_acc[...] = jnp.zeros_like(gatt_acc)
        gout_acc[...] = jnp.zeros_like(gout_acc)
        gbeta_acc[...] = jnp.zeros_like(gbeta_acc)

    gather.host(step)

    @pl.when(step == 3)
    def _():
        scatter().start()

    for at, phase in ((5, 0), (6, 1), (7, 2)):
        @pl.when(step == at)
        def _():
            scatter().phase(phase)

    proj = proj_ref[...]
    meta = meta_ref[...]
    doc = meta[:, 0:1]
    masks = [meta[:, o : o + 1] for o in range(1, TAPS)]
    logit = bl_ref[:, 0:1]
    sig = sigmoid(logit)
    live = meta[:, 4:5]
    beta = sig * live
    taps = taps_ref[...]
    convs, sigs, acts = [], [], []
    for i in range(3):
        c = conv_forward(proj[:, i * DK : (i + 1) * DK], taps, i * TAPS, masks)
        s = sigmoid(c)
        convs.append(c)
        sigs.append(s)
        acts.append(c * s)
    uq, rq = unit(acts[0])
    uk, rk = unit(acts[1])
    q, k, v = uq.astype(BF), uk.astype(BF), acts[2].astype(BF)

    ga = chip_rows(ga_all, chip_at(step, me))
    gm = mm(ga, wo_ref[...], 1, 1)
    gout_acc[...] += mm(mixed_ref[...], ga, 0, 0)
    o = o_ref[...]
    gate = proj[:, 3 * DK :]
    sg = sigmoid(gate)
    z = gate * sg
    r_o = lax.rsqrt(jnp.mean(o * o, axis=-1, keepdims=True) + EPS)
    n_o = o * r_o
    gmh = gm * hg_ref[...]
    e = gmh * z
    go = r_o * (e - n_o * jnp.mean(e * n_o, axis=-1, keepdims=True))
    ggate = gmh * n_o * (sg * (1.0 + gate * (1.0 - sg)))
    ghg_ref[0:1] += jnp.sum(gm * n_o * z, axis=0, keepdims=True)

    row, col = iotas()
    gqs, gks, gvs, gbs = [], [], [], []
    for i, (dc, q_, k_, v_, bt, go_) in enumerate(zip(subs(doc), subs(q), subs(k), subs(v), subs(beta), subs(go))):
        at = pl.ds(i * SUB, SUB)
        same = dc == doc_ref[i]
        strict = same & (row > col)
        causal = same & (row >= col)
        kk = mm(k_, k_, 1, 1)
        p = jnp.where(causal, mm(q_, k_, 1, 1), 0.0)
        us = split(u_ref[at, :])
        gos = split(go_)
        dp = split(jnp.where(causal, mm3(gos, us, 1, 1), 0.0))
        du = mm3(split(p), gos, 0, 0)
        dw = mm3(split(t_ref[at, :]), split(du), 0, 0)
        da = jnp.where(strict, -mm3(split(dw), us, 1, 1), 0.0)
        dkk = split(bt * da)
        gqs.append(mm3(dp, (k_, None), 1, 0))
        gks.append(mm3(dp, (q_, None), 0, 0) + mm3(dkk, (k_, None), 1, 0) + mm3(dkk, (k_, None), 0, 0))
        gvs.append(bt * dw)
        gbs.append(
            jnp.sum(dw * v_.astype(F32), axis=-1, keepdims=True) + jnp.sum(da * kk, axis=-1, keepdims=True)
        )
    gq, gk, gv, gbeta = (jnp.concatenate(parts, axis=0) for parts in (gqs, gks, gvs, gbs))
    gbl = gbeta * live * sig * (1.0 - sig)
    gb = (gbl * hot_ref[...]).astype(BF)

    gacts = [
        (gq - uq * jnp.sum(uq * gq, axis=-1, keepdims=True)) * rq,
        (gk - uk * jnp.sum(uk * gk, axis=-1, keepdims=True)) * rk,
        gv,
    ]
    grads = []
    for i in range(3):
        x = proj[:, i * DK : (i + 1) * DK]
        gc = gacts[i] * (sigs[i] * (1.0 + convs[i] * (1.0 - sigs[i])))
        base = i * TAPS
        gx = gc * taps[base + TAPS - 1 : base + TAPS]
        j = base + TAPS - 1
        gtaps_ref[j : j + 1] += jnp.sum(gc * x, axis=0, keepdims=True)
        for off in range(1, TAPS):
            gco = gc * masks[off - 1]
            j = base + TAPS - 1 - off
            gtaps_ref[j : j + 1] += jnp.sum(gco * pltpu.roll(x, off, 0), axis=0, keepdims=True)
            gx = gx + pltpu.roll(gco, CHUNK - off, 0) * taps[j : j + 1]
        grads.append(gx.astype(BF))
    gproj = jnp.concatenate(grads + [ggate.astype(BF)], axis=1)
    part = mm(gproj, w_ref[...], 1, 1) + mm(gb, wb_ref[...], 1, 1)
    part_ref[...] = part.astype(BF)
    nx = nx_ref[...]
    gatt_acc[...] += mm(nx, gproj, 0, 0)
    gbeta_acc[...] += mm(gb, nx, 0, 0)

    @pl.when(step == pl.num_programs(0) - 1)
    def _():
        gatt_ref[...] = gatt_acc[...].astype(BF)
        gout_ref[...] = gout_acc[...].astype(BF)
        gbeta_ref[...] = jnp.broadcast_to(jnp.sum(gbeta_acc[...], axis=0, keepdims=True), gbeta_ref.shape)
        done = scatter()
        done.phase(3, lambda j, at, size, got: layer_out_store(layer_ref, resid_ref, at, size, got))
        done.finish()
        gather.sent()


def chip_rows(ref, chip):
    return jnp.concatenate([ref[2 * chip], ref[2 * chip + 1]], axis=0)


def layer_out_store(layer_ref, resid_ref, at, size, got):
    layer_ref[:, at : at + size] = (resid_ref[:, at : at + size] + got).astype(BF)


def mlp_kernel(
    groups, f, ffp, own_ref, cot_ref, w_ref, wd_ref,
    out_ref, gmid_ref, gw_ref, gd_ref, gw_away, gd_away, gw_acc, gd_acc, nm_all, *sems,
):
    step = pl.program_id(0)
    me_g, me = lax.axis_index("g"), lax.axis_index("m")
    gather = CubeGather(TURNED, me_g, me, own_ref, nm_all, *sems)

    @pl.when(step == 0)
    def _():
        greet_cube(me_g, me)
        gather.start()
        gw_acc[...] = jnp.zeros_like(gw_acc)
        gd_acc[...] = jnp.zeros_like(gd_acc)

    gather.host(step)
    nm = chip_rows(nm_all, chip_at(step, me))
    cot, w, wd = cot_ref[...], w_ref[...], wd_ref[...]
    act = mm(nm, w, 1, 0)
    gate, up = act[:, :ffp], act[:, ffp:]
    s = sigmoid(gate)
    z = gate * s
    hidden = (z * up).astype(BF)
    out_ref[...] = mm(hidden, wd, 1, 0).astype(BF)
    gh = mm(cot, wd, 1, 1)
    gg = (gh * up * (s * (1.0 + gate * (1.0 - s)))).astype(BF)
    gu = (gh * z).astype(BF)
    g = jnp.concatenate([gg, gu], axis=1)
    gmid_ref[...] = mm(g, w, 1, 1).astype(BF)
    gw_acc[...] += mm(nm, g, 0, 0)
    gd_acc[...] += mm(hidden, cot, 0, 0)

    @pl.when(step == pl.num_programs(0) - 1)
    def _():
        size = gw_ref.shape[0]
        gw_ref[...] = gw_acc[pl.ds(pl.multiple_of(me_g * size, 8), size), :]
        for k in range(1, groups):
            g = lax.rem(me_g + k, groups)
            gw_away[k - 1] = gw_acc[pl.ds(pl.multiple_of(g * size, 8), size), :].astype(BF)
        for g in range(groups):
            @pl.when(me_g == g)
            def _():
                gd_ref[...] = gd_acc[g * f : (g + 1) * f]
                for k in range(1, groups):
                    away = (g + k) % groups
                    gd_away[k - 1] = gd_acc[away * f : (away + 1) * f].astype(BF)
        gather.sent()


def rows(width):
    return pl.BlockSpec((CHUNK, width), lambda i: (i, 0))


def whole(shape):
    return pl.BlockSpec(shape, lambda i: (0,) * len(shape))


DOCROW = pl.BlockSpec((CHUNK // SUB, 1, SUB), lambda i: (i, 0, 0))


def chip_block(width):
    return pl.BlockSpec((CHUNK, width), lambda i: (chip_at(i, lax.axis_index("m")), 0))


def chip_docrow():
    return pl.BlockSpec((CHUNK // SUB, 1, SUB), lambda i: (chip_at(i, lax.axis_index("m")), 0, 0))


def att_forward(groups, members, tok, gain, w, wb, taps, hg, hot, wo, meta, docs, cot, wd):
    count, width = tok.shape
    shape = jax.ShapeDtypeStruct
    dma = pltpu.SemaphoreType.DMA
    return pl.pallas_call(
        functools.partial(att_fwd_kernel, groups, members),
        grid=(count // CHUNK,),
        in_specs=[
            rows(width), whole((1, width)), whole(w.shape), whole(wb.shape), whole(taps.shape), whole((1, DK)),
            whole((1, DK)), whole(wo.shape), rows(DK), DOCROW, ANY, ANY,
        ],
        out_specs=[rows(width), rows(4 * DK), rows(DK), rows(SUB), rows(DK), rows(DK), rows(DK), rows(width), ANY, ANY],
        out_shape=[
            shape((count, width), BF), shape((count, 4 * DK), F32), shape((count, DK), F32), shape((count, SUB), F32),
            shape((count, DK), F32), shape((count, DK), F32), shape((count, DK), BF), shape((count, width), BF),
            shape((members,) + cot.shape, BF), shape((groups,) + wd.shape, BF),
        ],
        scratch_shapes=GATHER_SEMS + [dma((groups,)), dma((groups,)), dma(())],
        compiler_params=pltpu.CompilerParams(collective_id=5, has_side_effects=True, vmem_limit_bytes=VMEM_LIMIT),
        name="att_fwd",
    )(tok, gain, w, wb, taps, hg, hot, wo, meta, docs, cot, wd)


def att_backward(members, ga, wo, nx, mixed, proj, bl, t, u, o, meta, docs, taps, hg, hot, w, wb, outp, resid):
    count, width = nx.shape
    own = resid.shape[0]
    shape = jax.ShapeDtypeStruct
    rows = chip_block
    return pl.pallas_call(
        att_bwd_kernel,
        grid=(count // CHUNK,),
        in_specs=[
            VM, whole(wo.shape), rows(width), rows(DK), rows(4 * DK), rows(DK), rows(SUB), rows(DK), rows(DK),
            rows(DK), chip_docrow(), whole(taps.shape), whole((1, DK)), whole((1, DK)), whole(w.shape), whole(wb.shape), ANY,
            VM,
        ],
        out_specs=[
            rows(width), whole((16, DK)), whole((8, DK)), whole((width, 4 * DK)), whole((DK, width)), whole((8, width)),
            whole((own, width)),
        ],
        out_shape=[
            shape((count, width), BF), shape((16, DK), F32), shape((8, DK), F32), shape((width, 4 * DK), BF),
            shape((DK, width), BF), shape((8, width), F32), shape((own, width), BF),
        ],
        scratch_shapes=[
            pltpu.VMEM((width, 4 * DK), F32), pltpu.VMEM((DK, width), F32), pltpu.VMEM((DK, width), F32),
            pltpu.VMEM((members,) + ga.shape, BF),
        ] + scatter_scratch(own, width) + GATHER_SEMS,
        compiler_params=pltpu.CompilerParams(collective_id=6, has_side_effects=True, vmem_limit_bytes=VMEM_LIMIT),
        name="att_bwd",
    )(ga, wo, nx, mixed, proj, bl, t, u, o, meta, docs, taps, hg, hot, w, wb, outp, resid)


def mlp(groups, members, f, nm, cot, w, wd):
    count, width = cot.shape
    ffp = wd.shape[0]
    shape = jax.ShapeDtypeStruct
    mine, down = (width // groups, 2 * ffp), (f, width)
    away = [(groups - 1,) + mine, (groups - 1,) + down]
    return pl.pallas_call(
        functools.partial(mlp_kernel, groups, f, ffp),
        grid=(count // CHUNK,),
        in_specs=[VM, chip_block(width), whole(w.shape), whole(wd.shape)],
        out_specs=[chip_block(width), chip_block(width), whole(mine), whole(down), whole(away[0]), whole(away[1])],
        out_shape=[
            shape((count, width), BF), shape((count, width), BF), shape(mine, F32), shape(down, F32), shape(away[0], BF),
            shape(away[1], BF),
        ],
        scratch_shapes=[
            pltpu.VMEM(w.shape, F32), pltpu.VMEM(wd.shape, F32), pltpu.VMEM((members,) + nm.shape, BF)
        ] + GATHER_SEMS,
        compiler_params=pltpu.CompilerParams(collective_id=7, has_side_effects=True, vmem_limit_bytes=VMEM_LIMIT),
        name="mlp",
    )(nm, cot, w, wd)


MESH = pl.DeviceIdType.MESH
CORE = 1
BITS = (2, 4, 8)
TURNED = (((0, 640, (2, 4, 8)), (640, 640, (4, 8, 2)), (1280, 768, (8, 2, 4))),)
LIGHT = tuple(
    tuple((b * 1024 + i * 512, 512, ((8, 2, 4), (8, 4, 2))[i]) for i in range(2)) for b in range(2)
)
PARTS = 4


def flat_plan(plan):
    return tuple(part for batch in plan for part in batch)


ANY = pl.BlockSpec(memory_space=pl.ANY)
VM = pl.BlockSpec(memory_space=pltpu.VMEM)


def flip(me, mask):
    out = me
    bit = 1
    while bit <= mask:
        if mask & bit:
            out = out + bit * (1 - 2 * lax.rem(me // bit, 2))
        bit *= 2
    return out


def greet_cube(me_g, me, groups=1):
    barrier = pltpu.get_barrier_semaphore()
    for bit in (CORE,) + BITS:
        pl.semaphore_signal(barrier, inc=1, device_id=(me_g, flip(me, bit)), device_id_type=MESH)
    for k in range(1, groups):
        pl.semaphore_signal(barrier, inc=1, device_id=(lax.rem(me_g + k, groups), me), device_id_type=MESH)
    pl.semaphore_wait(barrier, len(BITS) + groups)


def greet_members(me_g, me, members):
    barrier = pltpu.get_barrier_semaphore()

    @pl.loop(1, members)
    def _(k):
        pl.semaphore_signal(barrier, inc=1, device_id=(me_g, lax.rem(me + k, members)), device_id_type=MESH)

    pl.semaphore_wait(barrier, members - 1)


def remote(src, dst, send, recv, g, m):
    return pltpu.make_async_remote_copy(
        src_ref=src, dst_ref=dst, send_sem=send, recv_sem=recv, device_id=(g, m), device_id_type=MESH
    )


CHIPS = (0, 2, 4, 8, 6, 10, 12, 14)


def chip_at(step, me):
    out = me // 2
    for bit in BITS:
        hit = sum(jnp.where(step == at, 1, 0) for at, mask in enumerate(CHIPS) if mask & bit)
        half = bit // 2
        out = out + hit * half * (1 - 2 * lax.rem(out // half, 2))
    return out


class CubeGather:
    def __init__(self, plan, me_g, me, block, out, local, link_send, link_recv, core_send, core_recv):
        plan = flat_plan(plan)
        self.plan, self.me_g, self.me, self.block, self.out = plan, me_g, me, block, out
        self.local, self.ls, self.lr, self.cs, self.cr = local, link_send, link_recv, core_send, core_recv
        self.parts = range(len(plan))

    def view(self, slot, j):
        at, size, _ = self.plan[j]
        return self.out.at[slot, :, pl.ds(at, size)]

    def source(self, mask, j):
        at, size, _ = self.plan[j]
        return self.block.at[:, pl.ds(at, size)] if mask == 0 else self.view(flip(self.me, mask), j)

    def masks(self, j, step):
        held = [0]
        for bit in self.plan[j][2][:step]:
            held = held + [h + bit for h in held]
        return held

    def hop(self, mask, j, step):
        i = (1 << step) - 1 + self.masks(j, step).index(mask)
        return remote(
            self.source(mask, j), self.view(flip(self.me, mask), j), self.ls.at[j, i], self.lr.at[j, i], self.me_g,
            flip(self.me, self.plan[j][2][step]),
        )

    def core(self, mask, j):
        i = mask // 2
        return remote(
            self.source(mask, j), self.view(flip(self.me, mask), j), self.cs.at[j, i], self.cr.at[j, i], self.me_g,
            flip(self.me, CORE),
        )

    def own(self):
        return pltpu.make_async_copy(self.block, self.out.at[self.me], self.local)

    def start(self):
        for step in range(3):
            for j in self.parts:
                self.hop(0, j, step).start()
        for j in self.parts:
            self.core(0, j).start()
        self.own().start()

    def arrival(self, mask, j, step):
        i = (1 << step) - 1 + self.masks(j, step).index(mask)
        bit = self.plan[j][2][step]
        view = self.view(flip(self.me, mask + bit), j)
        return remote(view, view, self.ls.at[j, i], self.lr.at[j, i], self.me_g, flip(self.me, bit))

    def advance(self, step):
        for count in range(1 << step):
            for j in self.parts:
                mask = self.masks(j, step)[count]
                self.arrival(mask, j, step).wait_recv()
                got = mask + self.plan[j][2][step]
                for later in range(step + 1, 3):
                    self.hop(got, j, later).start()
                self.core(got, j).start()

    def take(self, got):
        for j in self.parts:
            order = self.plan[j][2]
            step = max(i for i in range(3) if order[i] & got)
            self.arrival(got - order[step], j, step).wait_recv()
            for later in range(step + 1, 3):
                self.hop(got, j, later).start()
            self.core(got, j).start()

    def take_core(self, mask):
        for j in self.parts:
            view = self.view(flip(self.me, mask + CORE), j)
            remote(
                view, view, self.cs.at[j, mask // 2], self.cr.at[j, mask // 2], self.me_g, flip(self.me, CORE)
            ).wait_recv()

    def sent(self):
        for j in self.parts:
            for step in range(3):
                for mask in self.masks(j, step):
                    self.hop(mask, j, step).wait_send()
            for mask in range(0, 16, 2):
                self.core(mask, j).wait_send()

    def host(self, step):
        for at, masks in ((1, (2, 4, 8)), (3, (6, 10, 12)), (5, (14,))):
            @pl.when(step == at)
            def _():
                for mask in masks:
                    self.take(mask)

        for at, mask in enumerate(CHIPS):
            @pl.when(step == at)
            def _():
                if mask == 0:
                    self.own().wait()
                self.take_core(mask)

    def finish(self):
        for mask in range(0, 16, 2):
            for j in self.parts:
                view = self.view(flip(self.me, mask + CORE), j)
                remote(
                    view, view, self.cs.at[j, mask // 2], self.cr.at[j, mask // 2], self.me_g, flip(self.me, CORE)
                ).wait_recv()
        for j in self.parts:
            for step in range(3):
                for mask in self.masks(j, step):
                    self.hop(mask, j, step).wait_send()
            for mask in range(0, 16, 2):
                self.core(mask, j).wait_send()
        self.own().wait()


GATHER_SEMS = [
    pltpu.SemaphoreType.DMA(()), pltpu.SemaphoreType.DMA((PARTS, 7)), pltpu.SemaphoreType.DMA((PARTS, 7)),
    pltpu.SemaphoreType.DMA((PARTS, 8)), pltpu.SemaphoreType.DMA((PARTS, 8)),
]


class CubeScatter:
    def __init__(self, plan, me_g, me, part, mine, other, sums, got, local, core_send, core_recv, link_send, link_recv):
        self.batches = plan
        self.plan = flat_plan(plan)
        self.me_g, self.me, self.part, self.mine, self.other = me_g, me, part, mine, other
        self.sums, self.got, self.local = sums, got, local
        self.cs, self.cr, self.ls, self.lr = core_send, core_recv, link_send, link_recv
        self.parts = range(len(self.plan))

    def order(self, j):
        return self.plan[j][2][::-1]

    ORDER = (14, 6, 10, 12, 2, 4, 8, 0)

    def core_copy(self, b, mask):
        i = mask // 2
        first = self.batches[b][0][0]
        columns = pl.ds(first, sum(part[1] for part in self.batches[b]))
        return remote(
            self.part.at[flip(self.me, mask + CORE), :, columns], self.other.at[i, :, columns], self.cs.at[b, i],
            self.cr.at[b, i], self.me_g, flip(self.me, CORE),
        )

    def load_copy(self, mask):
        i = mask // 2
        return pltpu.make_async_copy(self.part.at[flip(self.me, mask)], self.mine.at[i], self.local.at[i])

    def masks(self, j, step):
        b = self.order(j)
        rest = [0]
        for bit in b[step + 1 :]:
            rest = rest + [h + bit for h in rest]
        return [b[step] + h for h in rest]

    def slot(self, j, step, mask):
        return (0, 4, 6)[step] + self.masks(j, step).index(mask)

    def copy(self, j, step, mask):
        bit = self.order(j)[step]
        i = self.slot(j, step, mask)
        at, size, _ = self.plan[j]
        return remote(
            self.sums.at[i, :, pl.ds(at, size)], self.got.at[i, :, pl.ds(at, size)], self.ls.at[j, i], self.lr.at[j, i],
            self.me_g, flip(self.me, bit),
        )

    def total(self, j, mask, steps):
        at, size, _ = self.plan[j]
        i = mask // 2
        x = self.mine[i, :, at : at + size].astype(F32) + self.other[i, :, at : at + size].astype(F32)
        for step in range(steps):
            k = self.slot(j, step, mask + self.order(j)[step])
            x = x + self.got[k, :, at : at + size].astype(F32)
        return x

    def send(self, j, step, mask):
        at, size, _ = self.plan[j]
        self.sums[self.slot(j, step, mask), :, at : at + size] = self.total(j, mask, step).astype(BF)
        self.copy(j, step, mask).start()

    def start(self):
        for b in range(len(self.batches)):
            for mask in self.ORDER:
                self.core_copy(b, mask).start()
                if b == 0:
                    self.load_copy(mask).start()

    def phase(self, number, store=None):
        if number == 0:
            at = 0
            for b, batch in enumerate(self.batches):
                for mask in self.ORDER:
                    self.core_copy(b, mask).wait_recv()
                    if b == 0:
                        self.load_copy(mask).wait()
                    for j in range(at, at + len(batch)):
                        if mask in self.masks(j, 0):
                            self.send(j, 0, mask)
                at += len(batch)
        elif number < 3:
            for j in self.parts:
                bits = self.order(j)
                for mask in self.masks(j, number):
                    for earlier in range(number):
                        self.copy(j, earlier, mask + bits[earlier]).wait_recv()
                    self.send(j, number, mask)
        else:
            for j in self.parts:
                at, size, _ = self.plan[j]
                for step in range(3):
                    self.copy(j, step, self.order(j)[step]).wait_recv()
                store(j, at, size, self.total(j, 0, 3))

    def run(self, out):
        def store(j, at, size, got):
            out[:, at : at + size] = got

        for number in range(4):
            self.phase(number, store)

    def finish(self):
        for b in range(len(self.batches)):
            for mask in self.ORDER:
                self.core_copy(b, mask).wait_send()
        for j in self.parts:
            for step in range(3):
                for mask in self.masks(j, step):
                    self.copy(j, step, mask).wait_send()


def scatter_scratch(rows, width):
    dma = pltpu.SemaphoreType.DMA
    return [
        pltpu.VMEM((8, rows, width), BF), pltpu.VMEM((8, rows, width), BF), pltpu.VMEM((7, rows, width), BF),
        pltpu.VMEM((7, rows, width), BF), dma((8,)), dma((2, 8)), dma((2, 8)), dma((PARTS, 7)), dma((PARTS, 7)),
    ]


NS = 9
NG = len(GATHER_SEMS)


def middle_forward(got, flat, gain):
    resid = flat.astype(F32) + got
    r = lax.rsqrt(jnp.mean(resid * resid, axis=-1, keepdims=True) + EPS)
    return resid, (resid * r * gain).astype(BF)


def norm_backward(grad, x, gain):
    r = lax.rsqrt(jnp.mean(x * x, axis=-1, keepdims=True) + EPS)
    n = x * r
    e = grad * gain
    return r * (e - n * jnp.mean(e * n, axis=-1, keepdims=True)), jnp.sum(grad * n, axis=0, keepdims=True)


def forward_turn_kernel(part, flat, gain, resid, block, total, *sems):
    me_g, me = lax.axis_index("g"), lax.axis_index("m")
    greet_cube(me_g, me)
    scatter = CubeScatter(LIGHT, me_g, me, part, *sems)
    scatter.start()
    scatter.run(total)
    resid[...], block[...] = middle_forward(total[...], flat[...], gain[...])
    scatter.finish()


def backward_turn_kernel(part, resid, gain, cot, grad_resid, ggain, block, total, *sems):
    me_g, me = lax.axis_index("g"), lax.axis_index("m")
    greet_cube(me_g, me)
    scatter = CubeScatter(LIGHT, me_g, me, part, *sems)
    scatter.start()
    scatter.run(total)
    back, gsum = norm_backward(total[...], resid[...], gain[...])
    grad = cot[...].astype(F32) + back
    grad_resid[...] = grad
    ggain[...] = jnp.broadcast_to(gsum, ggain.shape)
    block[...] = grad.astype(BF)
    scatter.finish()


def turn_call(kernel, outs, rows, width, cid, name, args):
    return pl.pallas_call(
        kernel,
        in_specs=[ANY] + [VM] * (len(args) - 1),
        out_specs=[VM] * (len(outs) + 1),
        out_shape=outs + [jax.ShapeDtypeStruct((rows, width), BF)],
        scratch_shapes=[pltpu.VMEM((rows, width), F32)] + scatter_scratch(rows, width),
        compiler_params=pltpu.CompilerParams(collective_id=cid, has_side_effects=True, vmem_limit_bytes=VMEM_LIMIT),
        name=name,
    )(*args)


def forward_turn(part, flat, gain):
    _, rows, width = part.shape
    outs = [jax.ShapeDtypeStruct((rows, width), F32)]
    return turn_call(forward_turn_kernel, outs, rows, width, 1, "turn_fwd", (part, flat, gain))


def backward_turn(part, resid, gain, cot):
    _, rows, width = part.shape
    outs = [jax.ShapeDtypeStruct((rows, width), F32), jax.ShapeDtypeStruct((8, width), F32)]
    return turn_call(backward_turn_kernel, outs, rows, width, 2, "turn_bwd", (part, resid, gain, cot))


class Spread:
    def __init__(self, groups, members, me_g, me):
        self.groups, self.members = groups, members
        self.count = groups * members
        self.me_d = me_g * members + me

    def peer(self, k):
        d = lax.rem(self.me_d + k, self.count)
        return d, d // self.members, lax.rem(d, self.members)

    def back(self, k):
        return lax.rem(self.me_d + self.count - k, self.count)

    def greet(self):
        barrier = pltpu.get_barrier_semaphore()

        @pl.loop(1, self.count)
        def _(k):
            _, g, m = self.peer(k)
            pl.semaphore_signal(barrier, inc=1, device_id=(g, m), device_id_type=MESH)

        pl.semaphore_wait(barrier, self.count - 1)


def head_of(m, rho, srange):
    return (m % rho) * srange + m // rho


def ff_block(w, groups, members, m, f, ffp):
    lane = lax.broadcasted_iota(jnp.int32, (w.shape[0], ffp), 1)
    out = jnp.zeros((w.shape[0], ffp), F32)
    for g in range(groups):
        at, to = (g * members + m) * f, g * f
        first = min(at // DK * DK, w.shape[1] - ffp)
        x = pltpu.roll(w[:, first : first + ffp].astype(F32), (to - (at - first)) % ffp, 1)
        out = jnp.where((lane >= to) & (lane < to + f), x, out)
    return out.astype(BF)


def one_hot(rows, lanes, shift=0):
    row = lax.broadcasted_iota(jnp.int32, (rows, lanes), 0)
    lane = lax.broadcasted_iota(jnp.int32, (rows, lanes), 1)
    return (row + shift == lane).astype(BF)


PACK = 32


def make_pack(chan, docs):
    body = chan.astype(F32)
    row = lax.broadcasted_iota(jnp.int32, (8, DK), 0)
    lane = lax.broadcasted_iota(jnp.int32, (8, DK), 1)
    flags = jnp.where(lane == 0, 1, docs).astype(BF)
    src = lax.broadcasted_iota(jnp.int32, (DK, DK), 0)
    dst = lax.broadcasted_iota(jnp.int32, (DK, DK), 1) - SEQ
    count = mm(flags, ((src <= dst) & (src < SEQ)).astype(BF), 1, 0) - 1.0
    live = jnp.where(lane - SEQ < docs, 1.0, 0.0)
    upper = jnp.where(lane < SEQ, 0.0, jnp.where(row < 2, count, jnp.where(row < 4, live, 0.0)))
    return jnp.concatenate([body[:8] + upper, body[8:]], axis=0).astype(BF)


def read_packs(
    groups, members, rho, r, hgr, me_g, me, packs, gain_in, gain_mid, hg, wb, taps, meta, docs, rows_in, rows_mid, rows_hg
):
    n = groups * members
    lane1 = lax.broadcasted_iota(jnp.int32, (1, DK), 1)
    back = one_hot(PACK, DK)
    back = jnp.where(lax.broadcasted_iota(jnp.int32, (PACK, DK), 0) < members, back, jnp.zeros_like(back))

    @pl.loop(0, n)
    def _(d):
        p = packs[d]
        wb[pl.ds(pl.multiple_of(d * r, r), r), :] = mm(p, back, 0, 0)[:r].astype(BF)
        x = p.astype(F32)
        rows_in[pl.ds(d, 1), :] = x[28:29]
        rows_mid[pl.ds(d, 1), :] = x[29:30]
        rows_hg[pl.ds(d, 1), :] = x[30:31]

    per = DK // r
    for out, src in ((gain_in, rows_in), (gain_mid, rows_mid)):
        for i in range(n // per):
            tile = src[i * per : i * per + 1]
            for j in range(1, per):
                tile = tile + pltpu.roll(src[i * per + j : i * per + j + 1], j * r, 1)
            out[:, i * DK : (i + 1) * DK] = tile
    src = lax.broadcasted_iota(jnp.int32, (DK, DK), 0)
    dst = lax.broadcasted_iota(jnp.int32, (DK, DK), 1)
    spread = ((src < hgr) & (src == lax.rem(dst, hgr))).astype(BF)
    every = mm(rows_hg[...].astype(BF), spread, 1, 0)
    drow = lax.broadcasted_iota(jnp.int32, (n, DK), 0)
    dlane = lax.broadcasted_iota(jnp.int32, (n, DK), 1)
    hg[...] = jnp.sum(jnp.where(dlane // hgr == drow, every, 0.0), axis=0, keepdims=True)

    lane16 = lax.broadcasted_iota(jnp.int32, (16, DK), 1)
    total = jnp.zeros((16, DK), F32)
    for i in range(rho):
        d = lax.rem(me, rho) * members + (me // rho) * rho + i
        x = jnp.where(lane16 < r, packs[d].astype(F32)[16:32], 0.0)
        total = total + (pltpu.roll(x, i * r, 1) if i else x)
    taps[...] = total

    to_rows = one_hot(8, DK)
    row128 = lax.broadcasted_iota(jnp.int32, (SUB, DK), 0)
    lane128 = lax.broadcasted_iota(jnp.int32, (SUB, DK), 1)

    @pl.loop(0, members)
    def _(j):
        x = packs[me_g * members + j].astype(F32)[:8]
        turned = pltpu.roll(x, SEQ, 1)
        doc = jnp.where(lane1 < SEQ, turned[0:1], x[1:2])
        live = jnp.where(lane1 < SEQ, turned[2:3], x[3:4])
        lines = [doc]
        for o in range(1, TAPS):
            keep = (lax.rem(lane1, SEQ) >= o) & (pltpu.roll(doc, o, 1) == doc)
            lines.append(jnp.where(keep, 1.0, 0.0))
        lines += [live, jnp.zeros((3, DK), F32)]
        lines = jnp.concatenate(lines, axis=0).astype(BF)
        first = (2 * SEQ * j).astype(F32)
        docs[j] = doc + first + jnp.where(lane1 < SEQ, 0.0, float(SEQ))
        block = mm(lines, to_rows, 0, 0)
        shift = first + jnp.where(row128 < SEQ, 0.0, float(SEQ))
        meta[pl.ds(pl.multiple_of(j * SUB, SUB), SUB), :] = block + jnp.where(lane128 == 0, shift, 0.0)


def head_of(m, rho, srange):
    return (m % rho) * srange + m // rho


def start_kernel(
    groups, members, rho, hgr, tok, wq, wk, wv, wg, w_gate, w_up, wo, chan, starts,
    tok_all, w_att, w_out, ff_half, gain_in, gain_mid, hg, wb, taps, meta, docs,
    att, ff, pack, packs, rows_in, rows_mid, rows_hg, sa, ra, sx, rx, sp, rp, sf, rf, so, ro, loc, *sems,
):
    me_g, me = lax.axis_index("g"), lax.axis_index("m")
    spread = Spread(groups, members, me_g, me)
    me_d = spread.me_d
    r = wq.shape[0]
    f = w_gate.shape[1] // spread.count
    ffp = ff.shape[2] // 2
    spread.greet()
    gather = CubeGather(LIGHT, me_g, me, tok, tok_all, *sems)
    for m in range(members):
        h = head_of(m, rho, members // rho) * DK
        for i, w in enumerate((wq, wk, wv, wg)):
            att[m, :, i * DK : (i + 1) * DK] = w[:, h : h + DK]

    def att_copy(k):
        m = lax.rem(me + k, members)
        return remote(att.at[m], w_att.at[me_d], sa.at[k], ra.at[k], me_g, m)

    def att_far(k, step):
        d = me_g * members + lax.rem(me + members - k, members)
        return remote(
            w_att.at[d], w_att.at[d], sx.at[step, k], rx.at[step, k], lax.rem(me_g + step, groups), me
        )

    def att_far_own(step):
        return remote(
            att.at[me], w_att.at[me_d], sx.at[step, 0], rx.at[step, 0], lax.rem(me_g + step, groups), me
        )

    def ff_copy(k):
        m = lax.rem(me + k, members)
        return remote(ff.at[m], ff_half.at[me], sf.at[k], rf.at[k], me_g, m)

    def pack_copy(k, g, m):
        return remote(pack, packs.at[me_d], sp.at[k], rp.at[k], g, m)

    target = (me // rho) * rho + me_g
    place = lax.rem(me, rho)
    sources = [(lax.rem(me, rho), (me // rho) * rho + i) for i in range(rho)]

    def out_copy(g):
        return remote(wo, w_out.at[place], so.at[g], ro.at[place], g, target)

    for step in range(1, groups):
        att_far_own(step).start()

    @pl.loop(1, members)
    def _(k):
        att_copy(k).start()

    gather.start()
    pack[...] = make_pack(chan[...], starts[...])

    @pl.loop(1, spread.count)
    def _(k):
        _, g, m = spread.peer(k)
        pack_copy(k, g, m).start()

    packs[me_d] = pack[...]
    copies = [
        pltpu.make_async_copy(att.at[me], w_att.at[me_d], loc.at[0]),
    ]
    for copy in copies:
        copy.start()

    def relay(first, last):
        @pl.loop(first, last)
        def _(k):
            att_copy(k).wait_recv()
            for step in range(1, groups):
                att_far(k, step).start()

    relay(1, members // 2)
    gather.advance(0)
    relay(members // 2, members)
    for g in range(groups):
        @pl.when((me_g != g) | (me != target))
        def _():
            out_copy(g).start()

    @pl.when(me == target)
    def _():
        pltpu.make_async_copy(wo, w_out.at[place], loc.at[2]).start()

    for m in range(members):
        for i, w in enumerate((w_gate, w_up)):
            ff[m, :, i * ffp : (i + 1) * ffp] = ff_block(w, groups, members, m, f, ffp)
    gather.advance(1)

    @pl.loop(1, members)
    def _(k):
        ff_copy(k).start()

    ff_own = pltpu.make_async_copy(ff.at[me], ff_half.at[me], loc.at[3])
    ff_own.start()
    gather.advance(2)

    @pl.loop(1, spread.count)
    def _(k):
        _, g, m = spread.peer(k)
        pack_copy(k, g, m).wait()

    read_packs(
        groups, members, rho, r, hgr, me_g, me, packs, gain_in, gain_mid, hg, wb, taps, meta, docs, rows_in, rows_mid, rows_hg
    )
    gather.finish()

    @pl.loop(1, members)
    def _(k):
        att_copy(k).wait_send()
        ff_copy(k).wait()
        for step in range(1, groups):
            att_far(k, step).wait()

    for step in range(1, groups):
        att_far_own(step).wait()
    for copy in copies:
        copy.wait()
    ff_own.wait()
    for g in range(groups):
        @pl.when((me_g != g) | (me != target))
        def _():
            out_copy(g).wait_send()
    for i in range(rho):
        src_g, src_m = sources[i]
        @pl.when((me_g != src_g) | (me != src_m))
        def _():
            remote(wo, w_out.at[i], so.at[0], ro.at[i], me_g, me).wait_recv()

    @pl.when(me == target)
    def _():
        pltpu.make_async_copy(wo, w_out.at[place], loc.at[2]).wait()


def start_call(groups, members, rho, hgr, ffp, tok, weights, ffw, wo, chan, starts):
    shape = jax.ShapeDtypeStruct
    n = groups * members
    r, width = wo.shape
    count = members * tok.shape[0]
    dma = pltpu.SemaphoreType.DMA
    return pl.pallas_call(
        functools.partial(start_kernel, groups, members, rho, hgr),
        in_specs=[ANY] + [VM] * 6 + [ANY] + [VM] * 2,
        out_specs=[ANY] * 4 + [VM] * 7,
        out_shape=[
            shape((members,) + tok.shape, BF), shape((n, r, 4 * DK), BF), shape((rho, r, width), BF),
            shape((members, r, 2 * ffp), BF), shape((1, width), F32), shape((1, width), F32),
            shape((1, DK), F32), shape((width, DK), BF), shape((16, DK), F32), shape((count, DK), F32),
            shape((count // SUB, 1, SUB), F32),
        ],
        scratch_shapes=[
            pltpu.VMEM((members, r, 4 * DK), BF), pltpu.VMEM((members, r, 2 * ffp), BF), pltpu.VMEM((PACK, DK), BF),
            pltpu.VMEM((n, PACK, DK), BF), pltpu.VMEM((n, DK), F32), pltpu.VMEM((n, DK), F32), pltpu.VMEM((n, DK), F32),
            dma((members,)), dma((members,)), dma((groups, members)),
            dma((groups, members)), dma((n,)), dma((n,)), dma((members,)), dma((members,)), dma((groups,)), dma((rho,)),
            dma((4,)),
        ] + GATHER_SEMS,
        compiler_params=pltpu.CompilerParams(collective_id=3, has_side_effects=True, vmem_limit_bytes=VMEM_LIMIT),
        name="start",
    )(tok, *weights, *ffw, wo, chan, starts)


def ff_place(out, x, groups, members, m, f, ffp):
    x = x.astype(F32)
    lane = lax.broadcasted_iota(jnp.int32, x.shape, 1)
    for g in range(groups):
        at, to = (g * members + m) * f, g * f
        first = min(at // DK * DK, out.shape[1] - ffp)
        there = at - first
        y = pltpu.roll(x, (there - to) % ffp, 1)
        keep = (lane >= there) & (lane < there + f)
        out[:, first : first + ffp] = jnp.where(keep, y, out[:, first : first + ffp])


def end_kernel(
    groups, members, rho, hgr, part, flat, gain, gmid, gbeta, ghg, gtaps, gatt, gff, gout,
    grad_in, att_in, ff_in, out_in, small_in, tap_in, gain_in,
    total, vec, mine, far, sums, small, tapg, sa, ra, sx, rx, ss, rs, sf, rf, so, ro, st, rt, sg, rg, loc, *sems,
):
    me_g, me = lax.axis_index("g"), lax.axis_index("m")
    spread = Spread(groups, members, me_g, me)
    me_d = spread.me_d
    r = gout.shape[1]
    spread.greet()
    scatter = CubeScatter(LIGHT, me_g, me, part, *sems)

    def att_far(k, step):
        g = lax.rem(me_g + step, groups)
        m = lax.rem(me + k, members)
        return remote(gatt.at[g * members + m], far.at[step - 1, m], sx.at[step - 1, k], rx.at[step - 1, k], g, me)

    def att_copy(k):
        m = lax.rem(me + k, members)
        return remote(sums.at[m], att_in.at[me], sa.at[k], ra.at[k], me_g, m)

    def small_copy(k, d, g, m):
        return remote(small.at[d], small_in.at[me_d], ss.at[k], rs.at[k], g, m)

    def ff_copy(k):
        m = lax.rem(me + k, members)
        return remote(gff.at[m], ff_in.at[me], sf.at[k], rf.at[k], me_g, m)

    def gain_copy(k, g, m):
        return remote(vec, gain_in.at[me_d], sg.at[k], rg.at[k], g, m)

    home = lax.rem(me, rho)
    base = (me // rho) * rho

    def out_copy(i):
        return remote(gout.at[i], out_in.at[me_g], so.at[i], ro.at[me_g], home, base + i)

    def tap_copy(i):
        return remote(tapg.at[i], tap_in.at[me_g], st.at[i], rt.at[me_g], home, base + i)

    @pl.loop(0, members)
    def _(k):
        for step in range(1, groups):
            att_far(k, step).start()

    own_rows = pltpu.make_async_copy(gatt.at[pl.ds(me_g * members, members)], mine, loc.at[0])
    own_rows.start()
    scatter.start()
    lane = lax.broadcasted_iota(jnp.int32, (1, DK), 1)
    per = DK // r
    for d in range(spread.count):
        tile = pl.ds(d // per * DK, DK)
        back = (DK - d % per * r) % DK
        lines = [turned(gmid[0:1, tile], back), turned(gbeta[0:1, tile], back)]
        hg_back = (DK - d * hgr % DK) % DK
        small[d] = jnp.concatenate(
            [jnp.where(lane < r, x, 0.0) for x in lines]
            + [jnp.where(lane < hgr, turned(ghg[0:1], hg_back), 0.0), jnp.zeros((5, DK), F32)],
            axis=0,
        )
    lane16 = lax.broadcasted_iota(jnp.int32, (16, DK), 1)
    for i in range(rho):
        tapg[i] = jnp.where(lane16 < r, turned(gtaps[...], (DK - i * r) % DK), 0.0)

    @pl.loop(1, spread.count)
    def _(k):
        d, g, m = spread.peer(k)
        small_copy(k, d, g, m).start()

    copies = [
        pltpu.make_async_copy(small.at[me_d], small_in.at[me_d], loc.at[1]),
        pltpu.make_async_copy(gff.at[me], ff_in.at[me], loc.at[2]),
    ]
    for copy in copies:
        copy.start()
    for i in range(rho):
        @pl.when((me_g != home) | (me != base + i))
        def _():
            out_copy(i).start()
            tap_copy(i).start()

        @pl.when((me_g == home) & (me == base + i))
        def _():
            pltpu.make_async_copy(gout.at[i], out_in.at[me_g], loc.at[3]).start()
            pltpu.make_async_copy(tapg.at[i], tap_in.at[me_g], loc.at[4]).start()

    scatter.phase(0)

    @pl.loop(1, members)
    def _(k):
        ff_copy(k).start()

    def store(j, at, size, got):
        total[:, at : at + size] = got

    own_rows.wait()

    def relay(first, last):
        @pl.loop(first, last)
        def _(k):
            m = lax.rem(me + k, members)
            x = mine[m].astype(F32)
            for step in range(1, groups):
                att_far(k, step).wait_recv()
                x = x + far[step - 1, m].astype(F32)
            sums[m] = x.astype(BF)

            @pl.when(k > 0)
            def _():
                att_copy(k).start()

    relay(0, members // 4)
    scatter.phase(1)
    relay(members // 4, members // 2)
    scatter.phase(2)
    scatter.phase(3, store)
    back, gsum = norm_backward(total[...], flat[...].astype(F32), gain[...])
    grad_in[...] = back
    for i in range(vec.shape[0]):
        vec[i : i + 1, :] = gsum[:, i * DK : (i + 1) * DK]

    @pl.loop(1, spread.count)
    def _(k):
        _, g, m = spread.peer(k)
        gain_copy(k, g, m).start()

    own = pltpu.make_async_copy(vec, gain_in.at[me_d], loc.at[5])
    own.start()
    relay(members // 2, members)
    scatter.finish()
    kept = pltpu.make_async_copy(sums.at[me], att_in.at[me], loc.at[6])
    kept.start()

    @pl.loop(1, members)
    def _(k):
        att_copy(k).wait()
        ff_copy(k).wait()

    kept.wait()

    @pl.loop(0, members)
    def _(k):
        for step in range(1, groups):
            att_far(k, step).wait_send()

    @pl.loop(1, spread.count)
    def _(k):
        d, g, m = spread.peer(k)
        small_copy(k, d, g, m).wait()
        gain_copy(k, g, m).wait()

    for copy in copies:
        copy.wait()
    own.wait()
    for i in range(rho):
        @pl.when((me_g != home) | (me != base + i))
        def _():
            out_copy(i).wait_send()
            tap_copy(i).wait_send()

        @pl.when((me_g == home) & (me == base + i))
        def _():
            pltpu.make_async_copy(gout.at[i], out_in.at[me_g], loc.at[3]).wait()
            pltpu.make_async_copy(tapg.at[i], tap_in.at[me_g], loc.at[4]).wait()
    holder = base + me_g
    for g in range(groups):
        @pl.when((me_g != g) | (me != holder))
        def _():
            remote(gout.at[0], out_in.at[g], so.at[0], ro.at[g], me_g, me).wait_recv()
            remote(tapg.at[0], tap_in.at[g], st.at[0], rt.at[g], me_g, me).wait_recv()


def turned(x, shift):
    return pltpu.roll(x, shift, 1) if shift else x


def finish_kernel(
    groups, members, rho, grad_in, grad_resid, att_in, ff_in, out_in, small_in, tap_in, gain_in,
    input_grad, gq, gk, gv, gg, g_gate, g_up, g_out, s_in, s_mid, s_hg, g_beta, g_tq, g_tk, g_tv, vec,
):
    me_g, me = lax.axis_index("g"), lax.axis_index("m")
    n = groups * members
    me_d = me_g * members + me
    r = out_in.shape[1]
    ffp = ff_in.shape[2] // 2
    f = g_gate.shape[1] // n
    input_grad[...] = grad_resid[...] + grad_in[...]
    for m in range(members):
        h = head_of(m, rho, members // rho) * DK
        for i, out in enumerate((gq, gk, gv, gg)):
            out[:, h : h + DK] = att_in[m, :, i * DK : (i + 1) * DK].astype(F32)
    for m in range(members):
        for i, out in enumerate((g_gate, g_up)):
            ff_place(out, ff_in[m, :, i * ffp : (i + 1) * ffp], groups, members, m, f, ffp)
    g_out[...] = sum(out_in[g].astype(F32) for g in range(groups))
    taps = sum(tap_in[g] for g in range(groups))
    for i, out in enumerate((g_tq, g_tk, g_tv)):
        out[...] = taps[i * TAPS : (i + 1) * TAPS, :r]
    for m in range(members):
        row = small_in[m, 1:2]
        for g in range(1, groups):
            row = row + small_in[g * members + m, 1:2]
        h = head_of(m, rho, members // rho)
        g_beta[h : h + 1] = row[:, :r]
    acc = jnp.sum(small_in[...], axis=0)
    vec[...] = jnp.sum(gain_in[...], axis=0)
    at = me_d * r
    own_gain = pltpu.roll(vec[pl.ds(at // DK, 1), :], lax.rem(DK - lax.rem(at, DK), DK), 1)
    s_in[...] = own_gain[:, :r]
    s_mid[...] = acc[0:1, :r]
    s_hg[...] = acc[2:3, : s_hg.shape[1]]


def finish_call(groups, members, rho, hidden, hgr, heads, args):
    shape = jax.ShapeDtypeStruct
    rows, width = args[0].shape
    r = args[4].shape[1]
    outs = [(rows, width)] + [(r, width)] * 4 + [(r, hidden)] * 2 + [(r, width), (1, r), (1, r), (1, hgr), (heads, r)]
    outs += [(TAPS, r)] * 3
    return pl.pallas_call(
        functools.partial(finish_kernel, groups, members, rho),
        in_specs=[VM] * len(args),
        out_specs=[VM] * len(outs),
        out_shape=[shape(o, F32) for o in outs],
        scratch_shapes=[pltpu.VMEM((width // DK, DK), F32)],
        compiler_params=pltpu.CompilerParams(vmem_limit_bytes=VMEM_LIMIT),
        name="finish",
    )(*args)


def end_call(groups, members, rho, hgr, part, flat, gain, gmid, gbeta, ghg, gtaps, gatt, gff, gout):
    shape = jax.ShapeDtypeStruct
    n = groups * members
    _, rows, width = part.shape
    r = gout.shape[1]
    dma = pltpu.SemaphoreType.DMA
    piece = (r, 4 * DK)
    return pl.pallas_call(
        functools.partial(end_kernel, groups, members, rho, hgr),
        in_specs=[ANY] + [VM] * 6 + [ANY] * 3,
        out_specs=[VM] + [ANY] * 6,
        out_shape=[
            shape((rows, width), F32), shape((members,) + piece, BF), shape(gff.shape, BF),
            shape((groups,) + gout.shape[1:], BF), shape((n, 8, DK), F32), shape((groups, 16, DK), F32),
            shape((n, width // DK, DK), F32),
        ],
        scratch_shapes=[
            pltpu.VMEM((rows, width), F32), pltpu.VMEM((width // DK, DK), F32), pltpu.VMEM((members,) + piece, BF),
            pltpu.VMEM((groups - 1, members) + piece, BF), pltpu.VMEM((members,) + piece, BF),
            pltpu.VMEM((n, 8, DK), F32), pltpu.VMEM((rho, 16, DK), F32), dma((members,)), dma((members,)),
            dma((groups - 1, members)), dma((groups - 1, members)), dma((n,)), dma((n,)), dma((members,)), dma((members,)),
            dma((rho,)), dma((groups,)), dma((rho,)), dma((groups,)), dma((n,)), dma((n,)), dma((7,)),
        ] + scatter_scratch(rows, width),
        compiler_params=pltpu.CompilerParams(collective_id=4, has_side_effects=True, vmem_limit_bytes=VMEM_LIMIT),
        name="end",
    )(part, flat, gain, gmid, gbeta, ghg, gtaps, gatt, gff, gout)


def exchange_groups(x, groups):
    return [
        lax.ppermute(x[step - 1], "g", [(i, (i + step) % groups) for i in range(groups)]) for step in range(1, groups)
    ]


def make_shards(groups, members):
    def shards(
        tokens, doc_starts, seq_lengths, attn_gain, query_weight, key_weight, value_weight, out_gate_weight, beta_weight,
        query_conv, key_conv, value_conv, head_gain, out_weight, mlp_gain, mlp_gate_weight, mlp_up_weight,
        mlp_down_weight, cotangent,
    ):
        n = groups * members
        width = tokens.shape[-1]
        r = attn_gain.shape[0]
        f = mlp_down_weight.shape[0]
        hgr = head_gain.shape[0]
        heads = beta_weight.shape[1]
        rho = DK // r
        srange = members // rho
        me_g, me_m = lax.axis_index("g"), lax.axis_index("m")
        head = lax.rem(me_m, rho) * srange + me_m // rho
        seqs = tokens.shape[0] * tokens.shape[1]
        seq = tokens.shape[2]
        own = seqs * seq
        flat_bf = tokens.reshape(own, width)
        grad_out = cotangent.reshape(own, width)

        lines = [beta_weight.T, query_conv.T, key_conv.T, value_conv.T, attn_gain[None], mlp_gain[None]]
        lines.append(jnp.pad(head_gain, (0, r - hgr))[None])
        chan = jnp.concatenate(lines, axis=0)
        chan = jnp.pad(chan, ((0, PACK - chan.shape[0]), (0, DK - r)))
        starts = jnp.pad(doc_starts.reshape(seqs, seq), ((0, 0), (0, DK - seq)))
        lengths = jnp.broadcast_to(seq_lengths.reshape(seqs, 1), (seqs, DK))
        starts = jnp.pad(jnp.concatenate([starts, lengths]), ((0, 8 - 2 * seqs), (0, 0)))
        ffw = groups * f
        ffp = -(-ffw // DK) * DK
        hidden_size = mlp_gate_weight.shape[1]
        count = members * own
        tok_all, w_att, w_out, ff_half, gain_in, gain_mid, hg, beta_full, taps, meta, docs_row = start_call(
            groups, members, rho, hgr, ffp, flat_bf, (query_weight, key_weight, value_weight, out_gate_weight),
            (mlp_gate_weight, mlp_up_weight), out_weight, chan, starts,
        )
        w_ff = lax.all_gather(ff_half, "g", axis=0).reshape(width, 2 * ffp)
        w_att = w_att.reshape(width, 4 * DK)
        w_out = w_out.reshape(DK, width)
        hot = (jnp.arange(DK) == head).astype(F32).reshape(1, DK)

        blocks = (members, own, width)
        nx, proj, bl, t, u, o, mixed, part, cot_all, w_down = att_forward(
            groups, members, tok_all.reshape(count, width), gain_in, w_att, beta_full, taps, hg, hot, w_out, meta, docs_row,
            grad_out, mlp_down_weight,
        )
        w_down = jnp.pad(w_down.reshape(ffw, width), ((0, ffp - ffw), (0, 0)))
        resid, nm = forward_turn(part.reshape(blocks), flat_bf, gain_mid)
        out_part, gmid_part, g_ff, g_down, ff_away, down_away = mlp(
            groups, members, f, nm, cot_all.reshape(count, width), w_ff, w_down
        )
        ff_came = exchange_groups(ff_away, groups)
        g_down = sum((x.astype(F32) for x in exchange_groups(down_away, groups)), g_down)
        g_ff = sum((x.astype(F32) for x in ff_came), g_ff).astype(BF).reshape(members, r, 2 * ffp)
        grad_resid, g_mid_gain, ga = backward_turn(gmid_part.reshape(blocks), resid, gain_mid, grad_out)
        gpart, gtaps, ghg, gatt, gout, g_beta, layer_out = att_backward(
            members, ga, w_out, nx, mixed, proj, bl, t, u, o, meta, docs_row, taps, hg, hot, w_att, beta_full,
            out_part.reshape(blocks), resid,
        )
        gatt = gatt.reshape(n, r, 4 * DK)
        gout = gout.reshape(rho, r, width)
        came = end_call(
            groups, members, rho, hgr, gpart.reshape(blocks), flat_bf, gain_in, g_mid_gain, g_beta, ghg, gtaps, gatt, g_ff,
            gout,
        )
        args = (came[0], grad_resid) + tuple(came[1:])
        input_grad, gq, gk, gv, gg, g_gate, g_up, g_out, s_in, s_mid, s_hg, s_beta, s_q, s_k, s_v = finish_call(
            groups, members, rho, hidden_size, hgr, heads, args
        )
        s_in, s_mid, s_hg = s_in.reshape(r), s_mid.reshape(r), s_hg.reshape(hgr)
        s_beta, s_q, s_k, s_v = s_beta.T, s_q.T, s_k.T, s_v.T
        return (
            layer_out.reshape(tokens.shape), input_grad.reshape(tokens.shape),
            s_in, gq, gk, gv, gg, s_beta, s_q, s_k, s_v, s_hg, g_out, s_mid, g_gate, g_up,
            g_down,
        )

    return shards


def solution(mesh):
    n = mesh.devices.size
    members = 16
    groups = n // members
    inner = Mesh(mesh.devices.reshape(groups, members), ("g", "m"))
    both = ("g", "m")
    acts, mat, vec = P(None, both, None, None), P(both, None), P(both)
    return jax.shard_map(
        make_shards(groups, members),
        mesh=inner,
        in_specs=(acts, P(None, both, None), P(None, both), vec, mat, mat, mat, mat, mat, mat, mat, mat, vec, mat, vec,
                  mat, mat, mat, acts),
        out_specs=(acts, acts, vec, mat, mat, mat, mat, mat, mat, mat, mat, vec, mat, vec, mat, mat, mat),
        check_vma=False,
    )
```

```python
import functools

import jax
import jax.numpy as jnp
from jax import lax
from jax.experimental import pallas as pl
from jax.experimental.pallas import tpu as pltpu
from jax.sharding import Mesh
from jax.sharding import PartitionSpec as P

DK = 128
EPS = 1e-05
L2EPS = 1e-06
CHUNK = 256
SEQ = 64
SUB = 128
TAPS = 4
BF = jnp.bfloat16
F32 = jnp.float32
VMEM_LIMIT = 60 << 20


def mm(a, b, ca, cb):
    return lax.dot_general(a, b, (((ca,), (cb,)), ((), ())), preferred_element_type=F32)


def split(x):
    hi = x.astype(BF)
    return hi, (x - hi.astype(F32)).astype(BF)


def mm3(a, b, ca, cb):
    (ah, al), (bh, bl) = a, b
    out = mm(ah, bh, ca, cb)
    if bl is not None:
        out = out + mm(ah, bl, ca, cb)
    if al is not None:
        out = out + mm(al, bh, ca, cb)
    return out


def sigmoid(x):
    return 1.0 / (1.0 + jnp.exp(-x))


def iotas():
    row = lax.broadcasted_iota(jnp.int32, (SUB, SUB), 0)
    col = lax.broadcasted_iota(jnp.int32, (SUB, SUB), 1)
    return row, col


def unit_lower_inverses(blocks, row, col):
    eye = (row == col).astype(F32)
    pair = (row // 2) == (col // 2)
    xs = [eye - jnp.where(pair, a, 0.0) for a in blocks]
    size = 2
    while size < SEQ:
        keep = ((row // (2 * size)) == (col // (2 * size))) & ((row // size) != (col // size))
        offs = [split(jnp.where(keep, a, 0.0)) for a in blocks]
        parts = [split(x) for x in xs]
        ys = [split(mm3(off, p, 1, 0)) for off, p in zip(offs, parts)]
        xs = [x - mm3(p, y, 1, 0) for x, p, y in zip(xs, parts, ys)]
        size *= 2
    return xs


def conv_forward(x, taps, base, masks):
    out = x * taps[base + TAPS - 1 : base + TAPS]
    for o in range(1, TAPS):
        out = out + pltpu.roll(x, o, 0) * masks[o - 1] * taps[base + TAPS - 1 - o : base + TAPS - o]
    return out


def unit(act):
    r = lax.rsqrt(jnp.sum(act * act, axis=-1, keepdims=True) + L2EPS)
    return act * r, r


def subs(x):
    return [x[i * SUB : (i + 1) * SUB] for i in range(CHUNK // SUB)]


def att_fwd_kernel(
    tok_ref, gain_ref, w_ref, wb_ref, taps_ref, hg_ref, hot_ref, wo_ref, meta_ref, doc_ref, cot_ref, flat_ref, mid_ref,
    nx_ref, proj_ref, bl_ref, t_ref, u_ref, o_ref, mixed_ref, resid_ref, nm_ref, cot_all, part_ref, *sems,
):
    step = pl.program_id(0)
    me_g, me = lax.axis_index("g"), lax.axis_index("m")
    scatter = CubeScatter(STREAM, me_g, me, part_ref, None, *sems[NG:])

    def gather():
        return CubeGather(LIGHT, me_g, me, cot_ref, cot_all, *sems[:NG])

    @pl.when(step == 0)
    def _():
        greet_cube(me_g, me)
        gather().start()

    scatter.host(step, FAR, LATE)

    for at, hop in ((2, 0), (4, 1), (6, 2)):
        @pl.when(step == at)
        def _():
            gather().advance(hop)

    x = tok_ref[...].astype(F32)
    nx = (x * lax.rsqrt(jnp.mean(x * x, axis=-1, keepdims=True) + EPS) * gain_ref[...]).astype(BF)
    nx_ref[...] = nx
    proj = mm(nx, w_ref[...], 1, 0)
    proj_ref[...] = proj
    logits = mm(nx, wb_ref[...], 1, 0)
    logit = jnp.sum(logits * hot_ref[...], axis=-1, keepdims=True)
    bl_ref[...] = jnp.broadcast_to(logit, (CHUNK, DK))
    meta = meta_ref[...]
    doc = meta[:, 0:1]
    masks = [meta[:, o : o + 1] for o in range(1, TAPS)]
    beta = sigmoid(logit) * meta[:, 4:5]
    taps = taps_ref[...]
    acts = []
    for i in range(3):
        c = conv_forward(proj[:, i * DK : (i + 1) * DK], taps, i * TAPS, masks)
        acts.append(c * sigmoid(c))
    qs = subs(unit(acts[0])[0].astype(BF))
    ks = subs(unit(acts[1])[0].astype(BF))
    vs = subs(acts[2].astype(BF))
    betas, docs = subs(beta), subs(doc)
    row, col = iotas()
    sames = [d == doc_ref[i] for i, d in enumerate(docs)]
    blocks = [jnp.where(same & (row > col), bt * mm(k, k, 1, 1), 0.0) for same, bt, k in zip(sames, betas, ks)]
    ts = unit_lower_inverses(blocks, row, col)
    os = []
    for i, (t, bt, v, q, k, same) in enumerate(zip(ts, betas, vs, qs, ks, sames)):
        at = pl.ds(i * SUB, SUB)
        t_ref[at, :] = t
        u = mm3(split(t), split(bt * v.astype(F32)), 1, 0)
        u_ref[at, :] = u
        p = jnp.where(same & (row >= col), mm(q, k, 1, 1), 0.0)
        os.append(mm3(split(p), split(u), 1, 0))
    o = jnp.concatenate(os, axis=0)
    o_ref[...] = o
    gate = proj[:, 3 * DK :]
    n_o = o * lax.rsqrt(jnp.mean(o * o, axis=-1, keepdims=True) + EPS)
    mixed = (n_o * hg_ref[...] * (gate * sigmoid(gate))).astype(BF)
    mixed_ref[...] = mixed
    part = mm(mixed, wo_ref[...], 1, 0).astype(BF)
    chip = chip_at(step, me, FAR)
    part_ref[2 * chip] = part[:SUB]
    part_ref[2 * chip + 1] = part[SUB:]
    scatter.made(step, FAR)

    @pl.when(step == pl.num_programs(0) - 1)
    def _():
        def store(j, at, size, got):
            resid_ref[:, at : at + size] = flat_ref[:, at : at + size].astype(F32) + got

        scatter.last(0, ())
        scatter.phase(3, store)
        resid = resid_ref[...]
        r = lax.rsqrt(jnp.mean(resid * resid, axis=-1, keepdims=True) + EPS)
        nm_ref[...] = (resid * r * mid_ref[...]).astype(BF)
        scatter.finish()
        gather().finish()


def att_bwd_kernel(
    own_ref, wo_ref, nx_ref, mixed_ref, proj_ref, bl_ref, t_ref, u_ref, o_ref, meta_ref, doc_ref, taps_ref, hg_ref, hot_ref,
    w_ref, wb_ref, outp_ref, resid_ref,
    part_ref, gtaps_ref, ghg_ref, gatt_ref, gout_ref, gbeta_ref, layer_ref,
    gatt_acc, gout_acc, gbeta_acc, ga_all, *sems,
):
    step = pl.program_id(0)
    me_g, me = lax.axis_index("g"), lax.axis_index("m")

    def scatter():
        return CubeScatter(OUT_PLAN, me_g, me, outp_ref, *sems[:NS])

    gather = CubeGather(LIGHT, me_g, me, own_ref, ga_all, *sems[NS:])

    @pl.when(step == 0)
    def _():
        greet_cube(me_g, me)
        gather.start()
        gtaps_ref[...] = jnp.zeros_like(gtaps_ref)
        ghg_ref[...] = jnp.zeros_like(ghg_ref)
        gatt_acc[...] = jnp.zeros_like(gatt_acc)
        gout_acc[...] = jnp.zeros_like(gout_acc)
        gbeta_acc[...] = jnp.zeros_like(gbeta_acc)

    gather.host(step)

    @pl.when(step == OUT_STEPS[0])
    def _():
        scatter().start()

    for at, phase in zip(OUT_STEPS[1:], range(3)):
        @pl.when(step == at)
        def _():
            scatter().phase(phase)

    proj = proj_ref[...]
    meta = meta_ref[...]
    doc = meta[:, 0:1]
    masks = [meta[:, o : o + 1] for o in range(1, TAPS)]
    logit = bl_ref[:, 0:1]
    sig = sigmoid(logit)
    live = meta[:, 4:5]
    beta = sig * live
    taps = taps_ref[...]
    convs, sigs, acts = [], [], []
    for i in range(3):
        c = conv_forward(proj[:, i * DK : (i + 1) * DK], taps, i * TAPS, masks)
        s = sigmoid(c)
        convs.append(c)
        sigs.append(s)
        acts.append(c * s)
    uq, rq = unit(acts[0])
    uk, rk = unit(acts[1])
    q, k, v = uq.astype(BF), uk.astype(BF), acts[2].astype(BF)

    ga = chip_rows(ga_all, chip_at(step, me))
    gm = mm(ga, wo_ref[...], 1, 1)
    gout_acc[...] += mm(mixed_ref[...], ga, 0, 0)
    o = o_ref[...]
    gate = proj[:, 3 * DK :]
    sg = sigmoid(gate)
    z = gate * sg
    r_o = lax.rsqrt(jnp.mean(o * o, axis=-1, keepdims=True) + EPS)
    n_o = o * r_o
    gmh = gm * hg_ref[...]
    e = gmh * z
    go = r_o * (e - n_o * jnp.mean(e * n_o, axis=-1, keepdims=True))
    ggate = gmh * n_o * (sg * (1.0 + gate * (1.0 - sg)))
    ghg_ref[0:1] += jnp.sum(gm * n_o * z, axis=0, keepdims=True)

    row, col = iotas()
    gqs, gks, gvs, gbs = [], [], [], []
    for i, (dc, q_, k_, v_, bt, go_) in enumerate(zip(subs(doc), subs(q), subs(k), subs(v), subs(beta), subs(go))):
        at = pl.ds(i * SUB, SUB)
        same = dc == doc_ref[i]
        strict = same & (row > col)
        causal = same & (row >= col)
        kk = mm(k_, k_, 1, 1)
        p = jnp.where(causal, mm(q_, k_, 1, 1), 0.0)
        us = split(u_ref[at, :])
        gos = split(go_)
        dp = split(jnp.where(causal, mm3(gos, us, 1, 1), 0.0))
        du = mm3(split(p), gos, 0, 0)
        dw = mm3(split(t_ref[at, :]), split(du), 0, 0)
        da = jnp.where(strict, -mm3(split(dw), us, 1, 1), 0.0)
        dkk = split(bt * da)
        gqs.append(mm3(dp, (k_, None), 1, 0))
        gks.append(mm3(dp, (q_, None), 0, 0) + mm3(dkk, (k_, None), 1, 0) + mm3(dkk, (k_, None), 0, 0))
        gvs.append(bt * dw)
        gbs.append(
            jnp.sum(dw * v_.astype(F32), axis=-1, keepdims=True) + jnp.sum(da * kk, axis=-1, keepdims=True)
        )
    gq, gk, gv, gbeta = (jnp.concatenate(parts, axis=0) for parts in (gqs, gks, gvs, gbs))
    gbl = gbeta * live * sig * (1.0 - sig)
    gb = (gbl * hot_ref[...]).astype(BF)

    gacts = [
        (gq - uq * jnp.sum(uq * gq, axis=-1, keepdims=True)) * rq,
        (gk - uk * jnp.sum(uk * gk, axis=-1, keepdims=True)) * rk,
        gv,
    ]
    grads = []
    for i in range(3):
        x = proj[:, i * DK : (i + 1) * DK]
        gc = gacts[i] * (sigs[i] * (1.0 + convs[i] * (1.0 - sigs[i])))
        base = i * TAPS
        gx = gc * taps[base + TAPS - 1 : base + TAPS]
        j = base + TAPS - 1
        gtaps_ref[j : j + 1] += jnp.sum(gc * x, axis=0, keepdims=True)
        for off in range(1, TAPS):
            gco = gc * masks[off - 1]
            j = base + TAPS - 1 - off
            gtaps_ref[j : j + 1] += jnp.sum(gco * pltpu.roll(x, off, 0), axis=0, keepdims=True)
            gx = gx + pltpu.roll(gco, CHUNK - off, 0) * taps[j : j + 1]
        grads.append(gx.astype(BF))
    gproj = jnp.concatenate(grads + [ggate.astype(BF)], axis=1)
    part = mm(gproj, w_ref[...], 1, 1) + mm(gb, wb_ref[...], 1, 1)
    part_ref[...] = part.astype(BF)
    nx = nx_ref[...]
    gatt_acc[...] += mm(nx, gproj, 0, 0)
    gbeta_acc[...] += mm(gb, nx, 0, 0)

    @pl.when(step == pl.num_programs(0) - 1)
    def _():
        gatt_ref[...] = gatt_acc[...].astype(BF)
        gout_ref[...] = gout_acc[...].astype(BF)
        gbeta_ref[...] = jnp.broadcast_to(jnp.sum(gbeta_acc[...], axis=0, keepdims=True), gbeta_ref.shape)
        done = scatter()
        done.phase(3, lambda j, at, size, got: layer_out_store(layer_ref, resid_ref, at, size, got))
        done.finish()
        gather.sent()


def chip_rows(ref, chip):
    return jnp.concatenate([ref[2 * chip], ref[2 * chip + 1]], axis=0)


def layer_out_store(layer_ref, resid_ref, at, size, got):
    layer_ref[:, at : at + size] = (resid_ref[:, at : at + size] + got).astype(BF)


def mlp_kernel(
    groups, f, ffp, own_ref, cot_ref, w_ref, wd_ref, resid_ref, mid_ref, grad_ref,
    out_ref, gw_ref, gd_ref, gw_away, gd_away, gresid_ref, ggain_ref, ga_ref, gw_acc, gd_acc, nm_all, part_ref, *sems,
):
    step = pl.program_id(0)
    me_g, me = lax.axis_index("g"), lax.axis_index("m")
    gather = CubeGather(TURNED, me_g, me, own_ref, nm_all, *sems[:NG])
    scatter = CubeScatter(STREAM, me_g, me, part_ref, None, *sems[NG:])

    @pl.when(step == 0)
    def _():
        greet_cube(me_g, me)
        gather.start()
        gw_acc[...] = jnp.zeros_like(gw_acc)
        gd_acc[...] = jnp.zeros_like(gd_acc)

    gather.host(step)
    scatter.host(step, CHIPS, NEAR_LATE)
    chip = chip_at(step, me)
    nm = chip_rows(nm_all, chip)
    cot, w, wd = cot_ref[...], w_ref[...], wd_ref[...]
    act = mm(nm, w, 1, 0)
    gate, up = act[:, :ffp], act[:, ffp:]
    s = sigmoid(gate)
    z = gate * s
    hidden = (z * up).astype(BF)
    out_ref[...] = mm(hidden, wd, 1, 0).astype(BF)
    gh = mm(cot, wd, 1, 1)
    gg = (gh * up * (s * (1.0 + gate * (1.0 - s)))).astype(BF)
    gu = (gh * z).astype(BF)
    g = jnp.concatenate([gg, gu], axis=1)
    part = mm(g, w, 1, 1).astype(BF)
    part_ref[2 * chip] = part[:SUB]
    part_ref[2 * chip + 1] = part[SUB:]
    scatter.made(step, CHIPS)

    @pl.when(step == pl.num_programs(0) - 1)
    def _():
        scatter.last(CHIPS[7], ())

    gw_acc[...] += mm(nm, g, 0, 0)
    gd_acc[...] += mm(hidden, cot, 0, 0)

    @pl.when(step == pl.num_programs(0) - 1)
    def _():
        scatter.late(1, 10)
        scatter.late(1, 12)
        size = gw_ref.shape[0]
        gw_ref[...] = gw_acc[pl.ds(pl.multiple_of(me_g * size, 8), size), :].astype(BF)
        for k in range(1, groups):
            g = lax.rem(me_g + k, groups)
            gw_away[k - 1] = gw_acc[pl.ds(pl.multiple_of(g * size, 8), size), :].astype(BF)
        for g in range(groups):
            @pl.when(me_g == g)
            def _():
                gd_ref[...] = gd_acc[g * f : (g + 1) * f].astype(BF)
                for k in range(1, groups):
                    away = (g + k) % groups
                    gd_away[k - 1] = gd_acc[away * f : (away + 1) * f].astype(BF)
        scatter.late(2, 8)

        def store(j, at, size, got):
            gresid_ref[:, at : at + size] = got

        scatter.phase(3, store)
        back, gsum = norm_backward(gresid_ref[...], resid_ref[...], mid_ref[...])
        grad = grad_ref[...].astype(F32) + back
        gresid_ref[...] = grad
        ggain_ref[...] = jnp.broadcast_to(gsum, ggain_ref.shape)
        ga_ref[...] = grad.astype(BF)
        scatter.finish()
        gather.sent()


def rows(width):
    return pl.BlockSpec((CHUNK, width), lambda i: (i, 0))


def whole(shape):
    return pl.BlockSpec(shape, lambda i: (0,) * len(shape))


DOCROW = pl.BlockSpec((CHUNK // SUB, 1, SUB), lambda i: (i, 0, 0))


def chip_block(width):
    return pl.BlockSpec((CHUNK, width), lambda i: (chip_at(i, lax.axis_index("m")), 0))


def chip_docrow():
    return pl.BlockSpec((CHUNK // SUB, 1, SUB), lambda i: (chip_at(i, lax.axis_index("m")), 0, 0))


def far_block(width):
    return pl.BlockSpec((CHUNK, width), lambda i: (chip_at(i, lax.axis_index("m"), FAR), 0))


def far_docrow():
    return pl.BlockSpec((CHUNK // SUB, 1, SUB), lambda i: (chip_at(i, lax.axis_index("m"), FAR), 0, 0))


def att_forward(members, tok, gain, w, wb, taps, hg, hot, wo, meta, docs, cot, flat, mid):
    count, width = tok.shape
    own = flat.shape[0]
    shape = jax.ShapeDtypeStruct
    rows = far_block
    return pl.pallas_call(
        att_fwd_kernel,
        grid=(count // CHUNK,),
        in_specs=[
            rows(width), whole((1, width)), whole(w.shape), whole(wb.shape), whole(taps.shape), whole((1, DK)),
            whole((1, DK)), whole(wo.shape), rows(DK), far_docrow(), ANY, VM, VM,
        ],
        out_specs=[
            rows(width), rows(4 * DK), rows(DK), rows(SUB), rows(DK), rows(DK), rows(DK), whole((own, width)),
            whole((own, width)), ANY,
        ],
        out_shape=[
            shape((count, width), BF), shape((count, 4 * DK), F32), shape((count, DK), F32), shape((count, SUB), F32),
            shape((count, DK), F32), shape((count, DK), F32), shape((count, DK), BF), shape((own, width), F32),
            shape((own, width), BF), shape((members,) + cot.shape, BF),
        ],
        scratch_shapes=[pltpu.VMEM((members, own, width), BF)] + GATHER_SEMS + scatter_scratch(own, width)[1:],
        compiler_params=pltpu.CompilerParams(collective_id=5, has_side_effects=True, vmem_limit_bytes=VMEM_LIMIT),
        name="att_fwd",
    )(tok, gain, w, wb, taps, hg, hot, wo, meta, docs, cot, flat, mid)


def att_backward(members, ga, wo, nx, mixed, proj, bl, t, u, o, meta, docs, taps, hg, hot, w, wb, outp, resid):
    count, width = nx.shape
    own = resid.shape[0]
    shape = jax.ShapeDtypeStruct
    rows = chip_block
    return pl.pallas_call(
        att_bwd_kernel,
        grid=(count // CHUNK,),
        in_specs=[
            VM, whole(wo.shape), rows(width), rows(DK), rows(4 * DK), rows(DK), rows(SUB), rows(DK), rows(DK),
            rows(DK), chip_docrow(), whole(taps.shape), whole((1, DK)), whole((1, DK)), whole(w.shape), whole(wb.shape), ANY,
            VM,
        ],
        out_specs=[
            rows(width), whole((16, DK)), whole((8, DK)), whole((width, 4 * DK)), whole((DK, width)), whole((8, width)),
            whole((own, width)),
        ],
        out_shape=[
            shape((count, width), BF), shape((16, DK), F32), shape((8, DK), F32), shape((width, 4 * DK), BF),
            shape((DK, width), BF), shape((8, width), F32), shape((own, width), BF),
        ],
        scratch_shapes=[
            pltpu.VMEM((width, 4 * DK), F32), pltpu.VMEM((DK, width), F32), pltpu.VMEM((DK, width), F32),
            pltpu.VMEM((members,) + ga.shape, BF),
        ] + scatter_scratch(own, width) + GATHER_SEMS,
        compiler_params=pltpu.CompilerParams(collective_id=6, has_side_effects=True, vmem_limit_bytes=VMEM_LIMIT),
        name="att_bwd",
    )(ga, wo, nx, mixed, proj, bl, t, u, o, meta, docs, taps, hg, hot, w, wb, outp, resid)


def once(shape):
    return pl.BlockSpec(shape, lambda i: (0,) * len(shape), pipeline_mode=pl.Buffered(1))


def mlp(groups, members, f, nm, cot, w, wd, resid, mid, grad_out):
    count, width = cot.shape
    ffp = wd.shape[0]
    own = nm.shape[0]
    shape = jax.ShapeDtypeStruct
    mine, down = (width // groups, 2 * ffp), (f, width)
    away = [(groups - 1,) + mine, (groups - 1,) + down]
    outs = [(mine, BF), (down, BF), (away[0], BF), (away[1], BF), ((own, width), F32), ((8, width), F32), ((own, width), BF)]
    return pl.pallas_call(
        functools.partial(mlp_kernel, groups, f, ffp),
        grid=(count // CHUNK,),
        in_specs=[
            once(nm.shape), chip_block(width), once(w.shape), once(wd.shape), once(resid.shape), once(mid.shape),
            once(grad_out.shape),
        ],
        out_specs=[chip_block(width)] + [once(o) for o, _ in outs],
        out_shape=[shape((count, width), BF)] + [shape(o, t) for o, t in outs],
        scratch_shapes=[
            pltpu.VMEM(w.shape, F32), pltpu.VMEM(wd.shape, F32), pltpu.VMEM((members,) + nm.shape, BF),
            pltpu.VMEM((members,) + nm.shape, BF),
        ] + GATHER_SEMS + scatter_scratch(own, width)[1:],
        compiler_params=pltpu.CompilerParams(collective_id=7, has_side_effects=True, vmem_limit_bytes=VMEM_LIMIT),
        name="mlp",
    )(nm, cot, w, wd, resid, mid, grad_out)


MESH = pl.DeviceIdType.MESH
CORE = 1
BITS = (2, 4, 8)
TURNED = (((0, 640, (2, 4, 8)), (640, 640, (4, 8, 2)), (1280, 768, (8, 2, 4))),)
LIGHT = tuple(
    tuple((b * 1024 + i * 512, 512, ((8, 2, 4), (8, 4, 2))[i]) for i in range(2)) for b in range(2)
)
STREAM = (tuple((i * 512, 512, ((8, 2, 4), (8, 4, 2))[i % 2]) for i in range(4)),)
PARTS = 4
OUT_STEPS = (0, 2, 4, 6)
OUT_PLAN = LIGHT
CUTS = (8, 12)


def flat_plan(plan):
    return tuple(part for batch in plan for part in batch)


ANY = pl.BlockSpec(memory_space=pl.ANY)
VM = pl.BlockSpec(memory_space=pltpu.VMEM)


def flip(me, mask):
    out = me
    bit = 1
    while bit <= mask:
        if mask & bit:
            out = out + bit * (1 - 2 * lax.rem(me // bit, 2))
        bit *= 2
    return out


def greet_cube(me_g, me, groups=1):
    barrier = pltpu.get_barrier_semaphore()
    for bit in (CORE,) + BITS:
        pl.semaphore_signal(barrier, inc=1, device_id=(me_g, flip(me, bit)), device_id_type=MESH)
    for k in range(1, groups):
        pl.semaphore_signal(barrier, inc=1, device_id=(lax.rem(me_g + k, groups), me), device_id_type=MESH)
    pl.semaphore_wait(barrier, len(BITS) + groups)


def greet_members(me_g, me, members):
    barrier = pltpu.get_barrier_semaphore()

    @pl.loop(1, members)
    def _(k):
        pl.semaphore_signal(barrier, inc=1, device_id=(me_g, lax.rem(me + k, members)), device_id_type=MESH)

    pl.semaphore_wait(barrier, members - 1)


def remote(src, dst, send, recv, g, m):
    return pltpu.make_async_remote_copy(
        src_ref=src, dst_ref=dst, send_sem=send, recv_sem=recv, device_id=(g, m), device_id_type=MESH
    )


CHIPS = (0, 2, 4, 8, 6, 10, 12, 14)


def chip_at(step, me, chips=CHIPS):
    out = me // 2
    for bit in BITS:
        hit = sum(jnp.where(step == at, 1, 0) for at, mask in enumerate(chips) if mask & bit)
        half = bit // 2
        out = out + hit * half * (1 - 2 * lax.rem(out // half, 2))
    return out


class CubeGather:
    def __init__(self, plan, me_g, me, block, out, local, link_send, link_recv, core_send, core_recv):
        plan = flat_plan(plan)
        self.plan, self.me_g, self.me, self.block, self.out = plan, me_g, me, block, out
        self.local, self.ls, self.lr, self.cs, self.cr = local, link_send, link_recv, core_send, core_recv
        self.parts = range(len(plan))

    def view(self, slot, j):
        at, size, _ = self.plan[j]
        return self.out.at[slot, :, pl.ds(at, size)]

    def source(self, mask, j):
        at, size, _ = self.plan[j]
        return self.block.at[:, pl.ds(at, size)] if mask == 0 else self.view(flip(self.me, mask), j)

    def masks(self, j, step):
        held = [0]
        for bit in self.plan[j][2][:step]:
            held = held + [h + bit for h in held]
        return held

    def hop(self, mask, j, step):
        i = (1 << step) - 1 + self.masks(j, step).index(mask)
        return remote(
            self.source(mask, j), self.view(flip(self.me, mask), j), self.ls.at[j, i], self.lr.at[j, i], self.me_g,
            flip(self.me, self.plan[j][2][step]),
        )

    def core(self, mask, j):
        i = mask // 2
        return remote(
            self.source(mask, j), self.view(flip(self.me, mask), j), self.cs.at[j, i], self.cr.at[j, i], self.me_g,
            flip(self.me, CORE),
        )

    def own(self):
        return pltpu.make_async_copy(self.block, self.out.at[self.me], self.local)

    def start(self):
        for step in range(3):
            for j in self.parts:
                self.hop(0, j, step).start()
        for j in self.parts:
            self.core(0, j).start()
        self.own().start()

    def arrival(self, mask, j, step):
        i = (1 << step) - 1 + self.masks(j, step).index(mask)
        bit = self.plan[j][2][step]
        view = self.view(flip(self.me, mask + bit), j)
        return remote(view, view, self.ls.at[j, i], self.lr.at[j, i], self.me_g, flip(self.me, bit))

    def advance(self, step):
        for count in range(1 << step):
            for j in self.parts:
                mask = self.masks(j, step)[count]
                self.arrival(mask, j, step).wait_recv()
                got = mask + self.plan[j][2][step]
                for later in range(step + 1, 3):
                    self.hop(got, j, later).start()
                self.core(got, j).start()

    def take(self, got):
        for j in self.parts:
            order = self.plan[j][2]
            step = max(i for i in range(3) if order[i] & got)
            self.arrival(got - order[step], j, step).wait_recv()
            for later in range(step + 1, 3):
                self.hop(got, j, later).start()
            self.core(got, j).start()

    def take_core(self, mask):
        for j in self.parts:
            view = self.view(flip(self.me, mask + CORE), j)
            remote(
                view, view, self.cs.at[j, mask // 2], self.cr.at[j, mask // 2], self.me_g, flip(self.me, CORE)
            ).wait_recv()

    def sent(self):
        for j in self.parts:
            for step in range(3):
                for mask in self.masks(j, step):
                    self.hop(mask, j, step).wait_send()
            for mask in range(0, 16, 2):
                self.core(mask, j).wait_send()

    def host(self, step):
        for at, masks in ((1, (2, 4, 8)), (3, (6, 10, 12)), (5, (14,))):
            @pl.when(step == at)
            def _():
                for mask in masks:
                    self.take(mask)

        for at, mask in enumerate(CHIPS):
            @pl.when(step == at)
            def _():
                if mask == 0:
                    self.own().wait()
                self.take_core(mask)

    def finish(self):
        for mask in range(0, 16, 2):
            for j in self.parts:
                view = self.view(flip(self.me, mask + CORE), j)
                remote(
                    view, view, self.cs.at[j, mask // 2], self.cr.at[j, mask // 2], self.me_g, flip(self.me, CORE)
                ).wait_recv()
        for j in self.parts:
            for step in range(3):
                for mask in self.masks(j, step):
                    self.hop(mask, j, step).wait_send()
            for mask in range(0, 16, 2):
                self.core(mask, j).wait_send()
        self.own().wait()


GATHER_SEMS = [
    pltpu.SemaphoreType.DMA(()), pltpu.SemaphoreType.DMA((PARTS, 7)), pltpu.SemaphoreType.DMA((PARTS, 7)),
    pltpu.SemaphoreType.DMA((PARTS, 8)), pltpu.SemaphoreType.DMA((PARTS, 8)),
]


FAR = (14, 12, 10, 6, 4, 2, 8, 0)
LATE = {4: ((1, 10), (1, 12)), 6: ((1, 4),), 7: ((1, 2), (2, 8))}
NEAR_LATE = {7: ((1, 2), (1, 4))}


class CubeScatter:
    def __init__(self, plan, me_g, me, part, mine, other, sums, got, local, core_send, core_recv, link_send, link_recv):
        self.batches = plan
        self.plan = flat_plan(plan)
        self.me_g, self.me, self.part, self.mine, self.other = me_g, me, part, mine, other
        self.sums, self.got, self.local = sums, got, local
        self.cs, self.cr, self.ls, self.lr = core_send, core_recv, link_send, link_recv
        self.parts = range(len(self.plan))

    def order(self, j):
        return self.plan[j][2][::-1]

    ORDER = (14, 6, 10, 12, 2, 4, 8, 0)

    def core_copy(self, b, mask):
        i = mask // 2
        first = self.batches[b][0][0]
        columns = pl.ds(first, sum(part[1] for part in self.batches[b]))
        return remote(
            self.part.at[flip(self.me, mask + CORE), :, columns], self.other.at[i, :, columns], self.cs.at[b, i],
            self.cr.at[b, i], self.me_g, flip(self.me, CORE),
        )

    def load_copy(self, mask):
        i = mask // 2
        return pltpu.make_async_copy(self.part.at[flip(self.me, mask)], self.mine.at[i], self.local.at[i])

    def masks(self, j, step):
        b = self.order(j)
        rest = [0]
        for bit in b[step + 1 :]:
            rest = rest + [h + bit for h in rest]
        return [b[step] + h for h in rest]

    def slot(self, j, step, mask):
        return (0, 4, 6)[step] + self.masks(j, step).index(mask)

    def copy(self, j, step, mask):
        bit = self.order(j)[step]
        i = self.slot(j, step, mask)
        at, size, _ = self.plan[j]
        return remote(
            self.sums.at[i, :, pl.ds(at, size)], self.got.at[i, :, pl.ds(at, size)], self.ls.at[j, i], self.lr.at[j, i],
            self.me_g, flip(self.me, bit),
        )

    def total(self, j, mask, steps):
        at, size, _ = self.plan[j]
        i = mask // 2
        if self.mine is None:
            x = self.part[flip(self.me, mask), :, at : at + size].astype(F32)
        else:
            x = self.mine[i, :, at : at + size].astype(F32)
        x = x + self.other[i, :, at : at + size].astype(F32)
        for step in range(steps):
            k = self.slot(j, step, mask + self.order(j)[step])
            x = x + self.got[k, :, at : at + size].astype(F32)
        return x

    def send(self, j, step, mask):
        at, size, _ = self.plan[j]
        self.sums[self.slot(j, step, mask), :, at : at + size] = self.total(j, mask, step).astype(BF)
        self.copy(j, step, mask).start()

    def start(self):
        for b in range(len(self.batches)):
            for mask in self.ORDER:
                self.core_copy(b, mask).start()
                if b == 0:
                    self.load_copy(mask).start()

    def phase(self, number, store=None):
        if number == 0:
            at = 0
            for b, batch in enumerate(self.batches):
                for mask in self.ORDER:
                    self.core_copy(b, mask).wait_recv()
                    if b == 0:
                        self.load_copy(mask).wait()
                    for j in range(at, at + len(batch)):
                        if mask in self.masks(j, 0):
                            self.send(j, 0, mask)
                at += len(batch)
        elif number < 3:
            for j in self.parts:
                bits = self.order(j)
                for mask in self.masks(j, number):
                    for earlier in range(number):
                        self.copy(j, earlier, mask + bits[earlier]).wait_recv()
                    self.send(j, number, mask)
        else:
            for j in self.parts:
                at, size, _ = self.plan[j]
                for step in range(3):
                    self.copy(j, step, self.order(j)[step]).wait_recv()
                store(j, at, size, self.total(j, 0, 3))

    def late(self, step, mask):
        for j in self.parts:
            if mask in self.masks(j, step):
                for earlier in range(step):
                    self.copy(j, earlier, mask + self.order(j)[earlier]).wait_recv()
                self.send(j, step, mask)

    def host(self, step, order, others):
        for at in range(1, 8):
            @pl.when(step == at)
            def _():
                mask = order[at - 1]
                self.core_copy(0, mask).wait_recv()
                for j in self.parts:
                    if mask in self.masks(j, 0):
                        self.send(j, 0, mask)
                for late, mask in others.get(at, ()):
                    self.late(late, mask)

    def made(self, step, order):
        for at in range(8):
            @pl.when(step == at)
            def _():
                self.core_copy(0, order[at]).start()

    def last(self, mask, others):
        self.core_copy(0, mask).wait_recv()
        for j in self.parts:
            if mask in self.masks(j, 0):
                self.send(j, 0, mask)
        for late, mask in others:
            self.late(late, mask)

    def run(self, out):
        def store(j, at, size, got):
            out[:, at : at + size] = got

        for number in range(4):
            self.phase(number, store)

    def finish(self):
        for b in range(len(self.batches)):
            for mask in self.ORDER:
                self.core_copy(b, mask).wait_send()
        for j in self.parts:
            for step in range(3):
                for mask in self.masks(j, step):
                    self.copy(j, step, mask).wait_send()


def scatter_scratch(rows, width):
    dma = pltpu.SemaphoreType.DMA
    return [
        pltpu.VMEM((8, rows, width), BF), pltpu.VMEM((8, rows, width), BF), pltpu.VMEM((7, rows, width), BF),
        pltpu.VMEM((7, rows, width), BF), dma((8,)), dma((2, 8)), dma((2, 8)), dma((PARTS, 7)), dma((PARTS, 7)),
    ]


NS = 9
NG = len(GATHER_SEMS)


def norm_backward(grad, x, gain):
    r = lax.rsqrt(jnp.mean(x * x, axis=-1, keepdims=True) + EPS)
    n = x * r
    e = grad * gain
    return r * (e - n * jnp.mean(e * n, axis=-1, keepdims=True)), jnp.sum(grad * n, axis=0, keepdims=True)


class Spread:
    def __init__(self, groups, members, me_g, me):
        self.groups, self.members = groups, members
        self.count = groups * members
        self.me_d = me_g * members + me

    def peer(self, k):
        d = lax.rem(self.me_d + k, self.count)
        return d, d // self.members, lax.rem(d, self.members)

    def back(self, k):
        return lax.rem(self.me_d + self.count - k, self.count)

    def greet(self):
        barrier = pltpu.get_barrier_semaphore()

        @pl.loop(1, self.count)
        def _(k):
            _, g, m = self.peer(k)
            pl.semaphore_signal(barrier, inc=1, device_id=(g, m), device_id_type=MESH)

        pl.semaphore_wait(barrier, self.count - 1)


def head_of(m, rho, srange):
    return (m % rho) * srange + m // rho


def ff_block(w, groups, members, m, f, ffp):
    lane = lax.broadcasted_iota(jnp.int32, (w.shape[0], ffp), 1)
    out = jnp.zeros((w.shape[0], ffp), F32)
    for g in range(groups):
        at, to = (g * members + m) * f, g * f
        first = min(at // DK * DK, w.shape[1] - ffp)
        x = pltpu.roll(w[:, first : first + ffp].astype(F32), (to - (at - first)) % ffp, 1)
        out = jnp.where((lane >= to) & (lane < to + f), x, out)
    return out.astype(BF)


def one_hot(rows, lanes, shift=0):
    row = lax.broadcasted_iota(jnp.int32, (rows, lanes), 0)
    lane = lax.broadcasted_iota(jnp.int32, (rows, lanes), 1)
    return (row + shift == lane).astype(BF)


PACK = 32


def make_pack(chan, docs):
    body = chan.astype(F32)
    row = lax.broadcasted_iota(jnp.int32, (8, DK), 0)
    lane = lax.broadcasted_iota(jnp.int32, (8, DK), 1)
    flags = jnp.where(lane == 0, 1, docs).astype(BF)
    src = lax.broadcasted_iota(jnp.int32, (DK, DK), 0)
    dst = lax.broadcasted_iota(jnp.int32, (DK, DK), 1) - SEQ
    count = mm(flags, ((src <= dst) & (src < SEQ)).astype(BF), 1, 0) - 1.0
    live = jnp.where(lane - SEQ < docs, 1.0, 0.0)
    upper = jnp.where(lane < SEQ, 0.0, jnp.where(row < 2, count, jnp.where(row < 4, live, 0.0)))
    return jnp.concatenate([body[:8] + upper, body[8:]], axis=0).astype(BF)


def read_packs(
    groups, members, rho, r, hgr, me_g, me, packs, gain_in, gain_mid, hg, wb, taps, meta, docs, rows_in, rows_mid, rows_hg
):
    n = groups * members
    lane1 = lax.broadcasted_iota(jnp.int32, (1, DK), 1)
    back = one_hot(PACK, DK)
    back = jnp.where(lax.broadcasted_iota(jnp.int32, (PACK, DK), 0) < members, back, jnp.zeros_like(back))

    @pl.loop(0, n)
    def _(d):
        p = packs[d]
        wb[pl.ds(pl.multiple_of(d * r, r), r), :] = mm(p, back, 0, 0)[:r].astype(BF)
        x = p.astype(F32)
        rows_in[pl.ds(d, 1), :] = x[28:29]
        rows_mid[pl.ds(d, 1), :] = x[29:30]
        rows_hg[pl.ds(d, 1), :] = x[30:31]

    per = DK // r
    for out, src in ((gain_in, rows_in), (gain_mid, rows_mid)):
        for i in range(n // per):
            tile = src[i * per : i * per + 1]
            for j in range(1, per):
                tile = tile + pltpu.roll(src[i * per + j : i * per + j + 1], j * r, 1)
            out[:, i * DK : (i + 1) * DK] = tile
    src = lax.broadcasted_iota(jnp.int32, (DK, DK), 0)
    dst = lax.broadcasted_iota(jnp.int32, (DK, DK), 1)
    spread = ((src < hgr) & (src == lax.rem(dst, hgr))).astype(BF)
    every = mm(rows_hg[...].astype(BF), spread, 1, 0)
    drow = lax.broadcasted_iota(jnp.int32, (n, DK), 0)
    dlane = lax.broadcasted_iota(jnp.int32, (n, DK), 1)
    hg[...] = jnp.sum(jnp.where(dlane // hgr == drow, every, 0.0), axis=0, keepdims=True)

    lane16 = lax.broadcasted_iota(jnp.int32, (16, DK), 1)
    total = jnp.zeros((16, DK), F32)
    for i in range(rho):
        d = lax.rem(me, rho) * members + (me // rho) * rho + i
        x = jnp.where(lane16 < r, packs[d].astype(F32)[16:32], 0.0)
        total = total + (pltpu.roll(x, i * r, 1) if i else x)
    taps[...] = total

    to_rows = one_hot(8, DK)
    row128 = lax.broadcasted_iota(jnp.int32, (SUB, DK), 0)
    lane128 = lax.broadcasted_iota(jnp.int32, (SUB, DK), 1)

    @pl.loop(0, members)
    def _(j):
        x = packs[me_g * members + j].astype(F32)[:8]
        turned = pltpu.roll(x, SEQ, 1)
        doc = jnp.where(lane1 < SEQ, turned[0:1], x[1:2])
        live = jnp.where(lane1 < SEQ, turned[2:3], x[3:4])
        lines = [doc]
        for o in range(1, TAPS):
            keep = (lax.rem(lane1, SEQ) >= o) & (pltpu.roll(doc, o, 1) == doc)
            lines.append(jnp.where(keep, 1.0, 0.0))
        lines += [live, jnp.zeros((3, DK), F32)]
        lines = jnp.concatenate(lines, axis=0).astype(BF)
        first = (2 * SEQ * j).astype(F32)
        docs[j] = doc + first + jnp.where(lane1 < SEQ, 0.0, float(SEQ))
        block = mm(lines, to_rows, 0, 0)
        shift = first + jnp.where(row128 < SEQ, 0.0, float(SEQ))
        meta[pl.ds(pl.multiple_of(j * SUB, SUB), SUB), :] = block + jnp.where(lane128 == 0, shift, 0.0)


def head_of(m, rho, srange):
    return (m % rho) * srange + m // rho


def start_kernel(
    groups, members, rho, hgr, tok, wq, wk, wv, wg, w_gate, w_up, wo, wd, chan, starts,
    tok_all, w_att, w_out, ff_half, down_all, gain_in, gain_mid, hg, wb, taps, meta, docs,
    att, ff, pack, packs, rows_in, rows_mid, rows_hg, sa, ra, sx, rx, sp, rp, sf, rf, so, ro, sd, rd, loc, *sems,
):
    me_g, me = lax.axis_index("g"), lax.axis_index("m")
    spread = Spread(groups, members, me_g, me)
    me_d = spread.me_d
    r = wq.shape[0]
    f = w_gate.shape[1] // spread.count
    ffp = ff.shape[2] // 2
    spread.greet()
    gather = CubeGather(LIGHT, me_g, me, tok, tok_all, *sems)
    for m in range(members):
        h = head_of(m, rho, members // rho) * DK
        for i, w in enumerate((wq, wk, wv, wg)):
            att[m, :, i * DK : (i + 1) * DK] = w[:, h : h + DK]

    def att_copy(k):
        m = lax.rem(me + k, members)
        return remote(att.at[m], w_att.at[me_d], sa.at[k], ra.at[k], me_g, m)

    def att_far(k, step):
        d = me_g * members + lax.rem(me + members - k, members)
        return remote(
            w_att.at[d], w_att.at[d], sx.at[step, k], rx.at[step, k], lax.rem(me_g + step, groups), me
        )

    def att_far_own(step):
        return remote(
            att.at[me], w_att.at[me_d], sx.at[step, 0], rx.at[step, 0], lax.rem(me_g + step, groups), me
        )

    def ff_copy(k):
        m = lax.rem(me + k, members)
        return remote(ff.at[m], ff_half.at[me], sf.at[k], rf.at[k], me_g, m)

    def down_copy(step):
        return remote(wd, down_all.at[me_g], sd.at[step], rd.at[step], lax.rem(me_g + step, groups), me)

    def down_arrival(step):
        src = lax.rem(me_g + groups - step, groups)
        return remote(wd, down_all.at[src], sd.at[step], rd.at[step], me_g, me)

    def pack_copy(k, g, m):
        return remote(pack, packs.at[me_d], sp.at[k], rp.at[k], g, m)

    target = (me // rho) * rho + me_g
    place = lax.rem(me, rho)
    sources = [(lax.rem(me, rho), (me // rho) * rho + i) for i in range(rho)]

    def out_copy(g):
        return remote(wo, w_out.at[place], so.at[g], ro.at[place], g, target)

    for step in range(1, groups):
        att_far_own(step).start()
        down_copy(step).start()

    @pl.loop(1, members)
    def _(k):
        att_copy(k).start()

    gather.start()
    pack[...] = make_pack(chan[...], starts[...])

    @pl.loop(1, spread.count)
    def _(k):
        _, g, m = spread.peer(k)
        pack_copy(k, g, m).start()

    packs[me_d] = pack[...]
    copies = [
        pltpu.make_async_copy(att.at[me], w_att.at[me_d], loc.at[0]),
        pltpu.make_async_copy(wd, down_all.at[me_g], loc.at[1]),
    ]
    for copy in copies:
        copy.start()

    def relay(first, last):
        @pl.loop(first, last)
        def _(k):
            att_copy(k).wait_recv()
            for step in range(1, groups):
                att_far(k, step).start()

    relay(1, members // 2)
    gather.advance(0)
    relay(members // 2, members)
    for g in range(groups):
        @pl.when((me_g != g) | (me != target))
        def _():
            out_copy(g).start()

    @pl.when(me == target)
    def _():
        pltpu.make_async_copy(wo, w_out.at[place], loc.at[2]).start()

    for m in range(members):
        for i, w in enumerate((w_gate, w_up)):
            ff[m, :, i * ffp : (i + 1) * ffp] = ff_block(w, groups, members, m, f, ffp)
    gather.advance(1)

    @pl.loop(1, members)
    def _(k):
        ff_copy(k).start()

    ff_own = pltpu.make_async_copy(ff.at[me], ff_half.at[me], loc.at[3])
    ff_own.start()
    gather.advance(2)

    @pl.loop(1, spread.count)
    def _(k):
        _, g, m = spread.peer(k)
        pack_copy(k, g, m).wait()

    read_packs(
        groups, members, rho, r, hgr, me_g, me, packs, gain_in, gain_mid, hg, wb, taps, meta, docs, rows_in, rows_mid, rows_hg
    )
    gather.finish()

    @pl.loop(1, members)
    def _(k):
        att_copy(k).wait_send()
        ff_copy(k).wait()
        for step in range(1, groups):
            att_far(k, step).wait()

    for step in range(1, groups):
        att_far_own(step).wait()
        down_copy(step).wait_send()
        down_arrival(step).wait_recv()
    for copy in copies:
        copy.wait()
    ff_own.wait()
    for g in range(groups):
        @pl.when((me_g != g) | (me != target))
        def _():
            out_copy(g).wait_send()
    for i in range(rho):
        src_g, src_m = sources[i]
        @pl.when((me_g != src_g) | (me != src_m))
        def _():
            remote(wo, w_out.at[i], so.at[0], ro.at[i], me_g, me).wait_recv()

    @pl.when(me == target)
    def _():
        pltpu.make_async_copy(wo, w_out.at[place], loc.at[2]).wait()


def start_call(groups, members, rho, hgr, ffp, tok, weights, ffw, wo, wd, chan, starts):
    shape = jax.ShapeDtypeStruct
    n = groups * members
    r, width = wo.shape
    count = members * tok.shape[0]
    dma = pltpu.SemaphoreType.DMA
    return pl.pallas_call(
        functools.partial(start_kernel, groups, members, rho, hgr),
        in_specs=[ANY] + [VM] * 6 + [ANY] * 2 + [VM] * 2,
        out_specs=[ANY] * 5 + [VM] * 7,
        out_shape=[
            shape((members,) + tok.shape, BF), shape((n, r, 4 * DK), BF), shape((rho, r, width), BF),
            shape((members, r, 2 * ffp), BF), shape((groups,) + wd.shape, BF), shape((1, width), F32), shape((1, width), F32),
            shape((1, DK), F32), shape((width, DK), BF), shape((16, DK), F32), shape((count, DK), F32),
            shape((count // SUB, 1, SUB), F32),
        ],
        scratch_shapes=[
            pltpu.VMEM((members, r, 4 * DK), BF), pltpu.VMEM((members, r, 2 * ffp), BF), pltpu.VMEM((PACK, DK), BF),
            pltpu.VMEM((n, PACK, DK), BF), pltpu.VMEM((n, DK), F32), pltpu.VMEM((n, DK), F32), pltpu.VMEM((n, DK), F32),
            dma((members,)), dma((members,)), dma((groups, members)),
            dma((groups, members)), dma((n,)), dma((n,)), dma((members,)), dma((members,)), dma((groups,)), dma((rho,)),
            dma((groups,)), dma((groups,)), dma((4,)),
        ] + GATHER_SEMS,
        compiler_params=pltpu.CompilerParams(collective_id=3, has_side_effects=True, vmem_limit_bytes=VMEM_LIMIT),
        name="start",
    )(tok, *weights, *ffw, wo, wd, chan, starts)


def ff_place(out, x, groups, members, m, f, ffp):
    x = x.astype(F32)
    lane = lax.broadcasted_iota(jnp.int32, x.shape, 1)
    for g in range(groups):
        at, to = (g * members + m) * f, g * f
        first = min(at // DK * DK, out.shape[1] - ffp)
        there = at - first
        y = pltpu.roll(x, (there - to) % ffp, 1)
        keep = (lane >= there) & (lane < there + f)
        out[:, first : first + ffp] = jnp.where(keep, y, out[:, first : first + ffp])


def end_kernel(
    groups, members, rho, hgr, part, flat, gain, gmid, gbeta, ghg, gtaps, gatt, gff, gout,
    grad_in, att_in, ff_in, out_in, small_in, tap_in, gain_in,
    total, vec, mine, far, sums, small, tapg, sa, ra, sx, rx, ss, rs, sf, rf, so, ro, st, rt, sg, rg, loc, *sems,
):
    me_g, me = lax.axis_index("g"), lax.axis_index("m")
    spread = Spread(groups, members, me_g, me)
    me_d = spread.me_d
    r = gout.shape[1]
    spread.greet()
    scatter = CubeScatter(LIGHT, me_g, me, part, *sems)

    def att_far(k, step):
        g = lax.rem(me_g + step, groups)
        m = lax.rem(me + k, members)
        return remote(gatt.at[g * members + m], far.at[step - 1, m], sx.at[step - 1, k], rx.at[step - 1, k], g, me)

    def att_copy(k):
        m = lax.rem(me + k, members)
        return remote(sums.at[m], att_in.at[me], sa.at[k], ra.at[k], me_g, m)

    def small_copy(k, d, g, m):
        return remote(small.at[d], small_in.at[me_d], ss.at[k], rs.at[k], g, m)

    def ff_copy(k):
        m = lax.rem(me + k, members)
        return remote(gff.at[m], ff_in.at[me], sf.at[k], rf.at[k], me_g, m)

    def gain_copy(k, g, m):
        return remote(vec, gain_in.at[me_d], sg.at[k], rg.at[k], g, m)

    home = lax.rem(me, rho)
    base = (me // rho) * rho

    def out_copy(i):
        return remote(gout.at[i], out_in.at[me_g], so.at[i], ro.at[me_g], home, base + i)

    def tap_copy(i):
        return remote(tapg.at[i], tap_in.at[me_g], st.at[i], rt.at[me_g], home, base + i)

    @pl.loop(0, members)
    def _(k):
        for step in range(1, groups):
            att_far(k, step).start()

    own_rows = pltpu.make_async_copy(gatt.at[pl.ds(me_g * members, members)], mine, loc.at[0])
    own_rows.start()
    scatter.start()
    lane = lax.broadcasted_iota(jnp.int32, (1, DK), 1)
    per = DK // r
    for d in range(spread.count):
        tile = pl.ds(d // per * DK, DK)
        back = (DK - d % per * r) % DK
        lines = [turned(gmid[0:1, tile], back), turned(gbeta[0:1, tile], back)]
        hg_back = (DK - d * hgr % DK) % DK
        small[d] = jnp.concatenate(
            [jnp.where(lane < r, x, 0.0) for x in lines]
            + [jnp.where(lane < hgr, turned(ghg[0:1], hg_back), 0.0), jnp.zeros((5, DK), F32)],
            axis=0,
        )
    lane16 = lax.broadcasted_iota(jnp.int32, (16, DK), 1)
    for i in range(rho):
        tapg[i] = jnp.where(lane16 < r, turned(gtaps[...], (DK - i * r) % DK), 0.0)

    @pl.loop(1, spread.count)
    def _(k):
        d, g, m = spread.peer(k)
        small_copy(k, d, g, m).start()

    copies = [
        pltpu.make_async_copy(small.at[me_d], small_in.at[me_d], loc.at[1]),
        pltpu.make_async_copy(gff.at[me], ff_in.at[me], loc.at[2]),
    ]
    for copy in copies:
        copy.start()
    for i in range(rho):
        @pl.when((me_g != home) | (me != base + i))
        def _():
            out_copy(i).start()
            tap_copy(i).start()

        @pl.when((me_g == home) & (me == base + i))
        def _():
            pltpu.make_async_copy(gout.at[i], out_in.at[me_g], loc.at[3]).start()
            pltpu.make_async_copy(tapg.at[i], tap_in.at[me_g], loc.at[4]).start()

    scatter.phase(0)

    @pl.loop(1, members)
    def _(k):
        ff_copy(k).start()

    def store(j, at, size, got):
        total[:, at : at + size] = got

    own_rows.wait()

    def relay(first, last):
        @pl.loop(first, last)
        def _(k):
            m = lax.rem(me + k, members)
            x = mine[m].astype(F32)
            for step in range(1, groups):
                att_far(k, step).wait_recv()
                x = x + far[step - 1, m].astype(F32)
            sums[m] = x.astype(BF)

            @pl.when(k > 0)
            def _():
                att_copy(k).start()

    relay(0, CUTS[0])
    scatter.phase(1)
    relay(CUTS[0], CUTS[1])
    scatter.phase(2)
    relay(CUTS[1], members)
    scatter.phase(3, store)
    back, gsum = norm_backward(total[...], flat[...].astype(F32), gain[...])
    grad_in[...] = back
    for i in range(vec.shape[0]):
        vec[i : i + 1, :] = gsum[:, i * DK : (i + 1) * DK]

    @pl.loop(1, spread.count)
    def _(k):
        _, g, m = spread.peer(k)
        gain_copy(k, g, m).start()

    own = pltpu.make_async_copy(vec, gain_in.at[me_d], loc.at[5])
    own.start()
    scatter.finish()
    kept = pltpu.make_async_copy(sums.at[me], att_in.at[me], loc.at[6])
    kept.start()

    @pl.loop(1, members)
    def _(k):
        att_copy(k).wait()
        ff_copy(k).wait()

    kept.wait()

    @pl.loop(0, members)
    def _(k):
        for step in range(1, groups):
            att_far(k, step).wait_send()

    @pl.loop(1, spread.count)
    def _(k):
        d, g, m = spread.peer(k)
        small_copy(k, d, g, m).wait()
        gain_copy(k, g, m).wait()

    for copy in copies:
        copy.wait()
    own.wait()
    for i in range(rho):
        @pl.when((me_g != home) | (me != base + i))
        def _():
            out_copy(i).wait_send()
            tap_copy(i).wait_send()

        @pl.when((me_g == home) & (me == base + i))
        def _():
            pltpu.make_async_copy(gout.at[i], out_in.at[me_g], loc.at[3]).wait()
            pltpu.make_async_copy(tapg.at[i], tap_in.at[me_g], loc.at[4]).wait()
    holder = base + me_g
    for g in range(groups):
        @pl.when((me_g != g) | (me != holder))
        def _():
            remote(gout.at[0], out_in.at[g], so.at[0], ro.at[g], me_g, me).wait_recv()
            remote(tapg.at[0], tap_in.at[g], st.at[0], rt.at[g], me_g, me).wait_recv()


def turned(x, shift):
    return pltpu.roll(x, shift, 1) if shift else x


def finish_kernel(
    groups, members, rho, grad_in, grad_resid, att_in, ff_in, out_in, small_in, tap_in, gain_in,
    input_grad, gq, gk, gv, gg, g_gate, g_up, g_out, s_in, s_mid, s_hg, g_beta, g_tq, g_tk, g_tv, vec,
):
    me_g, me = lax.axis_index("g"), lax.axis_index("m")
    n = groups * members
    me_d = me_g * members + me
    r = out_in.shape[1]
    ffp = ff_in.shape[2] // 2
    f = g_gate.shape[1] // n
    input_grad[...] = grad_resid[...] + grad_in[...]
    for m in range(members):
        h = head_of(m, rho, members // rho) * DK
        for i, out in enumerate((gq, gk, gv, gg)):
            out[:, h : h + DK] = att_in[m, :, i * DK : (i + 1) * DK].astype(F32)
    for m in range(members):
        for i, out in enumerate((g_gate, g_up)):
            ff_place(out, ff_in[m, :, i * ffp : (i + 1) * ffp], groups, members, m, f, ffp)
    g_out[...] = sum(out_in[g].astype(F32) for g in range(groups))
    taps = sum(tap_in[g] for g in range(groups))
    for i, out in enumerate((g_tq, g_tk, g_tv)):
        out[...] = taps[i * TAPS : (i + 1) * TAPS, :r]
    for m in range(members):
        row = small_in[m, 1:2]
        for g in range(1, groups):
            row = row + small_in[g * members + m, 1:2]
        h = head_of(m, rho, members // rho)
        g_beta[h : h + 1] = row[:, :r]
    acc = jnp.sum(small_in[...], axis=0)
    vec[...] = jnp.sum(gain_in[...], axis=0)
    at = me_d * r
    own_gain = pltpu.roll(vec[pl.ds(at // DK, 1), :], lax.rem(DK - lax.rem(at, DK), DK), 1)
    s_in[...] = own_gain[:, :r]
    s_mid[...] = acc[0:1, :r]
    s_hg[...] = acc[2:3, : s_hg.shape[1]]


def finish_call(groups, members, rho, hidden, hgr, heads, args):
    shape = jax.ShapeDtypeStruct
    rows, width = args[0].shape
    r = args[4].shape[1]
    outs = [(rows, width)] + [(r, width)] * 4 + [(r, hidden)] * 2 + [(r, width), (1, r), (1, r), (1, hgr), (heads, r)]
    outs += [(TAPS, r)] * 3
    return pl.pallas_call(
        functools.partial(finish_kernel, groups, members, rho),
        in_specs=[VM] * len(args),
        out_specs=[VM] * len(outs),
        out_shape=[shape(o, F32) for o in outs],
        scratch_shapes=[pltpu.VMEM((width // DK, DK), F32)],
        compiler_params=pltpu.CompilerParams(vmem_limit_bytes=VMEM_LIMIT),
        name="finish",
    )(*args)


def end_call(groups, members, rho, hgr, part, flat, gain, gmid, gbeta, ghg, gtaps, gatt, gff, gout):
    shape = jax.ShapeDtypeStruct
    n = groups * members
    _, rows, width = part.shape
    r = gout.shape[1]
    dma = pltpu.SemaphoreType.DMA
    piece = (r, 4 * DK)
    return pl.pallas_call(
        functools.partial(end_kernel, groups, members, rho, hgr),
        in_specs=[ANY] + [VM] * 6 + [ANY] * 3,
        out_specs=[VM] + [ANY] * 6,
        out_shape=[
            shape((rows, width), F32), shape((members,) + piece, BF), shape(gff.shape, BF),
            shape((groups,) + gout.shape[1:], BF), shape((n, 8, DK), F32), shape((groups, 16, DK), F32),
            shape((n, width // DK, DK), F32),
        ],
        scratch_shapes=[
            pltpu.VMEM((rows, width), F32), pltpu.VMEM((width // DK, DK), F32), pltpu.VMEM((members,) + piece, BF),
            pltpu.VMEM((groups - 1, members) + piece, BF), pltpu.VMEM((members,) + piece, BF),
            pltpu.VMEM((n, 8, DK), F32), pltpu.VMEM((rho, 16, DK), F32), dma((members,)), dma((members,)),
            dma((groups - 1, members)), dma((groups - 1, members)), dma((n,)), dma((n,)), dma((members,)), dma((members,)),
            dma((rho,)), dma((groups,)), dma((rho,)), dma((groups,)), dma((n,)), dma((n,)), dma((7,)),
        ] + scatter_scratch(rows, width),
        compiler_params=pltpu.CompilerParams(collective_id=4, has_side_effects=True, vmem_limit_bytes=VMEM_LIMIT),
        name="end",
    )(part, flat, gain, gmid, gbeta, ghg, gtaps, gatt, gff, gout)


def exchange_groups(x, groups):
    return [
        lax.ppermute(x[step - 1], "g", [(i, (i + step) % groups) for i in range(groups)]) for step in range(1, groups)
    ]


def make_shards(groups, members):
    def shards(
        tokens, doc_starts, seq_lengths, attn_gain, query_weight, key_weight, value_weight, out_gate_weight, beta_weight,
        query_conv, key_conv, value_conv, head_gain, out_weight, mlp_gain, mlp_gate_weight, mlp_up_weight,
        mlp_down_weight, cotangent,
    ):
        n = groups * members
        width = tokens.shape[-1]
        r = attn_gain.shape[0]
        f = mlp_down_weight.shape[0]
        hgr = head_gain.shape[0]
        heads = beta_weight.shape[1]
        rho = DK // r
        srange = members // rho
        me_g, me_m = lax.axis_index("g"), lax.axis_index("m")
        head = lax.rem(me_m, rho) * srange + me_m // rho
        seqs = tokens.shape[0] * tokens.shape[1]
        seq = tokens.shape[2]
        own = seqs * seq
        flat_bf = tokens.reshape(own, width)
        grad_out = cotangent.reshape(own, width)

        lines = [beta_weight.T, query_conv.T, key_conv.T, value_conv.T, attn_gain[None], mlp_gain[None]]
        lines.append(jnp.pad(head_gain, (0, r - hgr))[None])
        chan = jnp.concatenate(lines, axis=0)
        chan = jnp.pad(chan, ((0, PACK - chan.shape[0]), (0, DK - r)))
        starts = jnp.pad(doc_starts.reshape(seqs, seq), ((0, 0), (0, DK - seq)))
        lengths = jnp.broadcast_to(seq_lengths.reshape(seqs, 1), (seqs, DK))
        starts = jnp.pad(jnp.concatenate([starts, lengths]), ((0, 8 - 2 * seqs), (0, 0)))
        ffw = groups * f
        ffp = -(-ffw // DK) * DK
        hidden_size = mlp_gate_weight.shape[1]
        count = members * own
        tok_all, w_att, w_out, ff_half, w_down, gain_in, gain_mid, hg, beta_full, taps, meta, docs_row = start_call(
            groups, members, rho, hgr, ffp, flat_bf, (query_weight, key_weight, value_weight, out_gate_weight),
            (mlp_gate_weight, mlp_up_weight), out_weight, mlp_down_weight, chan, starts,
        )
        w_ff = lax.all_gather(ff_half, "g", axis=0).reshape(width, 2 * ffp)
        w_att = w_att.reshape(width, 4 * DK)
        w_out = w_out.reshape(DK, width)
        hot = (jnp.arange(DK) == head).astype(F32).reshape(1, DK)

        blocks = (members, own, width)
        w_down = jnp.pad(w_down.reshape(ffw, width), ((0, ffp - ffw), (0, 0)))
        nx, proj, bl, t, u, o, mixed, resid, nm, cot_all = att_forward(
            members, tok_all.reshape(count, width), gain_in, w_att, beta_full, taps, hg, hot, w_out, meta, docs_row, grad_out,
            flat_bf, gain_mid,
        )
        out_part, g_ff, g_down, ff_away, down_away, grad_resid, g_mid_gain, ga = mlp(
            groups, members, f, nm, cot_all.reshape(count, width), w_ff, w_down, resid, gain_mid, grad_out
        )
        ff_came = exchange_groups(ff_away, groups)
        g_down = sum((x.astype(F32) for x in exchange_groups(down_away, groups)), g_down.astype(F32))
        g_ff = sum((x.astype(F32) for x in ff_came), g_ff.astype(F32)).astype(BF).reshape(members, r, 2 * ffp)
        gpart, gtaps, ghg, gatt, gout, g_beta, layer_out = att_backward(
            members, ga, w_out, nx, mixed, proj, bl, t, u, o, meta, docs_row, taps, hg, hot, w_att, beta_full,
            out_part.reshape(blocks), resid,
        )
        gatt = gatt.reshape(n, r, 4 * DK)
        gout = gout.reshape(rho, r, width)
        came = end_call(
            groups, members, rho, hgr, gpart.reshape(blocks), flat_bf, gain_in, g_mid_gain, g_beta, ghg, gtaps, gatt, g_ff,
            gout,
        )
        args = (came[0], grad_resid) + tuple(came[1:])
        input_grad, gq, gk, gv, gg, g_gate, g_up, g_out, s_in, s_mid, s_hg, s_beta, s_q, s_k, s_v = finish_call(
            groups, members, rho, hidden_size, hgr, heads, args
        )
        s_in, s_mid, s_hg = s_in.reshape(r), s_mid.reshape(r), s_hg.reshape(hgr)
        s_beta, s_q, s_k, s_v = s_beta.T, s_q.T, s_k.T, s_v.T
        return (
            layer_out.reshape(tokens.shape), input_grad.reshape(tokens.shape),
            s_in, gq, gk, gv, gg, s_beta, s_q, s_k, s_v, s_hg, g_out, s_mid, g_gate, g_up,
            g_down,
        )

    return shards


def solution(mesh):
    n = mesh.devices.size
    members = 16
    groups = n // members
    inner = Mesh(mesh.devices.reshape(groups, members), ("g", "m"))
    both = ("g", "m")
    acts, mat, vec = P(None, both, None, None), P(both, None), P(both)
    return jax.shard_map(
        make_shards(groups, members),
        mesh=inner,
        in_specs=(acts, P(None, both, None), P(None, both), vec, mat, mat, mat, mat, mat, mat, mat, mat, vec, mat, vec,
                  mat, mat, mat, acts),
        out_specs=(acts, acts, vec, mat, mat, mat, mat, mat, mat, mat, mat, vec, mat, vec, mat, mat, mat),
        check_vma=False,
    )
```

```python
import functools

import jax
import jax.numpy as jnp
from jax import lax
from jax.experimental import pallas as pl
from jax.experimental.pallas import tpu as pltpu
from jax.sharding import Mesh
from jax.sharding import PartitionSpec as P

DK = 128
EPS = 1e-05
L2EPS = 1e-06
CHUNK = 256
SEQ = 64
SUB = 128
TAPS = 4
BF = jnp.bfloat16
F32 = jnp.float32
VMEM_LIMIT = 60 << 20


def mm(a, b, ca, cb):
    return lax.dot_general(a, b, (((ca,), (cb,)), ((), ())), preferred_element_type=F32)


def split(x):
    hi = x.astype(BF)
    return hi, (x - hi.astype(F32)).astype(BF)


def mm3(a, b, ca, cb):
    (ah, al), (bh, bl) = a, b
    out = mm(ah, bh, ca, cb)
    if bl is not None:
        out = out + mm(ah, bl, ca, cb)
    if al is not None:
        out = out + mm(al, bh, ca, cb)
    return out


def sigmoid(x):
    return 1.0 / (1.0 + jnp.exp(-x))


def iotas():
    row = lax.broadcasted_iota(jnp.int32, (SUB, SUB), 0)
    col = lax.broadcasted_iota(jnp.int32, (SUB, SUB), 1)
    return row, col


def unit_lower_inverses(blocks, row, col):
    eye = (row == col).astype(F32)
    pair = (row // 2) == (col // 2)
    xs = [eye - jnp.where(pair, a, 0.0) for a in blocks]
    size = 2
    while size < SEQ:
        keep = ((row // (2 * size)) == (col // (2 * size))) & ((row // size) != (col // size))
        offs = [split(jnp.where(keep, a, 0.0)) for a in blocks]
        parts = [split(x) for x in xs]
        ys = [split(mm3(off, p, 1, 0)) for off, p in zip(offs, parts)]
        xs = [x - mm3(p, y, 1, 0) for x, p, y in zip(xs, parts, ys)]
        size *= 2
    return xs


def conv_forward(x, taps, base, masks):
    out = x * taps[base + TAPS - 1 : base + TAPS]
    for o in range(1, TAPS):
        out = out + pltpu.roll(x, o, 0) * masks[o - 1] * taps[base + TAPS - 1 - o : base + TAPS - o]
    return out


def unit(act):
    r = lax.rsqrt(jnp.sum(act * act, axis=-1, keepdims=True) + L2EPS)
    return act * r, r


def subs(x):
    return [x[i * SUB : (i + 1) * SUB] for i in range(CHUNK // SUB)]


def att_fwd_kernel(
    tok_ref, gain_ref, w_ref, wb_ref, taps_ref, hg_ref, hot_ref, wo_ref, meta_ref, doc_ref, cot_ref, flat_ref, mid_ref,
    nx_ref, proj_ref, bl_ref, t_ref, u_ref, o_ref, mixed_ref, resid_ref, nm_ref, cot_all, part_ref, *sems,
):
    step = pl.program_id(0)
    me_g, me = lax.axis_index("g"), lax.axis_index("m")
    scatter = CubeScatter(STREAM, me_g, me, part_ref, None, *sems[NG:])

    def gather():
        return CubeGather(LIGHT, me_g, me, cot_ref, cot_all, *sems[:NG])

    @pl.when(step == 0)
    def _():
        greet_cube(me_g, me)
        gather().start()

    scatter.host(step, FAR, LATE)

    for at, hop in ((2, 0), (4, 1), (6, 2)):
        @pl.when(step == at)
        def _():
            gather().advance(hop)

    x = tok_ref[...].astype(F32)
    nx = (x * lax.rsqrt(jnp.mean(x * x, axis=-1, keepdims=True) + EPS) * gain_ref[...]).astype(BF)
    nx_ref[...] = nx
    proj = mm(nx, w_ref[...], 1, 0)
    proj_ref[...] = proj
    logits = mm(nx, wb_ref[...], 1, 0)
    logit = jnp.sum(logits * hot_ref[...], axis=-1, keepdims=True)
    bl_ref[...] = jnp.broadcast_to(logit, (CHUNK, DK))
    meta = meta_ref[...]
    doc = meta[:, 0:1]
    masks = [meta[:, o : o + 1] for o in range(1, TAPS)]
    beta = sigmoid(logit) * meta[:, 4:5]
    taps = taps_ref[...]
    acts = []
    for i in range(3):
        c = conv_forward(proj[:, i * DK : (i + 1) * DK], taps, i * TAPS, masks)
        acts.append(c * sigmoid(c))
    qs = subs(unit(acts[0])[0].astype(BF))
    ks = subs(unit(acts[1])[0].astype(BF))
    vs = subs(acts[2].astype(BF))
    betas, docs = subs(beta), subs(doc)
    row, col = iotas()
    sames = [d == doc_ref[i] for i, d in enumerate(docs)]
    blocks = [jnp.where(same & (row > col), bt * mm(k, k, 1, 1), 0.0) for same, bt, k in zip(sames, betas, ks)]
    ts = unit_lower_inverses(blocks, row, col)
    os = []
    for i, (t, bt, v, q, k, same) in enumerate(zip(ts, betas, vs, qs, ks, sames)):
        at = pl.ds(i * SUB, SUB)
        t_ref[at, :] = t
        u = mm3(split(t), split(bt * v.astype(F32)), 1, 0)
        u_ref[at, :] = u
        p = jnp.where(same & (row >= col), mm(q, k, 1, 1), 0.0)
        os.append(mm3(split(p), split(u), 1, 0))
    o = jnp.concatenate(os, axis=0)
    o_ref[...] = o
    gate = proj[:, 3 * DK :]
    n_o = o * lax.rsqrt(jnp.mean(o * o, axis=-1, keepdims=True) + EPS)
    mixed = (n_o * hg_ref[...] * (gate * sigmoid(gate))).astype(BF)
    mixed_ref[...] = mixed
    part = mm(mixed, wo_ref[...], 1, 0).astype(BF)
    chip = chip_at(step, me, FAR)
    part_ref[2 * chip] = part[:SUB]
    part_ref[2 * chip + 1] = part[SUB:]
    scatter.made(step, FAR)

    @pl.when(step == pl.num_programs(0) - 1)
    def _():
        def store(j, at, size, got):
            resid_ref[:, at : at + size] = flat_ref[:, at : at + size].astype(F32) + got

        scatter.last(0, ())
        scatter.phase(3, store)
        resid = resid_ref[...]
        r = lax.rsqrt(jnp.mean(resid * resid, axis=-1, keepdims=True) + EPS)
        nm_ref[...] = (resid * r * mid_ref[...]).astype(BF)
        scatter.finish()
        gather().finish()


def att_bwd_kernel(
    own_ref, wo_ref, nx_ref, mixed_ref, proj_ref, bl_ref, t_ref, u_ref, o_ref, meta_ref, doc_ref, taps_ref, hg_ref, hot_ref,
    w_ref, wb_ref, outp_ref, resid_ref,
    part_ref, gtaps_ref, ghg_ref, gatt_ref, gout_ref, gbeta_ref, layer_ref,
    gatt_acc, gout_acc, gbeta_acc, ga_all, *sems,
):
    step = pl.program_id(0)
    me_g, me = lax.axis_index("g"), lax.axis_index("m")

    def scatter():
        return CubeScatter(OUT_PLAN, me_g, me, outp_ref, *sems[:NS])

    gather = CubeGather(LIGHT, me_g, me, own_ref, ga_all, *sems[NS:])

    @pl.when(step == 0)
    def _():
        greet_cube(me_g, me)
        gather.start()
        gtaps_ref[...] = jnp.zeros_like(gtaps_ref)
        ghg_ref[...] = jnp.zeros_like(ghg_ref)
        gatt_acc[...] = jnp.zeros_like(gatt_acc)
        gout_acc[...] = jnp.zeros_like(gout_acc)
        gbeta_acc[...] = jnp.zeros_like(gbeta_acc)

    gather.host(step)

    @pl.when(step == OUT_STEPS[0])
    def _():
        scatter().start()

    for at, phase in zip(OUT_STEPS[1:], range(3)):
        @pl.when(step == at)
        def _():
            scatter().phase(phase)

    proj = proj_ref[...]
    meta = meta_ref[...]
    doc = meta[:, 0:1]
    masks = [meta[:, o : o + 1] for o in range(1, TAPS)]
    logit = bl_ref[:, 0:1]
    sig = sigmoid(logit)
    live = meta[:, 4:5]
    beta = sig * live
    taps = taps_ref[...]
    convs, sigs, acts = [], [], []
    for i in range(3):
        c = conv_forward(proj[:, i * DK : (i + 1) * DK], taps, i * TAPS, masks)
        s = sigmoid(c)
        convs.append(c)
        sigs.append(s)
        acts.append(c * s)
    uq, rq = unit(acts[0])
    uk, rk = unit(acts[1])
    q, k, v = uq.astype(BF), uk.astype(BF), acts[2].astype(BF)

    ga = chip_rows(ga_all, chip_at(step, me))
    gm = mm(ga, wo_ref[...], 1, 1)
    gout_acc[...] += mm(mixed_ref[...], ga, 0, 0)
    o = o_ref[...]
    gate = proj[:, 3 * DK :]
    sg = sigmoid(gate)
    z = gate * sg
    r_o = lax.rsqrt(jnp.mean(o * o, axis=-1, keepdims=True) + EPS)
    n_o = o * r_o
    gmh = gm * hg_ref[...]
    e = gmh * z
    go = r_o * (e - n_o * jnp.mean(e * n_o, axis=-1, keepdims=True))
    ggate = gmh * n_o * (sg * (1.0 + gate * (1.0 - sg)))
    ghg_ref[0:1] += jnp.sum(gm * n_o * z, axis=0, keepdims=True)

    row, col = iotas()
    gqs, gks, gvs, gbs = [], [], [], []
    for i, (dc, q_, k_, v_, bt, go_) in enumerate(zip(subs(doc), subs(q), subs(k), subs(v), subs(beta), subs(go))):
        at = pl.ds(i * SUB, SUB)
        same = dc == doc_ref[i]
        strict = same & (row > col)
        causal = same & (row >= col)
        kk = mm(k_, k_, 1, 1)
        p = jnp.where(causal, mm(q_, k_, 1, 1), 0.0)
        us = split(u_ref[at, :])
        gos = split(go_)
        dp = split(jnp.where(causal, mm3(gos, us, 1, 1), 0.0))
        du = mm3(split(p), gos, 0, 0)
        dw = mm3(split(t_ref[at, :]), split(du), 0, 0)
        da = jnp.where(strict, -mm3(split(dw), us, 1, 1), 0.0)
        dkk = split(bt * da)
        gqs.append(mm3(dp, (k_, None), 1, 0))
        gks.append(mm3(dp, (q_, None), 0, 0) + mm3(dkk, (k_, None), 1, 0) + mm3(dkk, (k_, None), 0, 0))
        gvs.append(bt * dw)
        gbs.append(
            jnp.sum(dw * v_.astype(F32), axis=-1, keepdims=True) + jnp.sum(da * kk, axis=-1, keepdims=True)
        )
    gq, gk, gv, gbeta = (jnp.concatenate(parts, axis=0) for parts in (gqs, gks, gvs, gbs))
    gbl = gbeta * live * sig * (1.0 - sig)
    gb = (gbl * hot_ref[...]).astype(BF)

    gacts = [
        (gq - uq * jnp.sum(uq * gq, axis=-1, keepdims=True)) * rq,
        (gk - uk * jnp.sum(uk * gk, axis=-1, keepdims=True)) * rk,
        gv,
    ]
    grads = []
    for i in range(3):
        x = proj[:, i * DK : (i + 1) * DK]
        gc = gacts[i] * (sigs[i] * (1.0 + convs[i] * (1.0 - sigs[i])))
        base = i * TAPS
        gx = gc * taps[base + TAPS - 1 : base + TAPS]
        j = base + TAPS - 1
        gtaps_ref[j : j + 1] += jnp.sum(gc * x, axis=0, keepdims=True)
        for off in range(1, TAPS):
            gco = gc * masks[off - 1]
            j = base + TAPS - 1 - off
            gtaps_ref[j : j + 1] += jnp.sum(gco * pltpu.roll(x, off, 0), axis=0, keepdims=True)
            gx = gx + pltpu.roll(gco, CHUNK - off, 0) * taps[j : j + 1]
        grads.append(gx.astype(BF))
    gproj = jnp.concatenate(grads + [ggate.astype(BF)], axis=1)
    part = mm(gproj, w_ref[...], 1, 1) + mm(gb, wb_ref[...], 1, 1)
    part_ref[...] = part.astype(BF)
    nx = nx_ref[...]
    gatt_acc[...] += mm(nx, gproj, 0, 0)
    gbeta_acc[...] += mm(gb, nx, 0, 0)

    @pl.when(step == pl.num_programs(0) - 1)
    def _():
        gatt_ref[...] = gatt_acc[...].astype(BF)
        gout_ref[...] = gout_acc[...].astype(BF)
        gbeta_ref[...] = jnp.broadcast_to(jnp.sum(gbeta_acc[...], axis=0, keepdims=True), gbeta_ref.shape)
        done = scatter()
        done.phase(3, lambda j, at, size, got: layer_out_store(layer_ref, resid_ref, at, size, got))
        done.finish()
        gather.sent()


def chip_rows(ref, chip):
    return jnp.concatenate([ref[2 * chip], ref[2 * chip + 1]], axis=0)


def layer_out_store(layer_ref, resid_ref, at, size, got):
    layer_ref[:, at : at + size] = (resid_ref[:, at : at + size] + got).astype(BF)


def mlp_kernel(
    groups, f, ffp, own_ref, cot_ref, w_ref, wd_ref, resid_ref, mid_ref, grad_ref,
    out_ref, gw_ref, gd_ref, gw_away, gd_away, gresid_ref, ggain_ref, ga_ref, gw_acc, gd_acc, nm_all, part_ref, *sems,
):
    step = pl.program_id(0)
    me_g, me = lax.axis_index("g"), lax.axis_index("m")
    gather = CubeGather(TURNED, me_g, me, own_ref, nm_all, *sems[:NG])
    scatter = CubeScatter(STREAM, me_g, me, part_ref, None, *sems[NG:])

    @pl.when(step == 0)
    def _():
        greet_cube(me_g, me)
        gather.start()
        gw_acc[...] = jnp.zeros_like(gw_acc)
        gd_acc[...] = jnp.zeros_like(gd_acc)

    gather.host(step)
    scatter.host(step, CHIPS, NEAR_LATE)
    chip = chip_at(step, me)
    nm = chip_rows(nm_all, chip)
    cot, w, wd = cot_ref[...], w_ref[...], wd_ref[...]
    act = mm(nm, w, 1, 0)
    gate, up = act[:, :ffp], act[:, ffp:]
    s = sigmoid(gate)
    z = gate * s
    hidden = (z * up).astype(BF)
    out_ref[...] = mm(hidden, wd, 1, 0).astype(BF)
    gh = mm(cot, wd, 1, 1)
    gg = (gh * up * (s * (1.0 + gate * (1.0 - s)))).astype(BF)
    gu = (gh * z).astype(BF)
    g = jnp.concatenate([gg, gu], axis=1)
    part = mm(g, w, 1, 1).astype(BF)
    part_ref[2 * chip] = part[:SUB]
    part_ref[2 * chip + 1] = part[SUB:]
    scatter.made(step, CHIPS)

    @pl.when(step == pl.num_programs(0) - 1)
    def _():
        scatter.last(CHIPS[7], ())

    gw_acc[...] += mm(nm, g, 0, 0)
    gd_acc[...] += mm(hidden, cot, 0, 0)

    @pl.when(step == pl.num_programs(0) - 1)
    def _():
        scatter.late(1, 10)
        scatter.late(1, 12)
        size = gw_ref.shape[0]
        gw_ref[...] = gw_acc[pl.ds(pl.multiple_of(me_g * size, 8), size), :].astype(BF)
        for k in range(1, groups):
            g = lax.rem(me_g + k, groups)
            gw_away[k - 1] = gw_acc[pl.ds(pl.multiple_of(g * size, 8), size), :].astype(BF)
        for g in range(groups):
            @pl.when(me_g == g)
            def _():
                gd_ref[...] = gd_acc[g * f : (g + 1) * f].astype(BF)
                for k in range(1, groups):
                    away = (g + k) % groups
                    gd_away[k - 1] = gd_acc[away * f : (away + 1) * f].astype(BF)
        scatter.late(2, 8)

        def store(j, at, size, got):
            gresid_ref[:, at : at + size] = got

        scatter.phase(3, store)
        back, gsum = norm_backward(gresid_ref[...], resid_ref[...], mid_ref[...])
        grad = grad_ref[...].astype(F32) + back
        gresid_ref[...] = grad
        ggain_ref[...] = jnp.broadcast_to(gsum, ggain_ref.shape)
        ga_ref[...] = grad.astype(BF)
        scatter.finish()
        gather.sent()


def rows(width):
    return pl.BlockSpec((CHUNK, width), lambda i: (i, 0))


def whole(shape):
    return pl.BlockSpec(shape, lambda i: (0,) * len(shape))


DOCROW = pl.BlockSpec((CHUNK // SUB, 1, SUB), lambda i: (i, 0, 0))


def chip_block(width):
    return pl.BlockSpec((CHUNK, width), lambda i: (chip_at(i, lax.axis_index("m")), 0))


def chip_docrow():
    return pl.BlockSpec((CHUNK // SUB, 1, SUB), lambda i: (chip_at(i, lax.axis_index("m")), 0, 0))


def far_block(width):
    return pl.BlockSpec((CHUNK, width), lambda i: (chip_at(i, lax.axis_index("m"), FAR), 0))


def far_docrow():
    return pl.BlockSpec((CHUNK // SUB, 1, SUB), lambda i: (chip_at(i, lax.axis_index("m"), FAR), 0, 0))


def att_forward(members, tok, gain, w, wb, taps, hg, hot, wo, meta, docs, cot, flat, mid):
    count, width = tok.shape
    own = flat.shape[0]
    shape = jax.ShapeDtypeStruct
    rows = far_block
    return pl.pallas_call(
        att_fwd_kernel,
        grid=(count // CHUNK,),
        in_specs=[
            rows(width), whole((1, width)), whole(w.shape), whole(wb.shape), whole(taps.shape), whole((1, DK)),
            whole((1, DK)), whole(wo.shape), rows(DK), far_docrow(), ANY, VM, VM,
        ],
        out_specs=[
            rows(width), rows(4 * DK), rows(DK), rows(SUB), rows(DK), rows(DK), rows(DK), whole((own, width)),
            whole((own, width)), ANY,
        ],
        out_shape=[
            shape((count, width), BF), shape((count, 4 * DK), F32), shape((count, DK), F32), shape((count, SUB), F32),
            shape((count, DK), F32), shape((count, DK), F32), shape((count, DK), BF), shape((own, width), F32),
            shape((own, width), BF), shape((members,) + cot.shape, BF),
        ],
        scratch_shapes=[pltpu.VMEM((members, own, width), BF)] + GATHER_SEMS + scatter_scratch(own, width)[1:],
        compiler_params=pltpu.CompilerParams(collective_id=5, has_side_effects=True, vmem_limit_bytes=VMEM_LIMIT),
        name="att_fwd",
    )(tok, gain, w, wb, taps, hg, hot, wo, meta, docs, cot, flat, mid)


def att_backward(members, ga, wo, nx, mixed, proj, bl, t, u, o, meta, docs, taps, hg, hot, w, wb, outp, resid):
    count, width = nx.shape
    own = resid.shape[0]
    shape = jax.ShapeDtypeStruct
    rows = chip_block
    return pl.pallas_call(
        att_bwd_kernel,
        grid=(count // CHUNK,),
        in_specs=[
            VM, whole(wo.shape), rows(width), rows(DK), rows(4 * DK), rows(DK), rows(SUB), rows(DK), rows(DK),
            rows(DK), chip_docrow(), whole(taps.shape), whole((1, DK)), whole((1, DK)), whole(w.shape), whole(wb.shape), ANY,
            VM,
        ],
        out_specs=[
            rows(width), whole((16, DK)), whole((8, DK)), whole((width, 4 * DK)), whole((DK, width)), whole((8, width)),
            whole((own, width)),
        ],
        out_shape=[
            shape((count, width), BF), shape((16, DK), F32), shape((8, DK), F32), shape((width, 4 * DK), BF),
            shape((DK, width), BF), shape((8, width), F32), shape((own, width), BF),
        ],
        scratch_shapes=[
            pltpu.VMEM((width, 4 * DK), F32), pltpu.VMEM((DK, width), F32), pltpu.VMEM((DK, width), F32),
            pltpu.VMEM((members,) + ga.shape, BF),
        ] + scatter_scratch(own, width) + GATHER_SEMS,
        compiler_params=pltpu.CompilerParams(collective_id=6, has_side_effects=True, vmem_limit_bytes=VMEM_LIMIT),
        name="att_bwd",
    )(ga, wo, nx, mixed, proj, bl, t, u, o, meta, docs, taps, hg, hot, w, wb, outp, resid)


def once(shape):
    return pl.BlockSpec(shape, lambda i: (0,) * len(shape), pipeline_mode=pl.Buffered(1))


def mlp(groups, members, f, nm, cot, w, wd, resid, mid, grad_out):
    count, width = cot.shape
    ffp = wd.shape[0]
    own = nm.shape[0]
    shape = jax.ShapeDtypeStruct
    mine, down = (width // groups, 2 * ffp), (f, width)
    away = [(groups - 1,) + mine, (groups - 1,) + down]
    outs = [(mine, BF), (down, BF), (away[0], BF), (away[1], BF), ((own, width), F32), ((8, width), F32), ((own, width), BF)]
    return pl.pallas_call(
        functools.partial(mlp_kernel, groups, f, ffp),
        grid=(count // CHUNK,),
        in_specs=[
            once(nm.shape), chip_block(width), once(w.shape), once(wd.shape), once(resid.shape), once(mid.shape),
            once(grad_out.shape),
        ],
        out_specs=[chip_block(width)] + [once(o) for o, _ in outs],
        out_shape=[shape((count, width), BF)] + [shape(o, t) for o, t in outs],
        scratch_shapes=[
            pltpu.VMEM(w.shape, F32), pltpu.VMEM(wd.shape, F32), pltpu.VMEM((members,) + nm.shape, BF),
            pltpu.VMEM((members,) + nm.shape, BF),
        ] + GATHER_SEMS + scatter_scratch(own, width)[1:],
        compiler_params=pltpu.CompilerParams(collective_id=7, has_side_effects=True, vmem_limit_bytes=VMEM_LIMIT),
        name="mlp",
    )(nm, cot, w, wd, resid, mid, grad_out)


MESH = pl.DeviceIdType.MESH
CORE = 1
BITS = (2, 4, 8)
TURNED = (((0, 640, (2, 4, 8)), (640, 640, (4, 8, 2)), (1280, 768, (8, 2, 4))),)
LIGHT = tuple(
    tuple((b * 1024 + i * 512, 512, ((8, 2, 4), (8, 4, 2))[i]) for i in range(2)) for b in range(2)
)
STREAM = (tuple((i * 512, 512, ((8, 2, 4), (8, 4, 2))[i % 2]) for i in range(4)),)
PARTS = 4
OUT_STEPS = (0, 2, 4, 6)
OUT_PLAN = LIGHT
CUTS = (8, 12)


def flat_plan(plan):
    return tuple(part for batch in plan for part in batch)


ANY = pl.BlockSpec(memory_space=pl.ANY)
VM = pl.BlockSpec(memory_space=pltpu.VMEM)


def flip(me, mask):
    out = me
    bit = 1
    while bit <= mask:
        if mask & bit:
            out = out + bit * (1 - 2 * lax.rem(me // bit, 2))
        bit *= 2
    return out


def greet_cube(me_g, me, groups=1):
    barrier = pltpu.get_barrier_semaphore()
    for bit in (CORE,) + BITS:
        pl.semaphore_signal(barrier, inc=1, device_id=(me_g, flip(me, bit)), device_id_type=MESH)
    for k in range(1, groups):
        pl.semaphore_signal(barrier, inc=1, device_id=(lax.rem(me_g + k, groups), me), device_id_type=MESH)
    pl.semaphore_wait(barrier, len(BITS) + groups)


def greet_members(me_g, me, members):
    barrier = pltpu.get_barrier_semaphore()

    @pl.loop(1, members)
    def _(k):
        pl.semaphore_signal(barrier, inc=1, device_id=(me_g, lax.rem(me + k, members)), device_id_type=MESH)

    pl.semaphore_wait(barrier, members - 1)


def remote(src, dst, send, recv, g, m):
    return pltpu.make_async_remote_copy(
        src_ref=src, dst_ref=dst, send_sem=send, recv_sem=recv, device_id=(g, m), device_id_type=MESH
    )


CHIPS = (0, 2, 4, 8, 6, 10, 12, 14)


def chip_at(step, me, chips=CHIPS):
    out = me // 2
    for bit in BITS:
        hit = sum(jnp.where(step == at, 1, 0) for at, mask in enumerate(chips) if mask & bit)
        half = bit // 2
        out = out + hit * half * (1 - 2 * lax.rem(out // half, 2))
    return out


class CubeGather:
    def __init__(self, plan, me_g, me, block, out, local, link_send, link_recv, core_send, core_recv):
        plan = flat_plan(plan)
        self.plan, self.me_g, self.me, self.block, self.out = plan, me_g, me, block, out
        self.local, self.ls, self.lr, self.cs, self.cr = local, link_send, link_recv, core_send, core_recv
        self.parts = range(len(plan))

    def view(self, slot, j):
        at, size, _ = self.plan[j]
        return self.out.at[slot, :, pl.ds(at, size)]

    def source(self, mask, j):
        at, size, _ = self.plan[j]
        return self.block.at[:, pl.ds(at, size)] if mask == 0 else self.view(flip(self.me, mask), j)

    def masks(self, j, step):
        held = [0]
        for bit in self.plan[j][2][:step]:
            held = held + [h + bit for h in held]
        return held

    def hop(self, mask, j, step):
        i = (1 << step) - 1 + self.masks(j, step).index(mask)
        return remote(
            self.source(mask, j), self.view(flip(self.me, mask), j), self.ls.at[j, i], self.lr.at[j, i], self.me_g,
            flip(self.me, self.plan[j][2][step]),
        )

    def core(self, mask, j):
        i = mask // 2
        return remote(
            self.source(mask, j), self.view(flip(self.me, mask), j), self.cs.at[j, i], self.cr.at[j, i], self.me_g,
            flip(self.me, CORE),
        )

    def own(self):
        return pltpu.make_async_copy(self.block, self.out.at[self.me], self.local)

    def start(self):
        for step in range(3):
            for j in self.parts:
                self.hop(0, j, step).start()
        for j in self.parts:
            self.core(0, j).start()
        self.own().start()

    def arrival(self, mask, j, step):
        i = (1 << step) - 1 + self.masks(j, step).index(mask)
        bit = self.plan[j][2][step]
        view = self.view(flip(self.me, mask + bit), j)
        return remote(view, view, self.ls.at[j, i], self.lr.at[j, i], self.me_g, flip(self.me, bit))

    def advance(self, step):
        for count in range(1 << step):
            for j in self.parts:
                mask = self.masks(j, step)[count]
                self.arrival(mask, j, step).wait_recv()
                got = mask + self.plan[j][2][step]
                for later in range(step + 1, 3):
                    self.hop(got, j, later).start()
                self.core(got, j).start()

    def take(self, got):
        for j in self.parts:
            order = self.plan[j][2]
            step = max(i for i in range(3) if order[i] & got)
            self.arrival(got - order[step], j, step).wait_recv()
            for later in range(step + 1, 3):
                self.hop(got, j, later).start()
            self.core(got, j).start()

    def take_core(self, mask):
        for j in self.parts:
            view = self.view(flip(self.me, mask + CORE), j)
            remote(
                view, view, self.cs.at[j, mask // 2], self.cr.at[j, mask // 2], self.me_g, flip(self.me, CORE)
            ).wait_recv()

    def sent(self):
        for j in self.parts:
            for step in range(3):
                for mask in self.masks(j, step):
                    self.hop(mask, j, step).wait_send()
            for mask in range(0, 16, 2):
                self.core(mask, j).wait_send()

    def host(self, step):
        for at, masks in ((1, (2, 4, 8)), (3, (6, 10, 12)), (5, (14,))):
            @pl.when(step == at)
            def _():
                for mask in masks:
                    self.take(mask)

        for at, mask in enumerate(CHIPS):
            @pl.when(step == at)
            def _():
                if mask == 0:
                    self.own().wait()
                self.take_core(mask)

    def finish(self):
        for mask in range(0, 16, 2):
            for j in self.parts:
                view = self.view(flip(self.me, mask + CORE), j)
                remote(
                    view, view, self.cs.at[j, mask // 2], self.cr.at[j, mask // 2], self.me_g, flip(self.me, CORE)
                ).wait_recv()
        for j in self.parts:
            for step in range(3):
                for mask in self.masks(j, step):
                    self.hop(mask, j, step).wait_send()
            for mask in range(0, 16, 2):
                self.core(mask, j).wait_send()
        self.own().wait()


GATHER_SEMS = [
    pltpu.SemaphoreType.DMA(()), pltpu.SemaphoreType.DMA((PARTS, 7)), pltpu.SemaphoreType.DMA((PARTS, 7)),
    pltpu.SemaphoreType.DMA((PARTS, 8)), pltpu.SemaphoreType.DMA((PARTS, 8)),
]


FAR = (14, 12, 10, 6, 4, 2, 8, 0)
LATE = {4: ((1, 10), (1, 12)), 6: ((1, 4),), 7: ((1, 2), (2, 8))}
NEAR_LATE = {7: ((1, 2), (1, 4))}


class CubeScatter:
    def __init__(self, plan, me_g, me, part, mine, other, sums, got, local, core_send, core_recv, link_send, link_recv):
        self.batches = plan
        self.plan = flat_plan(plan)
        self.me_g, self.me, self.part, self.mine, self.other = me_g, me, part, mine, other
        self.sums, self.got, self.local = sums, got, local
        self.cs, self.cr, self.ls, self.lr = core_send, core_recv, link_send, link_recv
        self.parts = range(len(self.plan))

    def order(self, j):
        return self.plan[j][2][::-1]

    ORDER = (14, 6, 10, 12, 2, 4, 8, 0)

    def core_copy(self, b, mask):
        i = mask // 2
        first = self.batches[b][0][0]
        columns = pl.ds(first, sum(part[1] for part in self.batches[b]))
        return remote(
            self.part.at[flip(self.me, mask + CORE), :, columns], self.other.at[i, :, columns], self.cs.at[b, i],
            self.cr.at[b, i], self.me_g, flip(self.me, CORE),
        )

    def load_copy(self, mask):
        i = mask // 2
        return pltpu.make_async_copy(self.part.at[flip(self.me, mask)], self.mine.at[i], self.local.at[i])

    def masks(self, j, step):
        b = self.order(j)
        rest = [0]
        for bit in b[step + 1 :]:
            rest = rest + [h + bit for h in rest]
        return [b[step] + h for h in rest]

    def slot(self, j, step, mask):
        return (0, 4, 6)[step] + self.masks(j, step).index(mask)

    def copy(self, j, step, mask):
        bit = self.order(j)[step]
        i = self.slot(j, step, mask)
        at, size, _ = self.plan[j]
        return remote(
            self.sums.at[i, :, pl.ds(at, size)], self.got.at[i, :, pl.ds(at, size)], self.ls.at[j, i], self.lr.at[j, i],
            self.me_g, flip(self.me, bit),
        )

    def total(self, j, mask, steps):
        at, size, _ = self.plan[j]
        i = mask // 2
        if self.mine is None:
            x = self.part[flip(self.me, mask), :, at : at + size].astype(F32)
        else:
            x = self.mine[i, :, at : at + size].astype(F32)
        x = x + self.other[i, :, at : at + size].astype(F32)
        for step in range(steps):
            k = self.slot(j, step, mask + self.order(j)[step])
            x = x + self.got[k, :, at : at + size].astype(F32)
        return x

    def send(self, j, step, mask):
        at, size, _ = self.plan[j]
        self.sums[self.slot(j, step, mask), :, at : at + size] = self.total(j, mask, step).astype(BF)
        self.copy(j, step, mask).start()

    def start(self):
        for b in range(len(self.batches)):
            for mask in self.ORDER:
                self.core_copy(b, mask).start()
                if b == 0:
                    self.load_copy(mask).start()

    def phase(self, number, store=None):
        if number == 0:
            at = 0
            for b, batch in enumerate(self.batches):
                for mask in self.ORDER:
                    self.core_copy(b, mask).wait_recv()
                    if b == 0:
                        self.load_copy(mask).wait()
                    for j in range(at, at + len(batch)):
                        if mask in self.masks(j, 0):
                            self.send(j, 0, mask)
                at += len(batch)
        elif number < 3:
            for j in self.parts:
                bits = self.order(j)
                for mask in self.masks(j, number):
                    for earlier in range(number):
                        self.copy(j, earlier, mask + bits[earlier]).wait_recv()
                    self.send(j, number, mask)
        else:
            for j in self.parts:
                at, size, _ = self.plan[j]
                for step in range(3):
                    self.copy(j, step, self.order(j)[step]).wait_recv()
                store(j, at, size, self.total(j, 0, 3))

    def late(self, step, mask):
        for j in self.parts:
            if mask in self.masks(j, step):
                for earlier in range(step):
                    self.copy(j, earlier, mask + self.order(j)[earlier]).wait_recv()
                self.send(j, step, mask)

    def host(self, step, order, others):
        for at in range(1, 8):
            @pl.when(step == at)
            def _():
                mask = order[at - 1]
                self.core_copy(0, mask).wait_recv()
                for j in self.parts:
                    if mask in self.masks(j, 0):
                        self.send(j, 0, mask)
                for late, mask in others.get(at, ()):
                    self.late(late, mask)

    def made(self, step, order):
        for at in range(8):
            @pl.when(step == at)
            def _():
                self.core_copy(0, order[at]).start()

    def last(self, mask, others):
        self.core_copy(0, mask).wait_recv()
        for j in self.parts:
            if mask in self.masks(j, 0):
                self.send(j, 0, mask)
        for late, mask in others:
            self.late(late, mask)

    def run(self, out):
        def store(j, at, size, got):
            out[:, at : at + size] = got

        for number in range(4):
            self.phase(number, store)

    def finish(self):
        for b in range(len(self.batches)):
            for mask in self.ORDER:
                self.core_copy(b, mask).wait_send()
        for j in self.parts:
            for step in range(3):
                for mask in self.masks(j, step):
                    self.copy(j, step, mask).wait_send()


def scatter_scratch(rows, width):
    dma = pltpu.SemaphoreType.DMA
    return [
        pltpu.VMEM((8, rows, width), BF), pltpu.VMEM((8, rows, width), BF), pltpu.VMEM((7, rows, width), BF),
        pltpu.VMEM((7, rows, width), BF), dma((8,)), dma((2, 8)), dma((2, 8)), dma((PARTS, 7)), dma((PARTS, 7)),
    ]


NS = 9
NG = len(GATHER_SEMS)


def norm_backward(grad, x, gain):
    r = lax.rsqrt(jnp.mean(x * x, axis=-1, keepdims=True) + EPS)
    n = x * r
    e = grad * gain
    return r * (e - n * jnp.mean(e * n, axis=-1, keepdims=True)), jnp.sum(grad * n, axis=0, keepdims=True)


class Spread:
    def __init__(self, groups, members, me_g, me):
        self.groups, self.members = groups, members
        self.count = groups * members
        self.me_d = me_g * members + me

    def peer(self, k):
        d = lax.rem(self.me_d + k, self.count)
        return d, d // self.members, lax.rem(d, self.members)

    def back(self, k):
        return lax.rem(self.me_d + self.count - k, self.count)

    def greet(self):
        barrier = pltpu.get_barrier_semaphore()

        @pl.loop(1, self.count)
        def _(k):
            _, g, m = self.peer(k)
            pl.semaphore_signal(barrier, inc=1, device_id=(g, m), device_id_type=MESH)

        pl.semaphore_wait(barrier, self.count - 1)


def head_of(m, rho, srange):
    return (m % rho) * srange + m // rho


def ff_block(w, groups, members, m, f, ffp):
    lane = lax.broadcasted_iota(jnp.int32, (w.shape[0], ffp), 1)
    out = jnp.zeros((w.shape[0], ffp), F32)
    for g in range(groups):
        at, to = (g * members + m) * f, g * f
        first = min(at // DK * DK, w.shape[1] - ffp)
        x = pltpu.roll(w[:, first : first + ffp].astype(F32), (to - (at - first)) % ffp, 1)
        out = jnp.where((lane >= to) & (lane < to + f), x, out)
    return out.astype(BF)


def one_hot(rows, lanes, shift=0):
    row = lax.broadcasted_iota(jnp.int32, (rows, lanes), 0)
    lane = lax.broadcasted_iota(jnp.int32, (rows, lanes), 1)
    return (row + shift == lane).astype(BF)


PACK = 32


def make_pack(chan, docs):
    body = chan.astype(F32)
    row = lax.broadcasted_iota(jnp.int32, (8, DK), 0)
    lane = lax.broadcasted_iota(jnp.int32, (8, DK), 1)
    flags = jnp.where(lane == 0, 1, docs).astype(BF)
    src = lax.broadcasted_iota(jnp.int32, (DK, DK), 0)
    dst = lax.broadcasted_iota(jnp.int32, (DK, DK), 1) - SEQ
    count = mm(flags, ((src <= dst) & (src < SEQ)).astype(BF), 1, 0) - 1.0
    live = jnp.where(lane - SEQ < docs, 1.0, 0.0)
    upper = jnp.where(lane < SEQ, 0.0, jnp.where(row < 2, count, jnp.where(row < 4, live, 0.0)))
    return jnp.concatenate([body[:8] + upper, body[8:]], axis=0).astype(BF)


def read_packs(
    groups, members, rho, r, hgr, me_g, me, packs, gain_in, gain_mid, hg, wb, taps, meta, docs, rows_in, rows_mid, rows_hg
):
    n = groups * members
    lane1 = lax.broadcasted_iota(jnp.int32, (1, DK), 1)
    back = one_hot(PACK, DK)
    back = jnp.where(lax.broadcasted_iota(jnp.int32, (PACK, DK), 0) < members, back, jnp.zeros_like(back))

    @pl.loop(0, n)
    def _(d):
        p = packs[d]
        wb[pl.ds(pl.multiple_of(d * r, r), r), :] = mm(p, back, 0, 0)[:r].astype(BF)
        x = p.astype(F32)
        rows_in[pl.ds(d, 1), :] = x[28:29]
        rows_mid[pl.ds(d, 1), :] = x[29:30]
        rows_hg[pl.ds(d, 1), :] = x[30:31]

    per = DK // r
    for out, src in ((gain_in, rows_in), (gain_mid, rows_mid)):
        for i in range(n // per):
            tile = src[i * per : i * per + 1]
            for j in range(1, per):
                tile = tile + pltpu.roll(src[i * per + j : i * per + j + 1], j * r, 1)
            out[:, i * DK : (i + 1) * DK] = tile
    src = lax.broadcasted_iota(jnp.int32, (DK, DK), 0)
    dst = lax.broadcasted_iota(jnp.int32, (DK, DK), 1)
    spread = ((src < hgr) & (src == lax.rem(dst, hgr))).astype(BF)
    every = mm(rows_hg[...].astype(BF), spread, 1, 0)
    drow = lax.broadcasted_iota(jnp.int32, (n, DK), 0)
    dlane = lax.broadcasted_iota(jnp.int32, (n, DK), 1)
    hg[...] = jnp.sum(jnp.where(dlane // hgr == drow, every, 0.0), axis=0, keepdims=True)

    lane16 = lax.broadcasted_iota(jnp.int32, (16, DK), 1)
    total = jnp.zeros((16, DK), F32)
    for i in range(rho):
        d = lax.rem(me, rho) * members + (me // rho) * rho + i
        x = jnp.where(lane16 < r, packs[d].astype(F32)[16:32], 0.0)
        total = total + (pltpu.roll(x, i * r, 1) if i else x)
    taps[...] = total

    to_rows = one_hot(8, DK)
    row128 = lax.broadcasted_iota(jnp.int32, (SUB, DK), 0)
    lane128 = lax.broadcasted_iota(jnp.int32, (SUB, DK), 1)

    @pl.loop(0, members)
    def _(j):
        x = packs[me_g * members + j].astype(F32)[:8]
        turned = pltpu.roll(x, SEQ, 1)
        doc = jnp.where(lane1 < SEQ, turned[0:1], x[1:2])
        live = jnp.where(lane1 < SEQ, turned[2:3], x[3:4])
        lines = [doc]
        for o in range(1, TAPS):
            keep = (lax.rem(lane1, SEQ) >= o) & (pltpu.roll(doc, o, 1) == doc)
            lines.append(jnp.where(keep, 1.0, 0.0))
        lines += [live, jnp.zeros((3, DK), F32)]
        lines = jnp.concatenate(lines, axis=0).astype(BF)
        first = (2 * SEQ * j).astype(F32)
        docs[j] = doc + first + jnp.where(lane1 < SEQ, 0.0, float(SEQ))
        block = mm(lines, to_rows, 0, 0)
        shift = first + jnp.where(row128 < SEQ, 0.0, float(SEQ))
        meta[pl.ds(pl.multiple_of(j * SUB, SUB), SUB), :] = block + jnp.where(lane128 == 0, shift, 0.0)


def head_of(m, rho, srange):
    return (m % rho) * srange + m // rho


def start_kernel(
    groups, members, rho, hgr, tok, wq, wk, wv, wg, w_gate, w_up, wo, wd, chan, starts,
    tok_all, w_att, w_out, ff_half, down_all, gain_in, gain_mid, hg, wb, taps, meta, docs,
    att, ff, pack, packs, rows_in, rows_mid, rows_hg, sa, ra, sx, rx, sp, rp, sf, rf, so, ro, sd, rd, loc, *sems,
):
    me_g, me = lax.axis_index("g"), lax.axis_index("m")
    spread = Spread(groups, members, me_g, me)
    me_d = spread.me_d
    r = wq.shape[0]
    f = w_gate.shape[1] // spread.count
    ffp = ff.shape[2] // 2
    spread.greet()
    gather = CubeGather(LIGHT, me_g, me, tok, tok_all, *sems)
    for m in range(members):
        h = head_of(m, rho, members // rho) * DK
        for i, w in enumerate((wq, wk, wv, wg)):
            att[m, :, i * DK : (i + 1) * DK] = w[:, h : h + DK]

    def att_copy(k):
        m = lax.rem(me + k, members)
        return remote(att.at[m], w_att.at[me_d], sa.at[k], ra.at[k], me_g, m)

    def att_far(k, step):
        d = me_g * members + lax.rem(me + members - k, members)
        return remote(
            w_att.at[d], w_att.at[d], sx.at[step, k], rx.at[step, k], lax.rem(me_g + step, groups), me
        )

    def att_far_own(step):
        return remote(
            att.at[me], w_att.at[me_d], sx.at[step, 0], rx.at[step, 0], lax.rem(me_g + step, groups), me
        )

    def ff_copy(k):
        m = lax.rem(me + k, members)
        return remote(ff.at[m], ff_half.at[me], sf.at[k], rf.at[k], me_g, m)

    def down_copy(step):
        return remote(wd, down_all.at[me_g], sd.at[step], rd.at[step], lax.rem(me_g + step, groups), me)

    def down_arrival(step):
        src = lax.rem(me_g + groups - step, groups)
        return remote(wd, down_all.at[src], sd.at[step], rd.at[step], me_g, me)

    def pack_copy(k, g, m):
        return remote(pack, packs.at[me_d], sp.at[k], rp.at[k], g, m)

    target = (me // rho) * rho + me_g
    place = lax.rem(me, rho)
    sources = [(lax.rem(me, rho), (me // rho) * rho + i) for i in range(rho)]

    def out_copy(g):
        return remote(wo, w_out.at[place], so.at[g], ro.at[place], g, target)

    for step in range(1, groups):
        att_far_own(step).start()
        down_copy(step).start()

    @pl.loop(1, members)
    def _(k):
        att_copy(k).start()

    gather.start()
    pack[...] = make_pack(chan[...], starts[...])

    @pl.loop(1, spread.count)
    def _(k):
        _, g, m = spread.peer(k)
        pack_copy(k, g, m).start()

    packs[me_d] = pack[...]
    copies = [
        pltpu.make_async_copy(att.at[me], w_att.at[me_d], loc.at[0]),
        pltpu.make_async_copy(wd, down_all.at[me_g], loc.at[1]),
    ]
    for copy in copies:
        copy.start()

    def relay(first, last):
        @pl.loop(first, last)
        def _(k):
            att_copy(k).wait_recv()
            for step in range(1, groups):
                att_far(k, step).start()

    relay(1, members // 2)
    gather.advance(0)
    relay(members // 2, members)
    for g in range(groups):
        @pl.when((me_g != g) | (me != target))
        def _():
            out_copy(g).start()

    @pl.when(me == target)
    def _():
        pltpu.make_async_copy(wo, w_out.at[place], loc.at[2]).start()

    for m in range(members):
        for i, w in enumerate((w_gate, w_up)):
            ff[m, :, i * ffp : (i + 1) * ffp] = ff_block(w, groups, members, m, f, ffp)
    gather.advance(1)

    @pl.loop(1, members)
    def _(k):
        ff_copy(k).start()

    ff_own = pltpu.make_async_copy(ff.at[me], ff_half.at[me], loc.at[3])
    ff_own.start()
    gather.advance(2)

    @pl.loop(1, spread.count)
    def _(k):
        _, g, m = spread.peer(k)
        pack_copy(k, g, m).wait()

    read_packs(
        groups, members, rho, r, hgr, me_g, me, packs, gain_in, gain_mid, hg, wb, taps, meta, docs, rows_in, rows_mid, rows_hg
    )
    gather.finish()

    @pl.loop(1, members)
    def _(k):
        att_copy(k).wait_send()
        ff_copy(k).wait()
        for step in range(1, groups):
            att_far(k, step).wait()

    for step in range(1, groups):
        att_far_own(step).wait()
        down_copy(step).wait_send()
        down_arrival(step).wait_recv()
    for copy in copies:
        copy.wait()
    ff_own.wait()
    for g in range(groups):
        @pl.when((me_g != g) | (me != target))
        def _():
            out_copy(g).wait_send()
    for i in range(rho):
        src_g, src_m = sources[i]
        @pl.when((me_g != src_g) | (me != src_m))
        def _():
            remote(wo, w_out.at[i], so.at[0], ro.at[i], me_g, me).wait_recv()

    @pl.when(me == target)
    def _():
        pltpu.make_async_copy(wo, w_out.at[place], loc.at[2]).wait()


def start_call(groups, members, rho, hgr, ffp, tok, weights, ffw, wo, wd, chan, starts):
    shape = jax.ShapeDtypeStruct
    n = groups * members
    r, width = wo.shape
    count = members * tok.shape[0]
    dma = pltpu.SemaphoreType.DMA
    return pl.pallas_call(
        functools.partial(start_kernel, groups, members, rho, hgr),
        in_specs=[ANY] + [VM] * 6 + [ANY] * 2 + [VM] * 2,
        out_specs=[ANY] * 5 + [VM] * 7,
        out_shape=[
            shape((members,) + tok.shape, BF), shape((n, r, 4 * DK), BF), shape((rho, r, width), BF),
            shape((members, r, 2 * ffp), BF), shape((groups,) + wd.shape, BF), shape((1, width), F32), shape((1, width), F32),
            shape((1, DK), F32), shape((width, DK), BF), shape((16, DK), F32), shape((count, DK), F32),
            shape((count // SUB, 1, SUB), F32),
        ],
        scratch_shapes=[
            pltpu.VMEM((members, r, 4 * DK), BF), pltpu.VMEM((members, r, 2 * ffp), BF), pltpu.VMEM((PACK, DK), BF),
            pltpu.VMEM((n, PACK, DK), BF), pltpu.VMEM((n, DK), F32), pltpu.VMEM((n, DK), F32), pltpu.VMEM((n, DK), F32),
            dma((members,)), dma((members,)), dma((groups, members)),
            dma((groups, members)), dma((n,)), dma((n,)), dma((members,)), dma((members,)), dma((groups,)), dma((rho,)),
            dma((groups,)), dma((groups,)), dma((4,)),
        ] + GATHER_SEMS,
        compiler_params=pltpu.CompilerParams(collective_id=3, has_side_effects=True, vmem_limit_bytes=VMEM_LIMIT),
        name="start",
    )(tok, *weights, *ffw, wo, wd, chan, starts)


def ff_place(out, x, groups, members, m, f, ffp):
    x = x.astype(F32)
    lane = lax.broadcasted_iota(jnp.int32, x.shape, 1)
    for g in range(groups):
        at, to = (g * members + m) * f, g * f
        first = min(at // DK * DK, out.shape[1] - ffp)
        there = at - first
        y = pltpu.roll(x, (there - to) % ffp, 1)
        keep = (lane >= there) & (lane < there + f)
        out[:, first : first + ffp] = jnp.where(keep, y, out[:, first : first + ffp])


def end_kernel(
    groups, members, rho, hgr, part, flat, gain, gmid, gbeta, ghg, gtaps, gatt, gff, gout,
    grad_in, att_in, ff_in, out_in, small_in, tap_in, gain_in,
    total, vec, mine, far, sums, small, tapg, sa, ra, sx, rx, ss, rs, sf, rf, so, ro, st, rt, sg, rg, loc, *sems,
):
    me_g, me = lax.axis_index("g"), lax.axis_index("m")
    spread = Spread(groups, members, me_g, me)
    me_d = spread.me_d
    r = gout.shape[1]
    spread.greet()
    scatter = CubeScatter(LIGHT, me_g, me, part, *sems)

    def att_far(k, step):
        g = lax.rem(me_g + step, groups)
        m = lax.rem(me + k, members)
        return remote(gatt.at[g * members + m], far.at[step - 1, m], sx.at[step - 1, k], rx.at[step - 1, k], g, me)

    def att_copy(k):
        m = lax.rem(me + k, members)
        return remote(sums.at[m], att_in.at[me], sa.at[k], ra.at[k], me_g, m)

    def small_copy(k, d, g, m):
        return remote(small.at[d], small_in.at[me_d], ss.at[k], rs.at[k], g, m)

    def ff_copy(k):
        m = lax.rem(me + k, members)
        return remote(gff.at[m], ff_in.at[me], sf.at[k], rf.at[k], me_g, m)

    def gain_copy(k, d, g, m):
        return remote(vec.at[d * r // DK], gain_in.at[me_d], sg.at[k], rg.at[k], g, m)

    home = lax.rem(me, rho)
    base = (me // rho) * rho

    def out_copy(i):
        return remote(gout.at[i], out_in.at[me_g], so.at[i], ro.at[me_g], home, base + i)

    def tap_copy(i):
        return remote(tapg.at[i], tap_in.at[me_g], st.at[i], rt.at[me_g], home, base + i)

    @pl.loop(0, members)
    def _(k):
        for step in range(1, groups):
            att_far(k, step).start()

    own_rows = pltpu.make_async_copy(gatt.at[pl.ds(me_g * members, members)], mine, loc.at[0])
    own_rows.start()
    scatter.start()
    lane = lax.broadcasted_iota(jnp.int32, (1, DK), 1)
    per = DK // r
    for d in range(spread.count):
        tile = pl.ds(d // per * DK, DK)
        back = (DK - d % per * r) % DK
        lines = [turned(gmid[0:1, tile], back), turned(gbeta[0:1, tile], back)]
        hg_back = (DK - d * hgr % DK) % DK
        small[d] = jnp.concatenate(
            [jnp.where(lane < r, x, 0.0) for x in lines]
            + [jnp.where(lane < hgr, turned(ghg[0:1], hg_back), 0.0), jnp.zeros((5, DK), F32)],
            axis=0,
        )
    lane16 = lax.broadcasted_iota(jnp.int32, (16, DK), 1)
    for i in range(rho):
        tapg[i] = jnp.where(lane16 < r, turned(gtaps[...], (DK - i * r) % DK), 0.0)

    @pl.loop(1, spread.count)
    def _(k):
        d, g, m = spread.peer(k)
        small_copy(k, d, g, m).start()

    copies = [
        pltpu.make_async_copy(small.at[me_d], small_in.at[me_d], loc.at[1]),
        pltpu.make_async_copy(gff.at[me], ff_in.at[me], loc.at[2]),
    ]
    for copy in copies:
        copy.start()
    for i in range(rho):
        @pl.when((me_g != home) | (me != base + i))
        def _():
            out_copy(i).start()
            tap_copy(i).start()

        @pl.when((me_g == home) & (me == base + i))
        def _():
            pltpu.make_async_copy(gout.at[i], out_in.at[me_g], loc.at[3]).start()
            pltpu.make_async_copy(tapg.at[i], tap_in.at[me_g], loc.at[4]).start()

    scatter.phase(0)

    @pl.loop(1, members)
    def _(k):
        ff_copy(k).start()

    def store(j, at, size, got):
        total[:, at : at + size] = got

    own_rows.wait()

    def relay(first, last):
        @pl.loop(first, last)
        def _(k):
            m = lax.rem(me + k, members)
            x = mine[m].astype(F32)
            for step in range(1, groups):
                att_far(k, step).wait_recv()
                x = x + far[step - 1, m].astype(F32)
            sums[m] = x.astype(BF)

            @pl.when(k > 0)
            def _():
                att_copy(k).start()

    relay(0, CUTS[0])
    scatter.phase(1)
    relay(CUTS[0], CUTS[1])
    scatter.phase(2)
    relay(CUTS[1], members)
    scatter.phase(3, store)
    back, gsum = norm_backward(total[...], flat[...].astype(F32), gain[...])
    grad_in[...] = back
    for i in range(vec.shape[0]):
        vec[i] = gsum[:, i * DK : (i + 1) * DK]

    @pl.loop(1, spread.count)
    def _(k):
        d, g, m = spread.peer(k)
        gain_copy(k, d, g, m).start()

    own = pltpu.make_async_copy(vec.at[me_d * r // DK], gain_in.at[me_d], loc.at[5])
    own.start()
    scatter.finish()
    kept = pltpu.make_async_copy(sums.at[me], att_in.at[me], loc.at[6])
    kept.start()

    @pl.loop(1, members)
    def _(k):
        att_copy(k).wait()
        ff_copy(k).wait()

    kept.wait()

    @pl.loop(0, members)
    def _(k):
        for step in range(1, groups):
            att_far(k, step).wait_send()

    @pl.loop(1, spread.count)
    def _(k):
        d, g, m = spread.peer(k)
        small_copy(k, d, g, m).wait()
        gain_copy(k, d, g, m).wait()

    for copy in copies:
        copy.wait()
    own.wait()
    for i in range(rho):
        @pl.when((me_g != home) | (me != base + i))
        def _():
            out_copy(i).wait_send()
            tap_copy(i).wait_send()

        @pl.when((me_g == home) & (me == base + i))
        def _():
            pltpu.make_async_copy(gout.at[i], out_in.at[me_g], loc.at[3]).wait()
            pltpu.make_async_copy(tapg.at[i], tap_in.at[me_g], loc.at[4]).wait()
    holder = base + me_g
    for g in range(groups):
        @pl.when((me_g != g) | (me != holder))
        def _():
            remote(gout.at[0], out_in.at[g], so.at[0], ro.at[g], me_g, me).wait_recv()
            remote(tapg.at[0], tap_in.at[g], st.at[0], rt.at[g], me_g, me).wait_recv()


def turned(x, shift):
    return pltpu.roll(x, shift, 1) if shift else x


def finish_kernel(
    groups, members, rho, grad_in, grad_resid, att_in, ff_in, out_in, small_in, tap_in, gain_in,
    input_grad, gq, gk, gv, gg, g_gate, g_up, g_out, s_in, s_mid, s_hg, g_beta, g_tq, g_tk, g_tv,
):
    me_g, me = lax.axis_index("g"), lax.axis_index("m")
    n = groups * members
    me_d = me_g * members + me
    r = out_in.shape[1]
    ffp = ff_in.shape[2] // 2
    f = g_gate.shape[1] // n
    input_grad[...] = grad_resid[...] + grad_in[...]
    for m in range(members):
        h = head_of(m, rho, members // rho) * DK
        for i, out in enumerate((gq, gk, gv, gg)):
            out[:, h : h + DK] = att_in[m, :, i * DK : (i + 1) * DK].astype(F32)
    for m in range(members):
        for i, out in enumerate((g_gate, g_up)):
            ff_place(out, ff_in[m, :, i * ffp : (i + 1) * ffp], groups, members, m, f, ffp)
    g_out[...] = sum(out_in[g].astype(F32) for g in range(groups))
    taps = sum(tap_in[g] for g in range(groups))
    for i, out in enumerate((g_tq, g_tk, g_tv)):
        out[...] = taps[i * TAPS : (i + 1) * TAPS, :r]
    for m in range(members):
        row = small_in[m, 1:2]
        for g in range(1, groups):
            row = row + small_in[g * members + m, 1:2]
        h = head_of(m, rho, members // rho)
        g_beta[h : h + 1] = row[:, :r]
    acc = jnp.sum(small_in[...], axis=0)
    gsum = jnp.sum(gain_in[...], axis=0)
    own_gain = pltpu.roll(gsum, lax.rem(DK - lax.rem(me_d * r, DK), DK), 1)
    s_in[...] = own_gain[:, :r]
    s_mid[...] = acc[0:1, :r]
    s_hg[...] = acc[2:3, : s_hg.shape[1]]


def finish_call(groups, members, rho, hidden, hgr, heads, args):
    shape = jax.ShapeDtypeStruct
    rows, width = args[0].shape
    r = args[4].shape[1]
    outs = [(rows, width)] + [(r, width)] * 4 + [(r, hidden)] * 2 + [(r, width), (1, r), (1, r), (1, hgr), (heads, r)]
    outs += [(TAPS, r)] * 3
    return pl.pallas_call(
        functools.partial(finish_kernel, groups, members, rho),
        in_specs=[VM] * len(args),
        out_specs=[VM] * len(outs),
        out_shape=[shape(o, F32) for o in outs],
        compiler_params=pltpu.CompilerParams(vmem_limit_bytes=VMEM_LIMIT),
        name="finish",
    )(*args)


def end_call(groups, members, rho, hgr, part, flat, gain, gmid, gbeta, ghg, gtaps, gatt, gff, gout):
    shape = jax.ShapeDtypeStruct
    n = groups * members
    _, rows, width = part.shape
    r = gout.shape[1]
    dma = pltpu.SemaphoreType.DMA
    piece = (r, 4 * DK)
    return pl.pallas_call(
        functools.partial(end_kernel, groups, members, rho, hgr),
        in_specs=[ANY] + [VM] * 6 + [ANY] * 3,
        out_specs=[VM] + [ANY] * 6,
        out_shape=[
            shape((rows, width), F32), shape((members,) + piece, BF), shape(gff.shape, BF),
            shape((groups,) + gout.shape[1:], BF), shape((n, 8, DK), F32), shape((groups, 16, DK), F32),
            shape((n, 1, DK), F32),
        ],
        scratch_shapes=[
            pltpu.VMEM((rows, width), F32), pltpu.VMEM((width // DK, 1, DK), F32), pltpu.VMEM((members,) + piece, BF),
            pltpu.VMEM((groups - 1, members) + piece, BF), pltpu.VMEM((members,) + piece, BF),
            pltpu.VMEM((n, 8, DK), F32), pltpu.VMEM((rho, 16, DK), F32), dma((members,)), dma((members,)),
            dma((groups - 1, members)), dma((groups - 1, members)), dma((n,)), dma((n,)), dma((members,)), dma((members,)),
            dma((rho,)), dma((groups,)), dma((rho,)), dma((groups,)), dma((n,)), dma((n,)), dma((7,)),
        ] + scatter_scratch(rows, width),
        compiler_params=pltpu.CompilerParams(collective_id=4, has_side_effects=True, vmem_limit_bytes=VMEM_LIMIT),
        name="end",
    )(part, flat, gain, gmid, gbeta, ghg, gtaps, gatt, gff, gout)


def exchange_groups(x, groups):
    return [
        lax.ppermute(x[step - 1], "g", [(i, (i + step) % groups) for i in range(groups)]) for step in range(1, groups)
    ]


def make_shards(groups, members):
    def shards(
        tokens, doc_starts, seq_lengths, attn_gain, query_weight, key_weight, value_weight, out_gate_weight, beta_weight,
        query_conv, key_conv, value_conv, head_gain, out_weight, mlp_gain, mlp_gate_weight, mlp_up_weight,
        mlp_down_weight, cotangent,
    ):
        n = groups * members
        width = tokens.shape[-1]
        r = attn_gain.shape[0]
        f = mlp_down_weight.shape[0]
        hgr = head_gain.shape[0]
        heads = beta_weight.shape[1]
        rho = DK // r
        srange = members // rho
        me_g, me_m = lax.axis_index("g"), lax.axis_index("m")
        head = lax.rem(me_m, rho) * srange + me_m // rho
        seqs = tokens.shape[0] * tokens.shape[1]
        seq = tokens.shape[2]
        own = seqs * seq
        flat_bf = tokens.reshape(own, width)
        grad_out = cotangent.reshape(own, width)

        lines = [beta_weight.T, query_conv.T, key_conv.T, value_conv.T, attn_gain[None], mlp_gain[None]]
        lines.append(jnp.pad(head_gain, (0, r - hgr))[None])
        chan = jnp.concatenate(lines, axis=0)
        chan = jnp.pad(chan, ((0, PACK - chan.shape[0]), (0, DK - r)))
        starts = jnp.pad(doc_starts.reshape(seqs, seq), ((0, 0), (0, DK - seq)))
        lengths = jnp.broadcast_to(seq_lengths.reshape(seqs, 1), (seqs, DK))
        starts = jnp.pad(jnp.concatenate([starts, lengths]), ((0, 8 - 2 * seqs), (0, 0)))
        ffw = groups * f
        ffp = -(-ffw // DK) * DK
        hidden_size = mlp_gate_weight.shape[1]
        count = members * own
        tok_all, w_att, w_out, ff_half, w_down, gain_in, gain_mid, hg, beta_full, taps, meta, docs_row = start_call(
            groups, members, rho, hgr, ffp, flat_bf, (query_weight, key_weight, value_weight, out_gate_weight),
            (mlp_gate_weight, mlp_up_weight), out_weight, mlp_down_weight, chan, starts,
        )
        w_ff = lax.all_gather(ff_half, "g", axis=0).reshape(width, 2 * ffp)
        w_att = w_att.reshape(width, 4 * DK)
        w_out = w_out.reshape(DK, width)
        hot = (jnp.arange(DK) == head).astype(F32).reshape(1, DK)

        blocks = (members, own, width)
        w_down = jnp.pad(w_down.reshape(ffw, width), ((0, ffp - ffw), (0, 0)))
        nx, proj, bl, t, u, o, mixed, resid, nm, cot_all = att_forward(
            members, tok_all.reshape(count, width), gain_in, w_att, beta_full, taps, hg, hot, w_out, meta, docs_row, grad_out,
            flat_bf, gain_mid,
        )
        out_part, g_ff, g_down, ff_away, down_away, grad_resid, g_mid_gain, ga = mlp(
            groups, members, f, nm, cot_all.reshape(count, width), w_ff, w_down, resid, gain_mid, grad_out
        )
        ff_came = exchange_groups(ff_away, groups)
        g_down = sum((x.astype(F32) for x in exchange_groups(down_away, groups)), g_down.astype(F32))
        g_ff = sum((x.astype(F32) for x in ff_came), g_ff.astype(F32)).astype(BF).reshape(members, r, 2 * ffp)
        gpart, gtaps, ghg, gatt, gout, g_beta, layer_out = att_backward(
            members, ga, w_out, nx, mixed, proj, bl, t, u, o, meta, docs_row, taps, hg, hot, w_att, beta_full,
            out_part.reshape(blocks), resid,
        )
        gatt = gatt.reshape(n, r, 4 * DK)
        gout = gout.reshape(rho, r, width)
        came = end_call(
            groups, members, rho, hgr, gpart.reshape(blocks), flat_bf, gain_in, g_mid_gain, g_beta, ghg, gtaps, gatt, g_ff,
            gout,
        )
        args = (came[0], grad_resid) + tuple(came[1:])
        input_grad, gq, gk, gv, gg, g_gate, g_up, g_out, s_in, s_mid, s_hg, s_beta, s_q, s_k, s_v = finish_call(
            groups, members, rho, hidden_size, hgr, heads, args
        )
        s_in, s_mid, s_hg = s_in.reshape(r), s_mid.reshape(r), s_hg.reshape(hgr)
        s_beta, s_q, s_k, s_v = s_beta.T, s_q.T, s_k.T, s_v.T
        return (
            layer_out.reshape(tokens.shape), input_grad.reshape(tokens.shape),
            s_in, gq, gk, gv, gg, s_beta, s_q, s_k, s_v, s_hg, g_out, s_mid, g_gate, g_up,
            g_down,
        )

    return shards


def solution(mesh):
    n = mesh.devices.size
    members = 16
    groups = n // members
    inner = Mesh(mesh.devices.reshape(groups, members), ("g", "m"))
    both = ("g", "m")
    acts, mat, vec = P(None, both, None, None), P(both, None), P(both)
    return jax.shard_map(
        make_shards(groups, members),
        mesh=inner,
        in_specs=(acts, P(None, both, None), P(None, both), vec, mat, mat, mat, mat, mat, mat, mat, mat, vec, mat, vec,
                  mat, mat, mat, acts),
        out_specs=(acts, acts, vec, mat, mat, mat, mat, mat, mat, mat, mat, vec, mat, vec, mat, mat, mat),
        check_vma=False,
    )
```

```python
import functools

import jax
import jax.numpy as jnp
from jax import lax
from jax.experimental import pallas as pl
from jax.experimental.pallas import tpu as pltpu
from jax.sharding import Mesh
from jax.sharding import PartitionSpec as P

DK = 128
EPS = 1e-05
L2EPS = 1e-06
CHUNK = 256
SEQ = 64
SUB = 128
TAPS = 4
BF = jnp.bfloat16
F32 = jnp.float32
VMEM_LIMIT = 60 << 20


def mm(a, b, ca, cb):
    return lax.dot_general(a, b, (((ca,), (cb,)), ((), ())), preferred_element_type=F32)


def split(x):
    hi = x.astype(BF)
    return hi, (x - hi.astype(F32)).astype(BF)


def mm3(a, b, ca, cb):
    (ah, al), (bh, bl) = a, b
    out = mm(ah, bh, ca, cb)
    if bl is not None:
        out = out + mm(ah, bl, ca, cb)
    if al is not None:
        out = out + mm(al, bh, ca, cb)
    return out


def sigmoid(x):
    return 1.0 / (1.0 + jnp.exp(-x))


def iotas():
    row = lax.broadcasted_iota(jnp.int32, (SUB, SUB), 0)
    col = lax.broadcasted_iota(jnp.int32, (SUB, SUB), 1)
    return row, col


def unit_lower_inverses(blocks, row, col):
    eye = (row == col).astype(F32)
    pair = (row // 2) == (col // 2)
    xs = [eye - jnp.where(pair, a, 0.0) for a in blocks]
    size = 2
    while size < SEQ:
        keep = ((row // (2 * size)) == (col // (2 * size))) & ((row // size) != (col // size))
        offs = [split(jnp.where(keep, a, 0.0)) for a in blocks]
        parts = [split(x) for x in xs]
        ys = [split(mm3(off, p, 1, 0)) for off, p in zip(offs, parts)]
        xs = [x - mm3(p, y, 1, 0) for x, p, y in zip(xs, parts, ys)]
        size *= 2
    return xs


def conv_forward(x, taps, base, masks):
    out = x * taps[base + TAPS - 1 : base + TAPS]
    for o in range(1, TAPS):
        out = out + pltpu.roll(x, o, 0) * masks[o - 1] * taps[base + TAPS - 1 - o : base + TAPS - o]
    return out


def unit(act):
    r = lax.rsqrt(jnp.sum(act * act, axis=-1, keepdims=True) + L2EPS)
    return act * r, r


def subs(x):
    return [x[i * SUB : (i + 1) * SUB] for i in range(CHUNK // SUB)]


def att_fwd_kernel(
    tok_ref, gain_ref, w_ref, wb_ref, taps_ref, hg_ref, hot_ref, wo_ref, meta_ref, doc_ref, cot_ref, flat_ref, mid_ref,
    nx_ref, proj_ref, bl_ref, t_ref, u_ref, o_ref, mixed_ref, resid_ref, nm_ref, cot_all, part_ref, *sems,
):
    step = pl.program_id(0)
    me_g, me = lax.axis_index("g"), lax.axis_index("m")
    scatter = CubeScatter(STREAM, me_g, me, part_ref, None, *sems[NG:])

    def gather():
        return CubeGather(LIGHT, me_g, me, cot_ref, cot_all, *sems[:NG])

    @pl.when(step == 0)
    def _():
        greet_cube(me_g, me)
        gather().start()

    scatter.host(step, FAR, LATE)

    for at, hop in ((2, 0), (4, 1), (6, 2)):
        @pl.when(step == at)
        def _():
            gather().advance(hop)

    x = tok_ref[...].astype(F32)
    nx = (x * lax.rsqrt(jnp.mean(x * x, axis=-1, keepdims=True) + EPS) * gain_ref[...]).astype(BF)
    nx_ref[...] = nx
    proj = mm(nx, w_ref[...], 1, 0)
    proj_ref[...] = proj
    logits = mm(nx, wb_ref[...], 1, 0)
    logit = jnp.sum(logits * hot_ref[...], axis=-1, keepdims=True)
    bl_ref[...] = jnp.broadcast_to(logit, (CHUNK, DK))
    meta = meta_ref[...]
    doc = meta[:, 0:1]
    masks = [meta[:, o : o + 1] for o in range(1, TAPS)]
    beta = sigmoid(logit) * meta[:, 4:5]
    taps = taps_ref[...]
    acts = []
    for i in range(3):
        c = conv_forward(proj[:, i * DK : (i + 1) * DK], taps, i * TAPS, masks)
        acts.append(c * sigmoid(c))
    qs = subs(unit(acts[0])[0].astype(BF))
    ks = subs(unit(acts[1])[0].astype(BF))
    vs = subs(acts[2].astype(BF))
    betas, docs = subs(beta), subs(doc)
    row, col = iotas()
    sames = [d == doc_ref[i] for i, d in enumerate(docs)]
    blocks = [jnp.where(same & (row > col), bt * mm(k, k, 1, 1), 0.0) for same, bt, k in zip(sames, betas, ks)]
    ts = unit_lower_inverses(blocks, row, col)
    os = []
    for i, (t, bt, v, q, k, same) in enumerate(zip(ts, betas, vs, qs, ks, sames)):
        at = pl.ds(i * SUB, SUB)
        t_ref[at, :] = t
        u = mm3(split(t), split(bt * v.astype(F32)), 1, 0)
        u_ref[at, :] = u
        p = jnp.where(same & (row >= col), mm(q, k, 1, 1), 0.0)
        os.append(mm3(split(p), split(u), 1, 0))
    o = jnp.concatenate(os, axis=0)
    o_ref[...] = o
    gate = proj[:, 3 * DK :]
    n_o = o * lax.rsqrt(jnp.mean(o * o, axis=-1, keepdims=True) + EPS)
    mixed = (n_o * hg_ref[...] * (gate * sigmoid(gate))).astype(BF)
    mixed_ref[...] = mixed
    part = mm(mixed, wo_ref[...], 1, 0).astype(BF)
    chip = chip_at(step, me, FAR)
    part_ref[2 * chip] = part[:SUB]
    part_ref[2 * chip + 1] = part[SUB:]
    scatter.made(step, FAR)

    @pl.when(step == pl.num_programs(0) - 1)
    def _():
        def store(j, at, size, got):
            resid_ref[:, at : at + size] = flat_ref[:, at : at + size].astype(F32) + got

        scatter.last(0, ())
        scatter.phase(3, store)
        resid = resid_ref[...]
        r = lax.rsqrt(jnp.mean(resid * resid, axis=-1, keepdims=True) + EPS)
        nm_ref[...] = (resid * r * mid_ref[...]).astype(BF)
        scatter.finish()
        gather().finish()


def att_bwd_kernel(
    own_ref, wo_ref, nx_ref, mixed_ref, proj_ref, bl_ref, t_ref, u_ref, o_ref, meta_ref, doc_ref, taps_ref, hg_ref, hot_ref,
    w_ref, wb_ref, outp_ref, resid_ref,
    part_ref, gtaps_ref, ghg_ref, gatt_ref, gout_ref, gbeta_ref, layer_ref,
    gatt_acc, gout_acc, gbeta_acc, ga_all, *sems,
):
    step = pl.program_id(0)
    me_g, me = lax.axis_index("g"), lax.axis_index("m")

    def scatter():
        return CubeScatter(OUT_PLAN, me_g, me, outp_ref, *sems[:NS])

    gather = CubeGather(LIGHT, me_g, me, own_ref, ga_all, *sems[NS:])

    @pl.when(step == 0)
    def _():
        greet_cube(me_g, me)
        gather.start()
        gtaps_ref[...] = jnp.zeros_like(gtaps_ref)
        ghg_ref[...] = jnp.zeros_like(ghg_ref)
        gatt_acc[...] = jnp.zeros_like(gatt_acc)
        gout_acc[...] = jnp.zeros_like(gout_acc)
        gbeta_acc[...] = jnp.zeros_like(gbeta_acc)

    gather.host(step)

    @pl.when(step == OUT_STEPS[0])
    def _():
        scatter().start()

    for at, phase in zip(OUT_STEPS[1:], range(3)):
        @pl.when(step == at)
        def _():
            scatter().phase(phase)

    proj = proj_ref[...]
    meta = meta_ref[...]
    doc = meta[:, 0:1]
    masks = [meta[:, o : o + 1] for o in range(1, TAPS)]
    logit = bl_ref[:, 0:1]
    sig = sigmoid(logit)
    live = meta[:, 4:5]
    beta = sig * live
    taps = taps_ref[...]
    convs, sigs, acts = [], [], []
    for i in range(3):
        c = conv_forward(proj[:, i * DK : (i + 1) * DK], taps, i * TAPS, masks)
        s = sigmoid(c)
        convs.append(c)
        sigs.append(s)
        acts.append(c * s)
    uq, rq = unit(acts[0])
    uk, rk = unit(acts[1])
    q, k, v = uq.astype(BF), uk.astype(BF), acts[2].astype(BF)

    ga = chip_rows(ga_all, chip_at(step, me))
    gm = mm(ga, wo_ref[...], 1, 1)
    gout_acc[...] += mm(mixed_ref[...], ga, 0, 0)
    o = o_ref[...]
    gate = proj[:, 3 * DK :]
    sg = sigmoid(gate)
    z = gate * sg
    r_o = lax.rsqrt(jnp.mean(o * o, axis=-1, keepdims=True) + EPS)
    n_o = o * r_o
    gmh = gm * hg_ref[...]
    e = gmh * z
    go = r_o * (e - n_o * jnp.mean(e * n_o, axis=-1, keepdims=True))
    ggate = gmh * n_o * (sg * (1.0 + gate * (1.0 - sg)))
    ghg_ref[0:1] += jnp.sum(gm * n_o * z, axis=0, keepdims=True)

    row, col = iotas()
    gqs, gks, gvs, gbs = [], [], [], []
    for i, (dc, q_, k_, v_, bt, go_) in enumerate(zip(subs(doc), subs(q), subs(k), subs(v), subs(beta), subs(go))):
        at = pl.ds(i * SUB, SUB)
        same = dc == doc_ref[i]
        strict = same & (row > col)
        causal = same & (row >= col)
        kk = mm(k_, k_, 1, 1)
        p = jnp.where(causal, mm(q_, k_, 1, 1), 0.0)
        us = split(u_ref[at, :])
        gos = split(go_)
        dp = split(jnp.where(causal, mm3(gos, us, 1, 1), 0.0))
        du = mm3(split(p), gos, 0, 0)
        dw = mm3(split(t_ref[at, :]), split(du), 0, 0)
        da = jnp.where(strict, -mm3(split(dw), us, 1, 1), 0.0)
        dkk = split(bt * da)
        gqs.append(mm3(dp, (k_, None), 1, 0))
        gks.append(mm3(dp, (q_, None), 0, 0) + mm3(dkk, (k_, None), 1, 0) + mm3(dkk, (k_, None), 0, 0))
        gvs.append(bt * dw)
        gbs.append(
            jnp.sum(dw * v_.astype(F32), axis=-1, keepdims=True) + jnp.sum(da * kk, axis=-1, keepdims=True)
        )
    gq, gk, gv, gbeta = (jnp.concatenate(parts, axis=0) for parts in (gqs, gks, gvs, gbs))
    gbl = gbeta * live * sig * (1.0 - sig)
    gb = (gbl * hot_ref[...]).astype(BF)

    gacts = [
        (gq - uq * jnp.sum(uq * gq, axis=-1, keepdims=True)) * rq,
        (gk - uk * jnp.sum(uk * gk, axis=-1, keepdims=True)) * rk,
        gv,
    ]
    grads = []
    for i in range(3):
        x = proj[:, i * DK : (i + 1) * DK]
        gc = gacts[i] * (sigs[i] * (1.0 + convs[i] * (1.0 - sigs[i])))
        base = i * TAPS
        gx = gc * taps[base + TAPS - 1 : base + TAPS]
        j = base + TAPS - 1
        gtaps_ref[j : j + 1] += jnp.sum(gc * x, axis=0, keepdims=True)
        for off in range(1, TAPS):
            gco = gc * masks[off - 1]
            j = base + TAPS - 1 - off
            gtaps_ref[j : j + 1] += jnp.sum(gco * pltpu.roll(x, off, 0), axis=0, keepdims=True)
            gx = gx + pltpu.roll(gco, CHUNK - off, 0) * taps[j : j + 1]
        grads.append(gx.astype(BF))
    gproj = jnp.concatenate(grads + [ggate.astype(BF)], axis=1)
    part = mm(gproj, w_ref[...], 1, 1) + mm(gb, wb_ref[...], 1, 1)
    part_ref[...] = part.astype(BF)
    nx = nx_ref[...]
    gatt_acc[...] += mm(nx, gproj, 0, 0)
    gbeta_acc[...] += mm(gb, nx, 0, 0)

    @pl.when(step == pl.num_programs(0) - 1)
    def _():
        gatt_ref[...] = gatt_acc[...].astype(BF)
        gout_ref[...] = gout_acc[...].astype(BF)
        gbeta_ref[...] = jnp.broadcast_to(jnp.sum(gbeta_acc[...], axis=0, keepdims=True), gbeta_ref.shape)
        done = scatter()
        done.phase(3, lambda j, at, size, got: layer_out_store(layer_ref, resid_ref, at, size, got))
        done.finish()
        gather.sent()


def chip_rows(ref, chip):
    return jnp.concatenate([ref[2 * chip], ref[2 * chip + 1]], axis=0)


def layer_out_store(layer_ref, resid_ref, at, size, got):
    layer_ref[:, at : at + size] = (resid_ref[:, at : at + size] + got).astype(BF)


def mlp_kernel(
    groups, f, ffp, own_ref, cot_ref, w_ref, wd_ref, resid_ref, mid_ref, grad_ref,
    out_ref, gw_ref, gd_ref, gw_away, gd_away, gresid_ref, ggain_ref, ga_ref, gw_acc, gd_acc, nm_all, part_ref, *sems,
):
    step = pl.program_id(0)
    me_g, me = lax.axis_index("g"), lax.axis_index("m")
    gather = CubeGather(TURNED, me_g, me, own_ref, nm_all, *sems[:NG])
    scatter = CubeScatter(STREAM, me_g, me, part_ref, None, *sems[NG:])

    @pl.when(step == 0)
    def _():
        greet_cube(me_g, me)
        gather.start()
        gw_acc[...] = jnp.zeros_like(gw_acc)
        gd_acc[...] = jnp.zeros_like(gd_acc)

    gather.host(step)
    scatter.host(step, CHIPS, NEAR_LATE)
    chip = chip_at(step, me)
    nm = chip_rows(nm_all, chip)
    cot, w, wd = cot_ref[...], w_ref[...], wd_ref[...]
    act = mm(nm, w, 1, 0)
    gate, up = act[:, :ffp], act[:, ffp:]
    s = sigmoid(gate)
    z = gate * s
    hidden = (z * up).astype(BF)
    out_ref[...] = mm(hidden, wd, 1, 0).astype(BF)
    gh = mm(cot, wd, 1, 1)
    gg = (gh * up * (s * (1.0 + gate * (1.0 - s)))).astype(BF)
    gu = (gh * z).astype(BF)
    g = jnp.concatenate([gg, gu], axis=1)
    part = mm(g, w, 1, 1).astype(BF)
    part_ref[2 * chip] = part[:SUB]
    part_ref[2 * chip + 1] = part[SUB:]
    scatter.made(step, CHIPS)

    @pl.when(step == pl.num_programs(0) - 1)
    def _():
        scatter.last(CHIPS[7], ())

    gw_acc[...] += mm(nm, g, 0, 0)
    gd_acc[...] += mm(hidden, cot, 0, 0)

    @pl.when(step == pl.num_programs(0) - 1)
    def _():
        scatter.late(1, 10)
        scatter.late(1, 12)
        size = gw_ref.shape[0]
        gw_ref[...] = gw_acc[pl.ds(pl.multiple_of(me_g * size, 8), size), :].astype(BF)
        for k in range(1, groups):
            g = lax.rem(me_g + k, groups)
            gw_away[k - 1] = gw_acc[pl.ds(pl.multiple_of(g * size, 8), size), :].astype(BF)
        for g in range(groups):
            @pl.when(me_g == g)
            def _():
                gd_ref[...] = gd_acc[g * f : (g + 1) * f].astype(BF)
                for k in range(1, groups):
                    away = (g + k) % groups
                    gd_away[k - 1] = gd_acc[away * f : (away + 1) * f].astype(BF)
        scatter.late(2, 8)

        def store(j, at, size, got):
            gresid_ref[:, at : at + size] = got

        scatter.phase(3, store)
        back, gsum = norm_backward(gresid_ref[...], resid_ref[...], mid_ref[...])
        grad = grad_ref[...].astype(F32) + back
        gresid_ref[...] = grad
        ggain_ref[...] = jnp.broadcast_to(gsum, ggain_ref.shape)
        ga_ref[...] = grad.astype(BF)
        scatter.finish()
        gather.sent()


def rows(width):
    return pl.BlockSpec((CHUNK, width), lambda i: (i, 0))


def whole(shape):
    return pl.BlockSpec(shape, lambda i: (0,) * len(shape))


DOCROW = pl.BlockSpec((CHUNK // SUB, 1, SUB), lambda i: (i, 0, 0))


def chip_block(width):
    return pl.BlockSpec((CHUNK, width), lambda i: (chip_at(i, lax.axis_index("m")), 0))


def chip_docrow():
    return pl.BlockSpec((CHUNK // SUB, 1, SUB), lambda i: (chip_at(i, lax.axis_index("m")), 0, 0))


def far_block(width):
    return pl.BlockSpec((CHUNK, width), lambda i: (chip_at(i, lax.axis_index("m"), FAR), 0))


def far_docrow():
    return pl.BlockSpec((CHUNK // SUB, 1, SUB), lambda i: (chip_at(i, lax.axis_index("m"), FAR), 0, 0))


def att_forward(members, tok, gain, w, wb, taps, hg, hot, wo, meta, docs, cot, flat, mid):
    count, width = tok.shape
    own = flat.shape[0]
    shape = jax.ShapeDtypeStruct
    rows = far_block
    return pl.pallas_call(
        att_fwd_kernel,
        grid=(count // CHUNK,),
        in_specs=[
            rows(width), whole((1, width)), whole(w.shape), whole(wb.shape), whole(taps.shape), whole((1, DK)),
            whole((1, DK)), whole(wo.shape), rows(DK), far_docrow(), ANY, VM, VM,
        ],
        out_specs=[
            rows(width), rows(4 * DK), rows(DK), rows(SUB), rows(DK), rows(DK), rows(DK), whole((own, width)),
            whole((own, width)), ANY,
        ],
        out_shape=[
            shape((count, width), BF), shape((count, 4 * DK), F32), shape((count, DK), F32), shape((count, SUB), F32),
            shape((count, DK), F32), shape((count, DK), F32), shape((count, DK), BF), shape((own, width), F32),
            shape((own, width), BF), shape((members,) + cot.shape, BF),
        ],
        scratch_shapes=[pltpu.VMEM((members, own, width), BF)] + GATHER_SEMS + scatter_scratch(own, width)[1:],
        compiler_params=pltpu.CompilerParams(collective_id=5, has_side_effects=True, vmem_limit_bytes=VMEM_LIMIT),
        name="att_fwd",
    )(tok, gain, w, wb, taps, hg, hot, wo, meta, docs, cot, flat, mid)


def att_backward(members, ga, wo, nx, mixed, proj, bl, t, u, o, meta, docs, taps, hg, hot, w, wb, outp, resid):
    count, width = nx.shape
    own = resid.shape[0]
    shape = jax.ShapeDtypeStruct
    rows = chip_block
    return pl.pallas_call(
        att_bwd_kernel,
        grid=(count // CHUNK,),
        in_specs=[
            VM, whole(wo.shape), rows(width), rows(DK), rows(4 * DK), rows(DK), rows(SUB), rows(DK), rows(DK),
            rows(DK), chip_docrow(), whole(taps.shape), whole((1, DK)), whole((1, DK)), whole(w.shape), whole(wb.shape), ANY,
            VM,
        ],
        out_specs=[
            rows(width), whole((16, DK)), whole((8, DK)), whole((width, 4 * DK)), whole((DK, width)), whole((8, width)),
            whole((own, width)),
        ],
        out_shape=[
            shape((count, width), BF), shape((16, DK), F32), shape((8, DK), F32), shape((width, 4 * DK), BF),
            shape((DK, width), BF), shape((8, width), F32), shape((own, width), BF),
        ],
        scratch_shapes=[
            pltpu.VMEM((width, 4 * DK), F32), pltpu.VMEM((DK, width), F32), pltpu.VMEM((DK, width), F32),
            pltpu.VMEM((members,) + ga.shape, BF),
        ] + scatter_scratch(own, width) + GATHER_SEMS,
        compiler_params=pltpu.CompilerParams(collective_id=6, has_side_effects=True, vmem_limit_bytes=VMEM_LIMIT),
        name="att_bwd",
    )(ga, wo, nx, mixed, proj, bl, t, u, o, meta, docs, taps, hg, hot, w, wb, outp, resid)


def once(shape):
    return pl.BlockSpec(shape, lambda i: (0,) * len(shape), pipeline_mode=pl.Buffered(1))


def mlp(groups, members, f, nm, cot, w, wd, resid, mid, grad_out):
    count, width = cot.shape
    ffp = wd.shape[0]
    own = nm.shape[0]
    shape = jax.ShapeDtypeStruct
    mine, down = (width // groups, 2 * ffp), (f, width)
    away = [(groups - 1,) + mine, (groups - 1,) + down]
    outs = [(mine, BF), (down, BF), (away[0], BF), (away[1], BF), ((own, width), F32), ((8, width), F32), ((own, width), BF)]
    return pl.pallas_call(
        functools.partial(mlp_kernel, groups, f, ffp),
        grid=(count // CHUNK,),
        in_specs=[
            once(nm.shape), chip_block(width), once(w.shape), once(wd.shape), once(resid.shape), once(mid.shape),
            once(grad_out.shape),
        ],
        out_specs=[chip_block(width)] + [once(o) for o, _ in outs],
        out_shape=[shape((count, width), BF)] + [shape(o, t) for o, t in outs],
        scratch_shapes=[
            pltpu.VMEM(w.shape, F32), pltpu.VMEM(wd.shape, F32), pltpu.VMEM((members,) + nm.shape, BF),
            pltpu.VMEM((members,) + nm.shape, BF),
        ] + GATHER_SEMS + scatter_scratch(own, width)[1:],
        compiler_params=pltpu.CompilerParams(collective_id=7, has_side_effects=True, vmem_limit_bytes=VMEM_LIMIT),
        name="mlp",
    )(nm, cot, w, wd, resid, mid, grad_out)


MESH = pl.DeviceIdType.MESH
CORE = 1
BITS = (2, 4, 8)
TURNED = (((0, 640, (2, 4, 8)), (640, 640, (4, 8, 2)), (1280, 768, (8, 2, 4))),)
LIGHT = tuple(
    tuple((b * 1024 + i * 512, 512, ((8, 2, 4), (8, 4, 2))[i]) for i in range(2)) for b in range(2)
)
STREAM = (tuple((i * 512, 512, ((8, 2, 4), (8, 4, 2))[i % 2]) for i in range(4)),)
PARTS = 4
OUT_STEPS = (0, 2, 4, 6)
OUT_PLAN = LIGHT
CUTS = (5, 11)


def flat_plan(plan):
    return tuple(part for batch in plan for part in batch)


ANY = pl.BlockSpec(memory_space=pl.ANY)
VM = pl.BlockSpec(memory_space=pltpu.VMEM)


def flip(me, mask):
    out = me
    bit = 1
    while bit <= mask:
        if mask & bit:
            out = out + bit * (1 - 2 * lax.rem(me // bit, 2))
        bit *= 2
    return out


def greet_cube(me_g, me, groups=1):
    barrier = pltpu.get_barrier_semaphore()
    for bit in (CORE,) + BITS:
        pl.semaphore_signal(barrier, inc=1, device_id=(me_g, flip(me, bit)), device_id_type=MESH)
    for k in range(1, groups):
        pl.semaphore_signal(barrier, inc=1, device_id=(lax.rem(me_g + k, groups), me), device_id_type=MESH)
    pl.semaphore_wait(barrier, len(BITS) + groups)


def greet_members(me_g, me, members):
    barrier = pltpu.get_barrier_semaphore()

    @pl.loop(1, members)
    def _(k):
        pl.semaphore_signal(barrier, inc=1, device_id=(me_g, lax.rem(me + k, members)), device_id_type=MESH)

    pl.semaphore_wait(barrier, members - 1)


def remote(src, dst, send, recv, g, m):
    return pltpu.make_async_remote_copy(
        src_ref=src, dst_ref=dst, send_sem=send, recv_sem=recv, device_id=(g, m), device_id_type=MESH
    )


CHIPS = (0, 2, 4, 8, 6, 10, 12, 14)


def chip_at(step, me, chips=CHIPS):
    out = me // 2
    for bit in BITS:
        hit = sum(jnp.where(step == at, 1, 0) for at, mask in enumerate(chips) if mask & bit)
        half = bit // 2
        out = out + hit * half * (1 - 2 * lax.rem(out // half, 2))
    return out


class CubeGather:
    def __init__(self, plan, me_g, me, block, out, local, link_send, link_recv, core_send, core_recv):
        plan = flat_plan(plan)
        self.plan, self.me_g, self.me, self.block, self.out = plan, me_g, me, block, out
        self.local, self.ls, self.lr, self.cs, self.cr = local, link_send, link_recv, core_send, core_recv
        self.parts = range(len(plan))

    def view(self, slot, j):
        at, size, _ = self.plan[j]
        return self.out.at[slot, :, pl.ds(at, size)]

    def source(self, mask, j):
        at, size, _ = self.plan[j]
        return self.block.at[:, pl.ds(at, size)] if mask == 0 else self.view(flip(self.me, mask), j)

    def masks(self, j, step):
        held = [0]
        for bit in self.plan[j][2][:step]:
            held = held + [h + bit for h in held]
        return held

    def hop(self, mask, j, step):
        i = (1 << step) - 1 + self.masks(j, step).index(mask)
        return remote(
            self.source(mask, j), self.view(flip(self.me, mask), j), self.ls.at[j, i], self.lr.at[j, i], self.me_g,
            flip(self.me, self.plan[j][2][step]),
        )

    def core(self, mask, j):
        i = mask // 2
        return remote(
            self.source(mask, j), self.view(flip(self.me, mask), j), self.cs.at[j, i], self.cr.at[j, i], self.me_g,
            flip(self.me, CORE),
        )

    def own(self):
        return pltpu.make_async_copy(self.block, self.out.at[self.me], self.local)

    def start(self):
        for step in range(3):
            for j in self.parts:
                self.hop(0, j, step).start()
        for j in self.parts:
            self.core(0, j).start()
        self.own().start()

    def arrival(self, mask, j, step):
        i = (1 << step) - 1 + self.masks(j, step).index(mask)
        bit = self.plan[j][2][step]
        view = self.view(flip(self.me, mask + bit), j)
        return remote(view, view, self.ls.at[j, i], self.lr.at[j, i], self.me_g, flip(self.me, bit))

    def advance(self, step):
        for count in range(1 << step):
            for j in self.parts:
                mask = self.masks(j, step)[count]
                self.arrival(mask, j, step).wait_recv()
                got = mask + self.plan[j][2][step]
                for later in range(step + 1, 3):
                    self.hop(got, j, later).start()
                self.core(got, j).start()

    def take(self, got):
        for j in self.parts:
            order = self.plan[j][2]
            step = max(i for i in range(3) if order[i] & got)
            self.arrival(got - order[step], j, step).wait_recv()
            for later in range(step + 1, 3):
                self.hop(got, j, later).start()
            self.core(got, j).start()

    def take_core(self, mask):
        for j in self.parts:
            view = self.view(flip(self.me, mask + CORE), j)
            remote(
                view, view, self.cs.at[j, mask // 2], self.cr.at[j, mask // 2], self.me_g, flip(self.me, CORE)
            ).wait_recv()

    def sent(self):
        for j in self.parts:
            for step in range(3):
                for mask in self.masks(j, step):
                    self.hop(mask, j, step).wait_send()
            for mask in range(0, 16, 2):
                self.core(mask, j).wait_send()

    def host(self, step):
        for at, masks in ((1, (2, 4, 8)), (3, (6, 10, 12)), (5, (14,))):
            @pl.when(step == at)
            def _():
                for mask in masks:
                    self.take(mask)

        for at, mask in enumerate(CHIPS):
            @pl.when(step == at)
            def _():
                if mask == 0:
                    self.own().wait()
                self.take_core(mask)

    def finish(self):
        for mask in range(0, 16, 2):
            for j in self.parts:
                view = self.view(flip(self.me, mask + CORE), j)
                remote(
                    view, view, self.cs.at[j, mask // 2], self.cr.at[j, mask // 2], self.me_g, flip(self.me, CORE)
                ).wait_recv()
        for j in self.parts:
            for step in range(3):
                for mask in self.masks(j, step):
                    self.hop(mask, j, step).wait_send()
            for mask in range(0, 16, 2):
                self.core(mask, j).wait_send()
        self.own().wait()


GATHER_SEMS = [
    pltpu.SemaphoreType.DMA(()), pltpu.SemaphoreType.DMA((PARTS, 7)), pltpu.SemaphoreType.DMA((PARTS, 7)),
    pltpu.SemaphoreType.DMA((PARTS, 8)), pltpu.SemaphoreType.DMA((PARTS, 8)),
]


FAR = (14, 12, 10, 6, 4, 2, 8, 0)
LATE = {4: ((1, 10), (1, 12)), 6: ((1, 4),), 7: ((1, 2), (2, 8))}
NEAR_LATE = {7: ((1, 2), (1, 4))}


class CubeScatter:
    def __init__(self, plan, me_g, me, part, mine, other, sums, got, local, core_send, core_recv, link_send, link_recv):
        self.batches = plan
        self.plan = flat_plan(plan)
        self.me_g, self.me, self.part, self.mine, self.other = me_g, me, part, mine, other
        self.sums, self.got, self.local = sums, got, local
        self.cs, self.cr, self.ls, self.lr = core_send, core_recv, link_send, link_recv
        self.parts = range(len(self.plan))

    def order(self, j):
        return self.plan[j][2][::-1]

    ORDER = (14, 6, 10, 12, 2, 4, 8, 0)

    def core_copy(self, b, mask):
        i = mask // 2
        first = self.batches[b][0][0]
        columns = pl.ds(first, sum(part[1] for part in self.batches[b]))
        return remote(
            self.part.at[flip(self.me, mask + CORE), :, columns], self.other.at[i, :, columns], self.cs.at[b, i],
            self.cr.at[b, i], self.me_g, flip(self.me, CORE),
        )

    def load_copy(self, mask):
        i = mask // 2
        return pltpu.make_async_copy(self.part.at[flip(self.me, mask)], self.mine.at[i], self.local.at[i])

    def masks(self, j, step):
        b = self.order(j)
        rest = [0]
        for bit in b[step + 1 :]:
            rest = rest + [h + bit for h in rest]
        return [b[step] + h for h in rest]

    def slot(self, j, step, mask):
        return (0, 4, 6)[step] + self.masks(j, step).index(mask)

    def copy(self, j, step, mask):
        bit = self.order(j)[step]
        i = self.slot(j, step, mask)
        at, size, _ = self.plan[j]
        return remote(
            self.sums.at[i, :, pl.ds(at, size)], self.got.at[i, :, pl.ds(at, size)], self.ls.at[j, i], self.lr.at[j, i],
            self.me_g, flip(self.me, bit),
        )

    def total(self, j, mask, steps):
        at, size, _ = self.plan[j]
        i = mask // 2
        if self.mine is None:
            x = self.part[flip(self.me, mask), :, at : at + size].astype(F32)
        else:
            x = self.mine[i, :, at : at + size].astype(F32)
        x = x + self.other[i, :, at : at + size].astype(F32)
        for step in range(steps):
            k = self.slot(j, step, mask + self.order(j)[step])
            x = x + self.got[k, :, at : at + size].astype(F32)
        return x

    def send(self, j, step, mask):
        at, size, _ = self.plan[j]
        self.sums[self.slot(j, step, mask), :, at : at + size] = self.total(j, mask, step).astype(BF)
        self.copy(j, step, mask).start()

    def start(self):
        for b in range(len(self.batches)):
            for mask in self.ORDER:
                self.core_copy(b, mask).start()
                if b == 0:
                    self.load_copy(mask).start()

    def phase(self, number, store=None):
        if number == 0:
            at = 0
            for b, batch in enumerate(self.batches):
                for mask in self.ORDER:
                    self.core_copy(b, mask).wait_recv()
                    if b == 0:
                        self.load_copy(mask).wait()
                    for j in range(at, at + len(batch)):
                        if mask in self.masks(j, 0):
                            self.send(j, 0, mask)
                at += len(batch)
        elif number < 3:
            for j in self.parts:
                bits = self.order(j)
                for mask in self.masks(j, number):
                    for earlier in range(number):
                        self.copy(j, earlier, mask + bits[earlier]).wait_recv()
                    self.send(j, number, mask)
        else:
            for j in self.parts:
                at, size, _ = self.plan[j]
                for step in range(3):
                    self.copy(j, step, self.order(j)[step]).wait_recv()
                store(j, at, size, self.total(j, 0, 3))

    def late(self, step, mask):
        for j in self.parts:
            if mask in self.masks(j, step):
                for earlier in range(step):
                    self.copy(j, earlier, mask + self.order(j)[earlier]).wait_recv()
                self.send(j, step, mask)

    def host(self, step, order, others):
        for at in range(1, 8):
            @pl.when(step == at)
            def _():
                mask = order[at - 1]
                self.core_copy(0, mask).wait_recv()
                for j in self.parts:
                    if mask in self.masks(j, 0):
                        self.send(j, 0, mask)
                for late, mask in others.get(at, ()):
                    self.late(late, mask)

    def made(self, step, order):
        for at in range(8):
            @pl.when(step == at)
            def _():
                self.core_copy(0, order[at]).start()

    def last(self, mask, others):
        self.core_copy(0, mask).wait_recv()
        for j in self.parts:
            if mask in self.masks(j, 0):
                self.send(j, 0, mask)
        for late, mask in others:
            self.late(late, mask)

    def run(self, out):
        def store(j, at, size, got):
            out[:, at : at + size] = got

        for number in range(4):
            self.phase(number, store)

    def finish(self):
        for b in range(len(self.batches)):
            for mask in self.ORDER:
                self.core_copy(b, mask).wait_send()
        for j in self.parts:
            for step in range(3):
                for mask in self.masks(j, step):
                    self.copy(j, step, mask).wait_send()


def scatter_scratch(rows, width):
    dma = pltpu.SemaphoreType.DMA
    return [
        pltpu.VMEM((8, rows, width), BF), pltpu.VMEM((8, rows, width), BF), pltpu.VMEM((7, rows, width), BF),
        pltpu.VMEM((7, rows, width), BF), dma((8,)), dma((2, 8)), dma((2, 8)), dma((PARTS, 7)), dma((PARTS, 7)),
    ]


NS = 9
NG = len(GATHER_SEMS)


def norm_backward(grad, x, gain):
    r = lax.rsqrt(jnp.mean(x * x, axis=-1, keepdims=True) + EPS)
    n = x * r
    e = grad * gain
    return r * (e - n * jnp.mean(e * n, axis=-1, keepdims=True)), jnp.sum(grad * n, axis=0, keepdims=True)


class Spread:
    def __init__(self, groups, members, me_g, me):
        self.groups, self.members = groups, members
        self.count = groups * members
        self.me_d = me_g * members + me

    def peer(self, k):
        d = lax.rem(self.me_d + k, self.count)
        return d, d // self.members, lax.rem(d, self.members)

    def back(self, k):
        return lax.rem(self.me_d + self.count - k, self.count)

    def greet(self):
        barrier = pltpu.get_barrier_semaphore()

        @pl.loop(1, self.count)
        def _(k):
            _, g, m = self.peer(k)
            pl.semaphore_signal(barrier, inc=1, device_id=(g, m), device_id_type=MESH)

        pl.semaphore_wait(barrier, self.count - 1)


def head_of(m, rho, srange):
    return (m % rho) * srange + m // rho


def ff_block(w, groups, members, m, f, ffp):
    lane = lax.broadcasted_iota(jnp.int32, (w.shape[0], ffp), 1)
    out = jnp.zeros((w.shape[0], ffp), F32)
    for g in range(groups):
        at, to = (g * members + m) * f, g * f
        first = min(at // DK * DK, w.shape[1] - ffp)
        x = pltpu.roll(w[:, first : first + ffp].astype(F32), (to - (at - first)) % ffp, 1)
        out = jnp.where((lane >= to) & (lane < to + f), x, out)
    return out.astype(BF)


def one_hot(rows, lanes, shift=0):
    row = lax.broadcasted_iota(jnp.int32, (rows, lanes), 0)
    lane = lax.broadcasted_iota(jnp.int32, (rows, lanes), 1)
    return (row + shift == lane).astype(BF)


PACK = 32


def make_pack(chan, docs):
    body = chan.astype(F32)
    row = lax.broadcasted_iota(jnp.int32, (8, DK), 0)
    lane = lax.broadcasted_iota(jnp.int32, (8, DK), 1)
    flags = jnp.where(lane == 0, 1, docs).astype(BF)
    src = lax.broadcasted_iota(jnp.int32, (DK, DK), 0)
    dst = lax.broadcasted_iota(jnp.int32, (DK, DK), 1) - SEQ
    count = mm(flags, ((src <= dst) & (src < SEQ)).astype(BF), 1, 0) - 1.0
    live = jnp.where(lane - SEQ < docs, 1.0, 0.0)
    upper = jnp.where(lane < SEQ, 0.0, jnp.where(row < 2, count, jnp.where(row < 4, live, 0.0)))
    return jnp.concatenate([body[:8] + upper, body[8:]], axis=0).astype(BF)


def read_packs(
    groups, members, rho, r, hgr, me_g, me, packs, gain_in, gain_mid, hg, wb, taps, meta, docs, rows_in, rows_mid, rows_hg
):
    n = groups * members
    lane1 = lax.broadcasted_iota(jnp.int32, (1, DK), 1)
    back = one_hot(PACK, DK)
    back = jnp.where(lax.broadcasted_iota(jnp.int32, (PACK, DK), 0) < members, back, jnp.zeros_like(back))

    @pl.loop(0, n)
    def _(d):
        p = packs[d]
        wb[pl.ds(pl.multiple_of(d * r, r), r), :] = mm(p, back, 0, 0)[:r].astype(BF)
        x = p.astype(F32)
        rows_in[pl.ds(d, 1), :] = x[28:29]
        rows_mid[pl.ds(d, 1), :] = x[29:30]
        rows_hg[pl.ds(d, 1), :] = x[30:31]

    per = DK // r
    for out, src in ((gain_in, rows_in), (gain_mid, rows_mid)):
        for i in range(n // per):
            tile = src[i * per : i * per + 1]
            for j in range(1, per):
                tile = tile + pltpu.roll(src[i * per + j : i * per + j + 1], j * r, 1)
            out[:, i * DK : (i + 1) * DK] = tile
    src = lax.broadcasted_iota(jnp.int32, (DK, DK), 0)
    dst = lax.broadcasted_iota(jnp.int32, (DK, DK), 1)
    spread = ((src < hgr) & (src == lax.rem(dst, hgr))).astype(BF)
    every = mm(rows_hg[...].astype(BF), spread, 1, 0)
    drow = lax.broadcasted_iota(jnp.int32, (n, DK), 0)
    dlane = lax.broadcasted_iota(jnp.int32, (n, DK), 1)
    hg[...] = jnp.sum(jnp.where(dlane // hgr == drow, every, 0.0), axis=0, keepdims=True)

    lane16 = lax.broadcasted_iota(jnp.int32, (16, DK), 1)
    total = jnp.zeros((16, DK), F32)
    for i in range(rho):
        d = lax.rem(me, rho) * members + (me // rho) * rho + i
        x = jnp.where(lane16 < r, packs[d].astype(F32)[16:32], 0.0)
        total = total + (pltpu.roll(x, i * r, 1) if i else x)
    taps[...] = total

    to_rows = one_hot(8, DK)
    row128 = lax.broadcasted_iota(jnp.int32, (SUB, DK), 0)
    lane128 = lax.broadcasted_iota(jnp.int32, (SUB, DK), 1)

    @pl.loop(0, members)
    def _(j):
        x = packs[me_g * members + j].astype(F32)[:8]
        turned = pltpu.roll(x, SEQ, 1)
        doc = jnp.where(lane1 < SEQ, turned[0:1], x[1:2])
        live = jnp.where(lane1 < SEQ, turned[2:3], x[3:4])
        lines = [doc]
        for o in range(1, TAPS):
            keep = (lax.rem(lane1, SEQ) >= o) & (pltpu.roll(doc, o, 1) == doc)
            lines.append(jnp.where(keep, 1.0, 0.0))
        lines += [live, jnp.zeros((3, DK), F32)]
        lines = jnp.concatenate(lines, axis=0).astype(BF)
        first = (2 * SEQ * j).astype(F32)
        docs[j] = doc + first + jnp.where(lane1 < SEQ, 0.0, float(SEQ))
        block = mm(lines, to_rows, 0, 0)
        shift = first + jnp.where(row128 < SEQ, 0.0, float(SEQ))
        meta[pl.ds(pl.multiple_of(j * SUB, SUB), SUB), :] = block + jnp.where(lane128 == 0, shift, 0.0)


def head_of(m, rho, srange):
    return (m % rho) * srange + m // rho


def start_kernel(
    groups, members, rho, hgr, tok, wq, wk, wv, wg, w_gate, w_up, wo, wd, chan, starts,
    tok_all, w_att, w_out, ff_half, down_all, gain_in, gain_mid, hg, wb, taps, meta, docs,
    att, ff, pack, packs, rows_in, rows_mid, rows_hg, sa, ra, sx, rx, sp, rp, sf, rf, so, ro, sd, rd, loc, *sems,
):
    me_g, me = lax.axis_index("g"), lax.axis_index("m")
    spread = Spread(groups, members, me_g, me)
    me_d = spread.me_d
    r = wq.shape[0]
    f = w_gate.shape[1] // spread.count
    ffp = ff.shape[2] // 2
    spread.greet()
    gather = CubeGather(LIGHT, me_g, me, tok, tok_all, *sems)
    for m in range(members):
        h = head_of(m, rho, members // rho) * DK
        for i, w in enumerate((wq, wk, wv, wg)):
            att[m, :, i * DK : (i + 1) * DK] = w[:, h : h + DK]

    def att_copy(k):
        m = lax.rem(me + k, members)
        return remote(att.at[m], w_att.at[me_d], sa.at[k], ra.at[k], me_g, m)

    def att_far(k, step):
        d = me_g * members + lax.rem(me + members - k, members)
        return remote(
            w_att.at[d], w_att.at[d], sx.at[step, k], rx.at[step, k], lax.rem(me_g + step, groups), me
        )

    def att_far_own(step):
        return remote(
            att.at[me], w_att.at[me_d], sx.at[step, 0], rx.at[step, 0], lax.rem(me_g + step, groups), me
        )

    def ff_copy(k):
        m = lax.rem(me + k, members)
        return remote(ff.at[m], ff_half.at[me], sf.at[k], rf.at[k], me_g, m)

    def down_copy(step):
        return remote(wd, down_all.at[me_g], sd.at[step], rd.at[step], lax.rem(me_g + step, groups), me)

    def down_arrival(step):
        src = lax.rem(me_g + groups - step, groups)
        return remote(wd, down_all.at[src], sd.at[step], rd.at[step], me_g, me)

    def pack_copy(k, g, m):
        return remote(pack, packs.at[me_d], sp.at[k], rp.at[k], g, m)

    target = (me // rho) * rho + me_g
    place = lax.rem(me, rho)
    sources = [(lax.rem(me, rho), (me // rho) * rho + i) for i in range(rho)]

    def out_copy(g):
        return remote(wo, w_out.at[place], so.at[g], ro.at[place], g, target)

    for step in range(1, groups):
        att_far_own(step).start()
        down_copy(step).start()

    @pl.loop(1, members)
    def _(k):
        att_copy(k).start()

    gather.start()
    pack[...] = make_pack(chan[...], starts[...])

    @pl.loop(1, spread.count)
    def _(k):
        _, g, m = spread.peer(k)
        pack_copy(k, g, m).start()

    packs[me_d] = pack[...]
    copies = [
        pltpu.make_async_copy(att.at[me], w_att.at[me_d], loc.at[0]),
        pltpu.make_async_copy(wd, down_all.at[me_g], loc.at[1]),
    ]
    for copy in copies:
        copy.start()

    def relay(first, last):
        @pl.loop(first, last)
        def _(k):
            att_copy(k).wait_recv()
            for step in range(1, groups):
                att_far(k, step).start()

    relay(1, members // 2)
    gather.advance(0)
    relay(members // 2, members)
    for g in range(groups):
        @pl.when((me_g != g) | (me != target))
        def _():
            out_copy(g).start()

    @pl.when(me == target)
    def _():
        pltpu.make_async_copy(wo, w_out.at[place], loc.at[2]).start()

    for m in range(members):
        for i, w in enumerate((w_gate, w_up)):
            ff[m, :, i * ffp : (i + 1) * ffp] = ff_block(w, groups, members, m, f, ffp)
    gather.advance(1)

    @pl.loop(1, members)
    def _(k):
        ff_copy(k).start()

    ff_own = pltpu.make_async_copy(ff.at[me], ff_half.at[me], loc.at[3])
    ff_own.start()
    gather.advance(2)

    @pl.loop(1, spread.count)
    def _(k):
        _, g, m = spread.peer(k)
        pack_copy(k, g, m).wait()

    read_packs(
        groups, members, rho, r, hgr, me_g, me, packs, gain_in, gain_mid, hg, wb, taps, meta, docs, rows_in, rows_mid, rows_hg
    )
    gather.finish()

    @pl.loop(1, members)
    def _(k):
        att_copy(k).wait_send()
        ff_copy(k).wait()
        for step in range(1, groups):
            att_far(k, step).wait()

    for step in range(1, groups):
        att_far_own(step).wait()
        down_copy(step).wait_send()
        down_arrival(step).wait_recv()
    for copy in copies:
        copy.wait()
    ff_own.wait()
    for g in range(groups):
        @pl.when((me_g != g) | (me != target))
        def _():
            out_copy(g).wait_send()
    for i in range(rho):
        src_g, src_m = sources[i]
        @pl.when((me_g != src_g) | (me != src_m))
        def _():
            remote(wo, w_out.at[i], so.at[0], ro.at[i], me_g, me).wait_recv()

    @pl.when(me == target)
    def _():
        pltpu.make_async_copy(wo, w_out.at[place], loc.at[2]).wait()


def start_call(groups, members, rho, hgr, ffp, tok, weights, ffw, wo, wd, chan, starts):
    shape = jax.ShapeDtypeStruct
    n = groups * members
    r, width = wo.shape
    count = members * tok.shape[0]
    dma = pltpu.SemaphoreType.DMA
    return pl.pallas_call(
        functools.partial(start_kernel, groups, members, rho, hgr),
        in_specs=[ANY] + [VM] * 6 + [ANY] * 2 + [VM] * 2,
        out_specs=[ANY] * 5 + [VM] * 7,
        out_shape=[
            shape((members,) + tok.shape, BF), shape((n, r, 4 * DK), BF), shape((rho, r, width), BF),
            shape((members, r, 2 * ffp), BF), shape((groups,) + wd.shape, BF), shape((1, width), F32), shape((1, width), F32),
            shape((1, DK), F32), shape((width, DK), BF), shape((16, DK), F32), shape((count, DK), F32),
            shape((count // SUB, 1, SUB), F32),
        ],
        scratch_shapes=[
            pltpu.VMEM((members, r, 4 * DK), BF), pltpu.VMEM((members, r, 2 * ffp), BF), pltpu.VMEM((PACK, DK), BF),
            pltpu.VMEM((n, PACK, DK), BF), pltpu.VMEM((n, DK), F32), pltpu.VMEM((n, DK), F32), pltpu.VMEM((n, DK), F32),
            dma((members,)), dma((members,)), dma((groups, members)),
            dma((groups, members)), dma((n,)), dma((n,)), dma((members,)), dma((members,)), dma((groups,)), dma((rho,)),
            dma((groups,)), dma((groups,)), dma((4,)),
        ] + GATHER_SEMS,
        compiler_params=pltpu.CompilerParams(collective_id=3, has_side_effects=True, vmem_limit_bytes=VMEM_LIMIT),
        name="start",
    )(tok, *weights, *ffw, wo, wd, chan, starts)


def ff_place(out, x, groups, members, m, f, ffp):
    x = x.astype(F32)
    lane = lax.broadcasted_iota(jnp.int32, x.shape, 1)
    for g in range(groups):
        at, to = (g * members + m) * f, g * f
        first = min(at // DK * DK, out.shape[1] - ffp)
        there = at - first
        y = pltpu.roll(x, (there - to) % ffp, 1)
        keep = (lane >= there) & (lane < there + f)
        out[:, first : first + ffp] = jnp.where(keep, y, out[:, first : first + ffp])


def end_kernel(
    groups, members, rho, hgr, part, flat, gain, gmid, gbeta, ghg, gtaps, gatt, gff, gout,
    grad_in, att_in, ff_in, out_in, small_in, tap_in, gain_in,
    total, vec, mine, far, sums, small, tapg, sa, ra, sx, rx, ss, rs, sf, rf, so, ro, st, rt, sg, rg, loc, *sems,
):
    me_g, me = lax.axis_index("g"), lax.axis_index("m")
    spread = Spread(groups, members, me_g, me)
    me_d = spread.me_d
    r = gout.shape[1]
    spread.greet()
    scatter = CubeScatter(LIGHT, me_g, me, part, *sems)

    def att_far(k, step):
        g = lax.rem(me_g + step, groups)
        m = lax.rem(me + k, members)
        return remote(gatt.at[g * members + m], far.at[step - 1, m], sx.at[step - 1, k], rx.at[step - 1, k], g, me)

    def att_copy(k):
        m = lax.rem(me + k, members)
        return remote(sums.at[m], att_in.at[me], sa.at[k], ra.at[k], me_g, m)

    def small_copy(k, d, g, m):
        return remote(small.at[d], small_in.at[me_d], ss.at[k], rs.at[k], g, m)

    def ff_copy(k):
        m = lax.rem(me + k, members)
        return remote(gff.at[m], ff_in.at[me], sf.at[k], rf.at[k], me_g, m)

    def gain_copy(k, d, g, m):
        return remote(vec.at[d * r // DK], gain_in.at[me_d], sg.at[k], rg.at[k], g, m)

    home = lax.rem(me, rho)
    base = (me // rho) * rho

    def out_copy(i):
        return remote(gout.at[i], out_in.at[me_g], so.at[i], ro.at[me_g], home, base + i)

    def tap_copy(i):
        return remote(tapg.at[i], tap_in.at[me_g], st.at[i], rt.at[me_g], home, base + i)

    @pl.loop(0, members)
    def _(k):
        for step in range(1, groups):
            att_far(k, step).start()

    own_rows = pltpu.make_async_copy(gatt.at[pl.ds(me_g * members, members)], mine, loc.at[0])
    own_rows.start()
    scatter.start()
    lane = lax.broadcasted_iota(jnp.int32, (1, DK), 1)
    per = DK // r
    for d in range(spread.count):
        tile = pl.ds(d // per * DK, DK)
        back = (DK - d % per * r) % DK
        lines = [turned(gmid[0:1, tile], back), turned(gbeta[0:1, tile], back)]
        hg_back = (DK - d * hgr % DK) % DK
        small[d] = jnp.concatenate(
            [jnp.where(lane < r, x, 0.0) for x in lines]
            + [jnp.where(lane < hgr, turned(ghg[0:1], hg_back), 0.0), jnp.zeros((5, DK), F32)],
            axis=0,
        )
    lane16 = lax.broadcasted_iota(jnp.int32, (16, DK), 1)
    for i in range(rho):
        tapg[i] = jnp.where(lane16 < r, turned(gtaps[...], (DK - i * r) % DK), 0.0)

    @pl.loop(1, spread.count)
    def _(k):
        d, g, m = spread.peer(k)
        small_copy(k, d, g, m).start()

    copies = [
        pltpu.make_async_copy(small.at[me_d], small_in.at[me_d], loc.at[1]),
        pltpu.make_async_copy(gff.at[me], ff_in.at[me], loc.at[2]),
    ]
    for copy in copies:
        copy.start()
    for i in range(rho):
        @pl.when((me_g != home) | (me != base + i))
        def _():
            out_copy(i).start()
            tap_copy(i).start()

        @pl.when((me_g == home) & (me == base + i))
        def _():
            pltpu.make_async_copy(gout.at[i], out_in.at[me_g], loc.at[3]).start()
            pltpu.make_async_copy(tapg.at[i], tap_in.at[me_g], loc.at[4]).start()

    scatter.phase(0)

    @pl.loop(1, members)
    def _(k):
        ff_copy(k).start()

    def store(j, at, size, got):
        total[:, at : at + size] = got

    own_rows.wait()

    def relay(first, last):
        @pl.loop(first, last)
        def _(k):
            m = lax.rem(me + k, members)
            x = mine[m].astype(F32)
            for step in range(1, groups):
                att_far(k, step).wait_recv()
                x = x + far[step - 1, m].astype(F32)
            sums[m] = x.astype(BF)

            @pl.when(k > 0)
            def _():
                att_copy(k).start()

    relay(0, CUTS[0])
    scatter.phase(1)
    relay(CUTS[0], CUTS[1])
    scatter.phase(2)
    relay(CUTS[1], members)
    scatter.phase(3, store)
    back, gsum = norm_backward(total[...], flat[...].astype(F32), gain[...])
    grad_in[...] = back
    for i in range(vec.shape[0]):
        vec[i] = gsum[:, i * DK : (i + 1) * DK]

    @pl.loop(1, spread.count)
    def _(k):
        d, g, m = spread.peer(k)
        gain_copy(k, d, g, m).start()

    own = pltpu.make_async_copy(vec.at[me_d * r // DK], gain_in.at[me_d], loc.at[5])
    own.start()
    scatter.finish()
    kept = pltpu.make_async_copy(sums.at[me], att_in.at[me], loc.at[6])
    kept.start()

    @pl.loop(1, members)
    def _(k):
        att_copy(k).wait()
        ff_copy(k).wait()

    kept.wait()

    @pl.loop(0, members)
    def _(k):
        for step in range(1, groups):
            att_far(k, step).wait_send()

    @pl.loop(1, spread.count)
    def _(k):
        d, g, m = spread.peer(k)
        small_copy(k, d, g, m).wait()
        gain_copy(k, d, g, m).wait()

    for copy in copies:
        copy.wait()
    own.wait()
    for i in range(rho):
        @pl.when((me_g != home) | (me != base + i))
        def _():
            out_copy(i).wait_send()
            tap_copy(i).wait_send()

        @pl.when((me_g == home) & (me == base + i))
        def _():
            pltpu.make_async_copy(gout.at[i], out_in.at[me_g], loc.at[3]).wait()
            pltpu.make_async_copy(tapg.at[i], tap_in.at[me_g], loc.at[4]).wait()
    holder = base + me_g
    for g in range(groups):
        @pl.when((me_g != g) | (me != holder))
        def _():
            remote(gout.at[0], out_in.at[g], so.at[0], ro.at[g], me_g, me).wait_recv()
            remote(tapg.at[0], tap_in.at[g], st.at[0], rt.at[g], me_g, me).wait_recv()


def turned(x, shift):
    return pltpu.roll(x, shift, 1) if shift else x


def finish_kernel(
    groups, members, rho, grad_in, grad_resid, att_in, ff_in, out_in, small_in, tap_in, gain_in,
    input_grad, gq, gk, gv, gg, g_gate, g_up, g_out, s_in, s_mid, s_hg, g_beta, g_tq, g_tk, g_tv,
):
    me_g, me = lax.axis_index("g"), lax.axis_index("m")
    n = groups * members
    me_d = me_g * members + me
    r = out_in.shape[1]
    ffp = ff_in.shape[2] // 2
    f = g_gate.shape[1] // n
    input_grad[...] = grad_resid[...] + grad_in[...]
    for m in range(members):
        h = head_of(m, rho, members // rho) * DK
        for i, out in enumerate((gq, gk, gv, gg)):
            out[:, h : h + DK] = att_in[m, :, i * DK : (i + 1) * DK].astype(F32)
    for m in range(members):
        for i, out in enumerate((g_gate, g_up)):
            ff_place(out, ff_in[m, :, i * ffp : (i + 1) * ffp], groups, members, m, f, ffp)
    g_out[...] = sum(out_in[g].astype(F32) for g in range(groups))
    taps = sum(tap_in[g] for g in range(groups))
    for i, out in enumerate((g_tq, g_tk, g_tv)):
        out[...] = taps[i * TAPS : (i + 1) * TAPS, :r]
    for m in range(members):
        row = small_in[m, 1:2]
        for g in range(1, groups):
            row = row + small_in[g * members + m, 1:2]
        h = head_of(m, rho, members // rho)
        g_beta[h : h + 1] = row[:, :r]
    acc = jnp.sum(small_in[...], axis=0)
    gsum = jnp.sum(gain_in[...], axis=0)
    own_gain = pltpu.roll(gsum, lax.rem(DK - lax.rem(me_d * r, DK), DK), 1)
    s_in[...] = own_gain[:, :r]
    s_mid[...] = acc[0:1, :r]
    s_hg[...] = acc[2:3, : s_hg.shape[1]]


def finish_call(groups, members, rho, hidden, hgr, heads, args):
    shape = jax.ShapeDtypeStruct
    rows, width = args[0].shape
    r = args[4].shape[1]
    outs = [(rows, width)] + [(r, width)] * 4 + [(r, hidden)] * 2 + [(r, width), (1, r), (1, r), (1, hgr), (heads, r)]
    outs += [(TAPS, r)] * 3
    return pl.pallas_call(
        functools.partial(finish_kernel, groups, members, rho),
        in_specs=[VM] * len(args),
        out_specs=[VM] * len(outs),
        out_shape=[shape(o, F32) for o in outs],
        compiler_params=pltpu.CompilerParams(vmem_limit_bytes=VMEM_LIMIT),
        name="finish",
    )(*args)


def end_call(groups, members, rho, hgr, part, flat, gain, gmid, gbeta, ghg, gtaps, gatt, gff, gout):
    shape = jax.ShapeDtypeStruct
    n = groups * members
    _, rows, width = part.shape
    r = gout.shape[1]
    dma = pltpu.SemaphoreType.DMA
    piece = (r, 4 * DK)
    return pl.pallas_call(
        functools.partial(end_kernel, groups, members, rho, hgr),
        in_specs=[ANY] + [VM] * 6 + [ANY] * 3,
        out_specs=[VM] + [ANY] * 6,
        out_shape=[
            shape((rows, width), F32), shape((members,) + piece, BF), shape(gff.shape, BF),
            shape((groups,) + gout.shape[1:], BF), shape((n, 8, DK), F32), shape((groups, 16, DK), F32),
            shape((n, 1, DK), F32),
        ],
        scratch_shapes=[
            pltpu.VMEM((rows, width), F32), pltpu.VMEM((width // DK, 1, DK), F32), pltpu.VMEM((members,) + piece, BF),
            pltpu.VMEM((groups - 1, members) + piece, BF), pltpu.VMEM((members,) + piece, BF),
            pltpu.VMEM((n, 8, DK), F32), pltpu.VMEM((rho, 16, DK), F32), dma((members,)), dma((members,)),
            dma((groups - 1, members)), dma((groups - 1, members)), dma((n,)), dma((n,)), dma((members,)), dma((members,)),
            dma((rho,)), dma((groups,)), dma((rho,)), dma((groups,)), dma((n,)), dma((n,)), dma((7,)),
        ] + scatter_scratch(rows, width),
        compiler_params=pltpu.CompilerParams(collective_id=4, has_side_effects=True, vmem_limit_bytes=VMEM_LIMIT),
        name="end",
    )(part, flat, gain, gmid, gbeta, ghg, gtaps, gatt, gff, gout)


def exchange_groups(x, groups):
    return [
        lax.ppermute(x[step - 1], "g", [(i, (i + step) % groups) for i in range(groups)]) for step in range(1, groups)
    ]


def make_shards(groups, members):
    def shards(
        tokens, doc_starts, seq_lengths, attn_gain, query_weight, key_weight, value_weight, out_gate_weight, beta_weight,
        query_conv, key_conv, value_conv, head_gain, out_weight, mlp_gain, mlp_gate_weight, mlp_up_weight,
        mlp_down_weight, cotangent,
    ):
        n = groups * members
        width = tokens.shape[-1]
        r = attn_gain.shape[0]
        f = mlp_down_weight.shape[0]
        hgr = head_gain.shape[0]
        heads = beta_weight.shape[1]
        rho = DK // r
        srange = members // rho
        me_g, me_m = lax.axis_index("g"), lax.axis_index("m")
        head = lax.rem(me_m, rho) * srange + me_m // rho
        seqs = tokens.shape[0] * tokens.shape[1]
        seq = tokens.shape[2]
        own = seqs * seq
        flat_bf = tokens.reshape(own, width)
        grad_out = cotangent.reshape(own, width)

        lines = [beta_weight.T, query_conv.T, key_conv.T, value_conv.T, attn_gain[None], mlp_gain[None]]
        lines.append(jnp.pad(head_gain, (0, r - hgr))[None])
        chan = jnp.concatenate(lines, axis=0)
        chan = jnp.pad(chan, ((0, PACK - chan.shape[0]), (0, DK - r)))
        starts = jnp.pad(doc_starts.reshape(seqs, seq), ((0, 0), (0, DK - seq)))
        lengths = jnp.broadcast_to(seq_lengths.reshape(seqs, 1), (seqs, DK))
        starts = jnp.pad(jnp.concatenate([starts, lengths]), ((0, 8 - 2 * seqs), (0, 0)))
        ffw = groups * f
        ffp = -(-ffw // DK) * DK
        hidden_size = mlp_gate_weight.shape[1]
        count = members * own
        tok_all, w_att, w_out, ff_half, w_down, gain_in, gain_mid, hg, beta_full, taps, meta, docs_row = start_call(
            groups, members, rho, hgr, ffp, flat_bf, (query_weight, key_weight, value_weight, out_gate_weight),
            (mlp_gate_weight, mlp_up_weight), out_weight, mlp_down_weight, chan, starts,
        )
        w_ff = lax.all_gather(ff_half, "g", axis=0).reshape(width, 2 * ffp)
        w_att = w_att.reshape(width, 4 * DK)
        w_out = w_out.reshape(DK, width)
        hot = (jnp.arange(DK) == head).astype(F32).reshape(1, DK)

        blocks = (members, own, width)
        w_down = jnp.pad(w_down.reshape(ffw, width), ((0, ffp - ffw), (0, 0)))
        nx, proj, bl, t, u, o, mixed, resid, nm, cot_all = att_forward(
            members, tok_all.reshape(count, width), gain_in, w_att, beta_full, taps, hg, hot, w_out, meta, docs_row, grad_out,
            flat_bf, gain_mid,
        )
        out_part, g_ff, g_down, ff_away, down_away, grad_resid, g_mid_gain, ga = mlp(
            groups, members, f, nm, cot_all.reshape(count, width), w_ff, w_down, resid, gain_mid, grad_out
        )
        ff_came = exchange_groups(ff_away, groups)
        g_down = sum((x.astype(F32) for x in exchange_groups(down_away, groups)), g_down.astype(F32))
        g_ff = sum((x.astype(F32) for x in ff_came), g_ff.astype(F32)).astype(BF).reshape(members, r, 2 * ffp)
        gpart, gtaps, ghg, gatt, gout, g_beta, layer_out = att_backward(
            members, ga, w_out, nx, mixed, proj, bl, t, u, o, meta, docs_row, taps, hg, hot, w_att, beta_full,
            out_part.reshape(blocks), resid,
        )
        gatt = gatt.reshape(n, r, 4 * DK)
        gout = gout.reshape(rho, r, width)
        came = end_call(
            groups, members, rho, hgr, gpart.reshape(blocks), flat_bf, gain_in, g_mid_gain, g_beta, ghg, gtaps, gatt, g_ff,
            gout,
        )
        args = (came[0], grad_resid) + tuple(came[1:])
        input_grad, gq, gk, gv, gg, g_gate, g_up, g_out, s_in, s_mid, s_hg, s_beta, s_q, s_k, s_v = finish_call(
            groups, members, rho, hidden_size, hgr, heads, args
        )
        s_in, s_mid, s_hg = s_in.reshape(r), s_mid.reshape(r), s_hg.reshape(hgr)
        s_beta, s_q, s_k, s_v = s_beta.T, s_q.T, s_k.T, s_v.T
        return (
            layer_out.reshape(tokens.shape), input_grad.reshape(tokens.shape),
            s_in, gq, gk, gv, gg, s_beta, s_q, s_k, s_v, s_hg, g_out, s_mid, g_gate, g_up,
            g_down,
        )

    return shards


def solution(mesh):
    n = mesh.devices.size
    members = 16
    groups = n // members
    inner = Mesh(mesh.devices.reshape(groups, members), ("g", "m"))
    both = ("g", "m")
    acts, mat, vec = P(None, both, None, None), P(both, None), P(both)
    return jax.shard_map(
        make_shards(groups, members),
        mesh=inner,
        in_specs=(acts, P(None, both, None), P(None, both), vec, mat, mat, mat, mat, mat, mat, mat, mat, vec, mat, vec,
                  mat, mat, mat, acts),
        out_specs=(acts, acts, vec, mat, mat, mat, mat, mat, mat, mat, mat, vec, mat, vec, mat, mat, mat),
        check_vma=False,
    )
```
